128 devices in a mesh: rows: 16 (over y, x_lo, core), cols: 8 (over z, x_hi).
Axes of the slice: x: 4 (x_hi: 2, x_lo: 2; x = x_hi * 2 + x_lo), y: 4, z: 4, core: 2. Of those that a mesh axis runs over, the one named last changes fastest.
Arguments:
- feat_left: bfloat16 [256, 2048, 256], P('rows', 'cols'), may hold values from -6 to 6
- feat_right: bfloat16 [256, 2048, 256], P('rows', 'cols'), may hold values from -6 to 6
- hidden: bfloat16 [256, 2048, 128], P('rows', 'cols'), may hold values from -1 to 1
- disparity: int32 [256, 2048], P('rows', 'cols'), may hold values from 0 to 127
- motion_weight: bfloat16 [9, 128], replicated, may hold values from -2 to 2
- gate_weight: bfloat16 [3, 3, 256, 256], replicated, may hold values from -0.125 to 0.125
- cand_weight: bfloat16 [3, 3, 256, 128], replicated, may hold values from -0.125 to 0.125
- grad_hidden: bfloat16 [256, 2048, 128], P('rows', 'cols'), may hold values from -6 to 6
Outputs:
- new_hidden: bfloat16 [256, 2048, 128], P('rows', 'cols')
- grad_left: bfloat16 [256, 2048, 256], P('rows', 'cols')
- grad_right: bfloat16 [256, 2048, 256], P('rows', 'cols')
The draws below stay inside these ranges and needn't reach their ends.
Inputs may be any that keep to these rules, and one draw needn't show every extreme that they name: Whole disparity levels.
All inputs are finite; a program needn't handle non-finite values.
Results may differ from the reference program's by a relative error of at most 0.0075.
Values may be sent and summed in bfloat16 or wider, within the bound.
No kernel may reach another device: no remote copies, remote signals or barrier semaphores. Data moves between devices by JAX's collectives and lax.ppermute only.
A program may use at most 192 MiB of HBM per device.

```python
import math
import jax
import jax.numpy as jnp
from jax import lax

C = 256
HID = 128
MOT = 128
DISP = 128
RAD = 4
TAPS = 9
HEIGHT = 256
WIDTH = 2048


def set_ends(values, stream_key, low, largest):
    longest = values.shape.index(max(values.shape))
    spots = []
    for shift in (0, 1):
        where = [jax.random.randint(jax.random.fold_in(stream_key, axis), (), 0, length) for axis, length in enumerate(values.shape)]
        where[longest] = (where[longest] + shift) % values.shape[longest]
        spots.append(tuple(where))
    return values.at[spots[0]].set(low).at[spots[1]].set(largest)


def level_of(rng, shape, cuts, least, high):
    def one(dim, blocks):
        draws = jax.random.uniform(jax.random.fold_in(jax.random.fold_in(rng, 6), dim), (blocks,), jnp.float32, least / len(cuts), high / len(cuts))
        return jnp.repeat(jnp.exp(draws), shape[dim] // blocks).reshape((-1,) + (1,) * (len(shape) - dim - 1))

    level = one(*cuts[0])
    for cut in cuts[1:]:
        level = level * one(*cut)
    return level


def centred(rng, dims, scale, limit, shards=(), kind=jnp.bfloat16):
    level = level_of(rng, dims, shards, -0.22, 0.18) if shards else 1.0
    entries = jax.random.normal(rng, dims, jnp.float32) * scale * level
    return jnp.minimum(jnp.maximum(entries, -limit), limit).astype(kind)


def setup_inputs(seed: int = 0) -> dict:
    streams_of = jax.random.split(jax.random.key(seed), 9)
    feat_left = centred(streams_of[0], (HEIGHT, WIDTH, C), 1.0, 6.0, ((0, 16), (1, 8)))
    feat_right = centred(streams_of[1], (HEIGHT, WIDTH, C), 1.0, 6.0, ((0, 16), (1, 8)))
    hidden = jnp.clip(jax.random.uniform(streams_of[2], (HEIGHT, WIDTH, HID), jnp.float32, -1.0, 1.0) * level_of(streams_of[2], (HEIGHT, WIDTH, HID), ((0, 16), (1, 8)), -0.4, 0.0), -1.0, 1.0).astype(jnp.bfloat16)
    disparity = set_ends(jax.random.randint(streams_of[3], (HEIGHT, WIDTH), 0, DISP), jax.random.fold_in(streams_of[3], 1), 0, DISP - 1).astype(jnp.int32)
    motion_weight = centred(streams_of[4], (TAPS, MOT), TAPS ** -0.5, 2.0)
    gate_weight = centred(streams_of[5], (3, 3, HID + MOT, 2 * HID), (9 * (HID + MOT)) ** -0.5, 0.125)
    cand_weight = centred(streams_of[6], (3, 3, HID + MOT, HID), (9 * (HID + MOT)) ** -0.5, 0.125)
    grad_hidden = centred(streams_of[7], (HEIGHT, WIDTH, HID), 1.0, 6.0, ((0, 16), (1, 8)))
    return dict(feat_left=feat_left, feat_right=feat_right, hidden=hidden, disparity=disparity, motion_weight=motion_weight, gate_weight=gate_weight, cand_weight=cand_weight, grad_hidden=grad_hidden)


def band_windows(feat_right, band_size):
    row_count, col_count, chan_count = feat_right.shape
    extended = jnp.concatenate([jnp.zeros((row_count, band_size, chan_count), feat_right.dtype), feat_right], axis=1)
    blocks = extended.reshape(row_count, col_count // band_size + 1, band_size, chan_count)
    return jnp.concatenate([blocks[:, :-1], blocks[:, 1:]], axis=2)

def tap_index(disparity, band_size, radius):
    col_count = disparity.shape[1]
    inner = jnp.arange(col_count, dtype=jnp.int32) % band_size
    offsets = jnp.arange(2 * radius + 1, dtype=jnp.int32) - radius
    levels = disparity[:, :, None].astype(jnp.int32) + offsets[None, None, :]
    usable = (levels >= 0) & (levels < band_size)
    columns = jnp.clip(inner[None, :, None] + band_size - levels, 0, 2 * band_size - 1)
    return (columns.astype(jnp.int32), usable)

def conv_ref(padded, weight, row_count, col_count):
    result = jnp.zeros((row_count, col_count, weight.shape[3]), jnp.float32)
    for row_off in range(3):
        for col_off in range(3):
            result = result + jnp.einsum('hwi,io->hwo', padded[row_off:row_off + row_count, col_off:col_off + col_count].astype(jnp.float32), weight[row_off, col_off].astype(jnp.float32))
    return result

def flipped(weight):
    return jnp.transpose(weight[::-1, ::-1], (0, 1, 3, 2))

def pad_grid(field):
    return jnp.pad(field, ((1, 1), (1, 1), (0, 0)))

def reference(feat_left, feat_right, hidden, disparity, motion_weight, gate_weight, cand_weight, grad_hidden):
    row_count, col_count, chan_count = feat_left.shape
    scale = 1.0 / math.sqrt(chan_count)
    block_count = col_count // DISP
    windows = band_windows(feat_right, DISP).astype(jnp.float32)
    left_blocks = feat_left.reshape(row_count, block_count, DISP, chan_count).astype(jnp.float32)
    scores = jnp.einsum('hbic,hbjc->hbij', left_blocks, windows) * scale
    columns, usable = tap_index(disparity, DISP, RAD)
    taps = jnp.take_along_axis(scores.reshape(row_count, col_count, 2 * DISP), columns, axis=2)
    taps = jnp.where(usable, taps, 0.0).astype(jnp.bfloat16)
    motion_pre = jnp.einsum('hwk,km->hwm', taps.astype(jnp.float32), motion_weight.astype(jnp.float32))
    motion = jax.nn.silu(motion_pre).astype(jnp.bfloat16)
    inputs = jnp.concatenate([hidden, motion], axis=2)
    gates = conv_ref(pad_grid(inputs), gate_weight, row_count, col_count)
    update = jax.nn.sigmoid(gates[..., :HID])
    reset = jax.nn.sigmoid(gates[..., HID:])
    hidden_f = hidden.astype(jnp.float32)
    reset_state = (reset * hidden_f).astype(jnp.bfloat16)
    cand_in = jnp.concatenate([reset_state, motion], axis=2)
    cand = jnp.tanh(conv_ref(pad_grid(cand_in), cand_weight, row_count, col_count))
    new_hidden = ((1.0 - update) * hidden_f + update * cand).astype(jnp.bfloat16)
    cotangent = grad_hidden.astype(jnp.float32)
    cand_grad = (cotangent * update * (1.0 - cand * cand)).astype(jnp.bfloat16)
    update_grad = cotangent * (cand - hidden_f) * update * (1.0 - update)
    cand_back = conv_ref(pad_grid(cand_grad), flipped(cand_weight), row_count, col_count)
    reset_grad = cand_back[..., :HID] * hidden_f * reset * (1.0 - reset)
    gate_grads = jnp.concatenate([update_grad, reset_grad], axis=2).astype(jnp.bfloat16)
    gate_back = conv_ref(pad_grid(gate_grads), flipped(gate_weight), row_count, col_count)
    motion_grad = cand_back[..., HID:] + gate_back[..., HID:]
    sigmas = jax.nn.sigmoid(motion_pre)
    pre_grad = (motion_grad * sigmas * (1.0 + motion_pre * (1.0 - sigmas))).astype(jnp.bfloat16)
    tap_grad = jnp.einsum('hwm,km->hwk', pre_grad.astype(jnp.float32), motion_weight.astype(jnp.float32))
    tap_grad = jnp.where(usable, tap_grad, 0.0)
    positions = jnp.arange(2 * DISP, dtype=jnp.int32)
    score_grad = jnp.zeros((row_count, col_count, 2 * DISP), jnp.float32)
    for tap in range(2 * RAD + 1):
        score_grad = score_grad + jnp.where(columns[:, :, tap:tap + 1] == positions, tap_grad[:, :, tap:tap + 1], 0.0)
    score_grad = score_grad.astype(jnp.bfloat16).reshape(row_count, block_count, DISP, 2 * DISP).astype(jnp.float32)
    grad_left = (jnp.einsum('hbij,hbjc->hbic', score_grad, windows) * scale).reshape(row_count, col_count, chan_count).astype(jnp.bfloat16)
    window_grad = jnp.einsum('hbij,hbic->hbjc', score_grad, left_blocks) * scale
    far_part = lax.optimization_barrier(window_grad[:, :, :DISP].astype(jnp.bfloat16)).astype(jnp.float32)
    zero_block = jnp.zeros((row_count, 1, DISP, chan_count), jnp.float32)
    ext_grad = jnp.concatenate([far_part, zero_block], axis=1) + jnp.concatenate([zero_block, window_grad[:, :, DISP:]], axis=1)
    grad_right = ext_grad.reshape(row_count, (block_count + 1) * DISP, chan_count)[:, DISP:].astype(jnp.bfloat16)
    return (new_hidden, grad_left, grad_right)
```

```python
import math

import jax
import jax.numpy as jnp
from jax import lax
from jax.experimental import pallas as pl
from jax.experimental.pallas import tpu as pltpu
from jax.sharding import PartitionSpec as P

B = 128
HALO = 4
EDGE = 16
WC = B + EDGE
F32 = jnp.float32
BF16 = jnp.bfloat16
VMEM_LIMIT = 56 * 1024 * 1024


def shift(array, axis, by):
    size = lax.axis_size(axis)
    pairs = [(i, i + by) for i in range(size) if 0 <= i + by < size]
    return lax.ppermute(array, axis, pairs)


def dot_nt(a, b):
    return lax.dot_general(a, b, (((1,), (1,)), ((), ())), preferred_element_type=F32)


def dot(a, b):
    return jnp.dot(a, b, preferred_element_type=F32)


def iota(shape, dim):
    return lax.broadcasted_iota(jnp.int32, shape, dim)


def lane_gather(values, index):
    return jnp.take_along_axis(values, index, axis=1, mode="promise_in_bounds")


def sublane_gather(values, index):
    return jnp.take_along_axis(values, index, axis=0, mode="promise_in_bounds")


def down_lanes(row):
    return jnp.transpose(jnp.broadcast_to(row, (B, B)), (1, 0))


def pick_taps(far, near, disp, taps, radius, scale):
    count = far.shape[0]
    pixel = iota((count, B), 0)
    lane = iota((count, B), 1)
    merged = jnp.where(lane > pixel, far, near)
    level = disp + lane - radius
    usable = (level >= 0) & (level < B) & (lane < taps)
    picked = lane_gather(merged, (pixel - level) & (B - 1))
    return (jnp.where(usable, picked, 0.0) * scale).astype(BF16)


def silu(v):
    return v * jax.nn.sigmoid(v)


def right_corr_kernel(
    taps, radius, scale, left_ref, own_ref, disp_ref, edge_ref, weight_ref, mot_ref, pre_ref, pad_ref
):
    rows = left_ref.shape[0]
    pad_ref[...] = jnp.zeros_like(pad_ref)
    weight = weight_ref[...]
    for r in range(rows):
        left = left_ref[r]
        far = dot_nt(left, own_ref[r, :B])
        near = dot_nt(left, own_ref[r, B:])
        disp = down_lanes(disp_ref[r])
        picked = pick_taps(far, near, disp, taps, radius, scale)
        pre = dot(picked, weight)
        pre_ref[r, :B] = pre
        mot_ref[r, :B] = silu(pre).astype(BF16)
        edge = edge_ref[r]
        chan = own_ref.shape[2]
        pad_ref[:EDGE] = edge[:, chan : 2 * chan]
        left = edge[:, :chan]
        far = dot_nt(left, own_ref[r, B:])
        near = dot_nt(left, pad_ref[...])
        disp = edge[:, 2 * chan + 2 * B : 2 * chan + 3 * B].astype(F32).astype(jnp.int32)
        picked = pick_taps(far, near, disp, taps, radius, scale)
        pre = dot(picked, weight)
        pre_ref[r, B:] = pre
        mot_ref[r, B:] = silu(pre).astype(BF16)


def left_corr_kernel(
    taps,
    radius,
    scale,
    left_ref,
    own_ref,
    before_ref,
    disp_ref,
    edge_mot_ref,
    edge_pre_ref,
    weight_ref,
    mot_ref,
    pre_ref,
):
    rows = left_ref.shape[0]
    weight = weight_ref[...]
    for r in range(rows):
        left = left_ref[r]
        far = dot_nt(left, before_ref[r])
        near = dot_nt(left, own_ref[r])
        disp = down_lanes(disp_ref[r])
        picked = pick_taps(far, near, disp, taps, radius, scale)
        pre = dot(picked, weight)
        pre_ref[r, :B] = pre
        mot_ref[r, :B] = silu(pre).astype(BF16)
        pre_ref[r, B:] = edge_pre_ref[r]
        mot_ref[r, B:] = edge_mot_ref[r]


def store3(buf, row, at, step, value):
    buf[row, :, at : at + B] = pltpu.roll(value, 1, 0).astype(BF16)
    buf[row, :, at + step : at + step + B] = value.astype(BF16)
    buf[row, :, at + 2 * step : at + 2 * step + B] = pltpu.roll(value, WC - 1, 0).astype(BF16)


def chunks(start, stop, size):
    return [list(range(i, min(i + size, stop))) for i in range(start, stop, size)]


def gather_rows(buf, rows):
    return jnp.concatenate([buf[r] for r in rows], axis=0)


def gru_kernel(
    hg_ref,
    hgt_ref,
    hgb_ref,
    mot_ref,
    mott_ref,
    motb_ref,
    pre_ref,
    wg_ref,
    wc_ref,
    wcb_ref,
    wgb_ref,
    nh_ref,
    pg_ref,
    hm_ref,
    rm_ref,
    cg_ref,
    gg_ref,
    g_ref,
    up_ref,
    rs_ref,
    cb_ref,
):
    rows = hg_ref.shape[0]
    total = rows + 2 * HALO

    def piece(top, mid, low, row):
        if row < HALO:
            return top[row]
        if row < HALO + rows:
            return mid[row - HALO]
        return low[row - HALO - rows]

    for row in range(total):
        hg = piece(hgt_ref, hg_ref, hgb_ref, row)
        g_ref[row] = hg[:, B:]
        store3(hm_ref, row, 0, 2 * B, hg[:, :B].astype(F32))
        mot = piece(mott_ref, mot_ref, motb_ref, row).astype(F32)
        left = pltpu.roll(mot, 1, 0).astype(BF16)
        mid = mot.astype(BF16)
        right = pltpu.roll(mot, WC - 1, 0).astype(BF16)
        for buf in (hm_ref, rm_ref):
            buf[row, :, B : 2 * B] = left
            buf[row, :, 3 * B : 4 * B] = mid
            buf[row, :, 5 * B : 6 * B] = right

    def hidden_at(row):
        return hm_ref[row, :, 2 * B : 3 * B].astype(F32)

    for group in chunks(1, total - 1, 4):
        acc = None
        for a in range(3):
            part = dot(gather_rows(hm_ref, [r + a - 1 for r in group]), wg_ref[a])
            acc = part if acc is None else acc + part
        acc = jax.nn.sigmoid(acc)
        for n, row in enumerate(group):
            gate = acc[n * WC : (n + 1) * WC]
            up_ref[row] = gate[:, :B]
            reset = gate[:, B:]
            rs_ref[row] = reset
            store3(rm_ref, row, 0, 2 * B, reset * hidden_at(row))

    pairs = list(range(2, total - 2, 2))
    for i in range(0, len(pairs), 4):
        group = pairs[i : i + 4]
        acc = None
        for t in range(4):
            part = dot(gather_rows(rm_ref, [r + t - 1 for r in group]), wc_ref[t])
            acc = part if acc is None else acc + part
        acc = jnp.tanh(acc)
        for n, first in enumerate(group):
            for s in range(2):
                row = first + s
                cand = acc[n * WC : (n + 1) * WC, s * B : (s + 1) * B]
                hidden = hidden_at(row)
                update = up_ref[row]
                g = g_ref[row].astype(F32)
                if HALO <= row < HALO + rows:
                    nh_ref[row - HALO] = ((1.0 - update) * hidden + update * cand).astype(BF16)
                gu = g * update
                store3(cg_ref, row, 0, B, gu * (1.0 - cand * cand))
                if 3 <= row < total - 3:
                    store3(gg_ref, row, 0, 2 * B, gu * (cand - hidden) * (1.0 - update))

    for group in chunks(3, total - 3, 4):
        lhs = jnp.concatenate(
            [gather_rows(cg_ref, [r + a - 1 for r in group]) for a in range(3)], axis=1
        )
        acc = dot(lhs, wcb_ref[...])
        for n, row in enumerate(group):
            back = acc[n * WC : (n + 1) * WC]
            reset = rs_ref[row]
            value = back[:, :B] * hidden_at(row) * reset * (1.0 - reset)
            store3(gg_ref, row, B, 2 * B, value)
            if HALO <= row < HALO + rows:
                cb_ref[row - HALO] = back[:, B:]

    pairs = list(range(HALO, HALO + rows, 2))
    for i in range(0, len(pairs), 4):
        group = pairs[i : i + 4]
        acc = None
        for t in range(4):
            part = dot(gather_rows(gg_ref, [r + t - 1 for r in group]), wgb_ref[t])
            acc = part if acc is None else acc + part
        for n, first in enumerate(group):
            for s in range(2):
                row = first + s - HALO
                grad = cb_ref[row] + acc[n * WC : (n + 1) * WC, s * B : (s + 1) * B]
                pre = pre_ref[row]
                sig = jax.nn.sigmoid(pre)
                pg_ref[row] = (grad * sig * (1.0 + pre * (1.0 - sig))).astype(BF16)


def tap_grad_kernel(pg_ref, weight_ref, out_ref):
    weight = weight_ref[...]
    for r in range(pg_ref.shape[0]):
        out_ref[r] = dot_nt(weight, pg_ref[r, :B]).astype(BF16)


def spread(grad, disp, taps, radius):
    pixel = iota((B, B), 0)
    lane = iota((B, B), 1)
    tap = ((pixel - lane) & (B - 1)) - disp + radius
    ok = (tap >= 0) & (tap < taps)
    value = jnp.where(ok, lane_gather(grad, tap & (B - 1)), 0.0)
    far = jnp.where(lane > pixel, value, 0.0).astype(BF16)
    near = jnp.where(lane > pixel, 0.0, value).astype(BF16)
    return far, near


def spread_t(grad, disp, taps, radius):
    column = iota((B, B), 0)
    pixel = iota((B, B), 1)
    tap = ((pixel - column) & (B - 1)) - disp + radius
    value = jnp.zeros((B, B), F32)
    for k in range(taps):
        value = jnp.where(tap == k, grad[k : k + 1], value)
    far = jnp.where(column > pixel, value, 0.0).astype(BF16)
    near = jnp.where(column > pixel, 0.0, value).astype(BF16)
    return far, near


def grads_kernel(
    taps,
    radius,
    scale,
    pgl_ref,
    pgr_ref,
    nhl_ref,
    nhr_ref,
    left_ref,
    own_ref,
    before_ref,
    disp_ref,
    weight_ref,
    weight_t_ref,
    nh_ref,
    gl_ref,
    gr_ref,
    near_ref,
):
    rows = left_ref.shape[0]
    weight = weight_ref[...]
    weight_t = weight_t_ref[...]
    first = iota((B, B), 0) < HALO
    for r in range(rows):
        fars = []
        nears = []
        fars_t = []
        nears_t = []
        for block in range(2):
            if block == 0:
                pre_grad = pgl_ref[r, :B].astype(F32)
                new = nhl_ref[r, :B].astype(F32)
            else:
                tail = pgl_ref[r, B:].astype(F32)
                head = pgr_ref[r, :B].astype(F32)
                pre_grad = jnp.where(first, jnp.concatenate([tail, head[EDGE:]], axis=0), head)
                tail = nhl_ref[r, B:].astype(F32)
                head = nhr_ref[r, :B].astype(F32)
                new = jnp.where(first, jnp.concatenate([tail, head[EDGE:]], axis=0), head)
            nh_ref[r, block * B : (block + 1) * B] = new.astype(BF16)
            pre_grad = pre_grad.astype(BF16)
            row = disp_ref[r, :, block * B : (block + 1) * B]
            grad = dot(pre_grad, weight).astype(BF16).astype(F32)
            far, near = spread(grad, down_lanes(row), taps, radius)
            fars.append(far)
            nears.append(near)
            grad = dot_nt(weight_t, pre_grad).astype(BF16).astype(F32)
            far, near = spread_t(grad, row, taps, radius)
            fars_t.append(far)
            nears_t.append(near)
        window = jnp.concatenate([before_ref[r], own_ref[r, :B]], axis=0)
        sg = jnp.concatenate([fars[0], nears[0]], axis=1)
        gl_ref[r, :B] = (dot(sg, window) * scale).astype(BF16)
        sg = jnp.concatenate([fars[1], nears[1]], axis=1)
        gl_ref[r, B:] = (dot(sg, own_ref[r]) * scale).astype(BF16)
        sg = jnp.concatenate([nears_t[0], fars_t[1]], axis=1)
        gr_ref[r] = (dot(sg, left_ref[r]) * scale).astype(BF16)
        near_ref[r] = nears_t[1]


def last_kernel(
    taps, radius, scale, near_ref, grad_ref, disp_ref, left_ref, next_ref, first_ref, gr_ref
):
    rows = left_ref.shape[0]
    for r in range(rows):
        far, _ = spread_t(grad_ref[r].astype(F32), disp_ref[r], taps, radius)
        sg = jnp.concatenate([near_ref[r], far], axis=1)
        window = jnp.concatenate([left_ref[r], next_ref[r]], axis=0)
        gr_ref[r, :B] = first_ref[r]
        gr_ref[r, B:] = (dot(sg, window) * scale).astype(BF16)


def whole(array):
    nd = array.ndim
    return pl.BlockSpec(array.shape, lambda i: (0,) * nd)


def by_rows(array, size, block=None, at=None):
    block = tuple(array.shape[1:]) if block is None else block
    at = (0,) * len(block) if at is None else at
    return pl.BlockSpec((size,) + block, lambda i: (i,) + at)


def per_device(
    feat_left, feat_right, hidden, disparity, motion_weight, gate_weight, cand_weight, grad_hidden
):
    rows, cols, chan = feat_left.shape
    taps = motion_weight.shape[0]
    radius = taps // 2
    scale = 1.0 / math.sqrt(chan)
    args = (taps, radius, scale)
    size = 4
    grid = (rows // size,)
    params = pltpu.CompilerParams(vmem_limit_bytes=VMEM_LIMIT)

    pack = jnp.concatenate(
        [
            feat_left[:, :HALO],
            feat_right[:, :HALO],
            hidden[:, :HALO],
            grad_hidden[:, :HALO],
            jnp.broadcast_to(disparity[:, :HALO, None].astype(BF16), (rows, HALO, B)),
        ],
        axis=2,
    )
    from_right = shift(pack, "cols", -1)
    hg = jnp.concatenate([hidden, grad_hidden], axis=2)
    from_left = shift(hg[:, cols - HALO :], "cols", 1)
    before = shift(feat_right[:, cols - B :], "cols", 1)
    edge = jnp.pad(from_right, ((0, 0), (0, EDGE - HALO), (0, 0)))
    hg_right = jnp.concatenate([hg[:, B:], edge[:, :, 2 * chan : 2 * chan + 2 * B]], axis=1)
    hg_left = jnp.concatenate(
        [hg[:, : B + 8], jnp.zeros((rows, 8 - HALO, 2 * B), BF16), from_left], axis=1
    )

    def row_halo(array):
        return shift(array[rows - HALO :], "rows", 1), shift(array[:HALO], "rows", -1)

    hg_right_t, hg_right_b = row_halo(hg_right)

    wg = gate_weight.reshape(3, 3 * 2 * B, 2 * B)

    def paired(weight):
        return jnp.concatenate(
            [
                jnp.pad(weight, ((0, 1), (0, 0), (0, 0))),
                jnp.pad(weight, ((1, 0), (0, 0), (0, 0))),
            ],
            axis=2,
        )

    def flipped(weight):
        return jnp.transpose(weight[::-1, ::-1], (0, 1, 3, 2))

    wc = paired(cand_weight.reshape(3, 3 * 2 * B, B))
    wcb = flipped(cand_weight).reshape(9 * B, 2 * B)
    wgb = paired(flipped(gate_weight[:, :, B:]).reshape(3, 3 * 2 * B, B))
    mw = jnp.pad(motion_weight, ((0, B - taps), (0, 0)))
    mw_t = jnp.pad(motion_weight.T, ((0, 0), (0, B - taps)))
    mw16 = jnp.pad(motion_weight, ((0, 16 - taps), (0, 0)))
    disp3 = disparity[:, None, :]

    mot_shapes = (
        jax.ShapeDtypeStruct((rows, WC, B), BF16),
        jax.ShapeDtypeStruct((rows, WC, B), F32),
    )

    def cost(flops, bytes_accessed):
        return pl.CostEstimate(flops=flops, bytes_accessed=bytes_accessed, transcendentals=0)

    mot_right, pre_right = pl.pallas_call(
        lambda *refs: right_corr_kernel(*args, *refs),
        grid=grid,
        in_specs=[
            by_rows(feat_left, size, (B, chan), (1, 0)),
            by_rows(feat_right, size),
            by_rows(disp3, size, (1, B), (0, 1)),
            by_rows(edge, size),
            whole(mw),
        ],
        out_specs=[by_rows(s, size) for s in mot_shapes],
        out_shape=mot_shapes,
        scratch_shapes=[pltpu.VMEM((B, chan), BF16)],
        compiler_params=params,
        cost_estimate=cost(2 * rows * B * 2 * B * chan, 6 << 20),
        name="corr_right",
    )(feat_left, feat_right, disp3, edge, mw)
    mot_right_t, mot_right_b = row_halo(mot_right)
    mot_from_left = shift(mot_right[:, B - HALO : B], "cols", 1)

    gru_rows = rows + 2 * HALO

    def gru(hg_parts, mot_parts, pre, name):
        operands = (*hg_parts, *mot_parts, pre, wg, wc, wcb, wgb)
        out = jax.ShapeDtypeStruct((rows, WC, B), BF16)
        return pl.pallas_call(
            gru_kernel,
            out_shape=(out, out),
            in_specs=[pl.BlockSpec(memory_space=pltpu.VMEM)] * len(operands),
            out_specs=[pl.BlockSpec(memory_space=pltpu.VMEM)] * 2,
            scratch_shapes=[
                pltpu.VMEM((gru_rows, WC, 6 * B), BF16),
                pltpu.VMEM((gru_rows, WC, 6 * B), BF16),
                pltpu.VMEM((gru_rows, WC, 3 * B), BF16),
                pltpu.VMEM((gru_rows, WC, 6 * B), BF16),
                pltpu.VMEM((gru_rows, WC, B), BF16),
                pltpu.VMEM((gru_rows, WC, B), F32),
                pltpu.VMEM((gru_rows, WC, B), F32),
                pltpu.VMEM((rows, WC, B), F32),
            ],
            compiler_params=params,
            cost_estimate=cost(2 * 22 * WC * 256 * 256 * 24, 12 << 20),
            name=name,
        )(*operands)

    nh_right, pg_right = gru(
        (hg_right, hg_right_t, hg_right_b), (mot_right, mot_right_t, mot_right_b), pre_right, "gru_right"
    )

    hg_left_t, hg_left_b = row_halo(hg_left)
    edge_mot = jnp.concatenate(
        [mot_right[:, :8], jnp.zeros((rows, 8 - HALO, B), BF16), mot_from_left], axis=1
    )
    edge_pre = pre_right[:, :EDGE]
    mot_left, pre_left = pl.pallas_call(
        lambda *refs: left_corr_kernel(*args, *refs),
        grid=grid,
        in_specs=[
            by_rows(feat_left, size, (B, chan), (0, 0)),
            by_rows(feat_right, size, (B, chan), (0, 0)),
            by_rows(before, size),
            by_rows(disp3, size, (1, B), (0, 0)),
            by_rows(edge_mot, size),
            by_rows(edge_pre, size),
            whole(mw),
        ],
        out_specs=[by_rows(s, size) for s in mot_shapes],
        out_shape=mot_shapes,
        compiler_params=params,
        cost_estimate=cost(2 * rows * B * 2 * B * chan, 6 << 20),
        name="corr_left",
    )(feat_left, feat_right, before, disp3, edge_mot, edge_pre, mw)
    mot_left_t, mot_left_b = row_halo(mot_left)
    first_left, _ = lax.optimization_barrier((feat_left[:, :B], before))
    next_left = shift(first_left, "cols", -1)
    next_disp = shift(disp3[:, :, :B], "cols", -1)
    nh_left, pg_left = gru(
        (hg_left, hg_left_t, hg_left_b), (mot_left, mot_left_t, mot_left_b), pre_left, "gru_left"
    )
    tap_grad = pl.pallas_call(
        tap_grad_kernel,
        out_shape=jax.ShapeDtypeStruct((rows, 16, B), BF16),
        name="tap_grad",
        cost_estimate=cost(1 << 20, 1 << 20),
    )(pg_left, mw16)
    next_grad = shift(tap_grad, "cols", -1)

    out = jax.ShapeDtypeStruct
    grad_shapes = (
        out((rows, cols, B), BF16),
        out((rows, cols, chan), BF16),
        out((rows, B, chan), BF16),
        out((rows, B, B), BF16),
    )
    new_hidden, grad_left, grad_first, near = pl.pallas_call(
        lambda *refs: grads_kernel(*args, *refs),
        grid=grid,
        in_specs=[
            by_rows(pg_left, size),
            by_rows(pg_right, size),
            by_rows(nh_left, size),
            by_rows(nh_right, size),
            by_rows(feat_left, size),
            by_rows(feat_right, size),
            by_rows(before, size),
            by_rows(disp3, size),
            whole(mw_t),
            whole(mw16),
        ],
        out_specs=[by_rows(s, size) for s in grad_shapes],
        out_shape=grad_shapes,
        compiler_params=params,
        cost_estimate=cost(2 * rows * B * 2 * B * chan * 4, 12 << 20),
        name="grads",
    )(pg_left, pg_right, nh_left, nh_right, feat_left, feat_right, before, disp3, mw_t, mw16)
    grad_right = pl.pallas_call(
        lambda *refs: last_kernel(*args, *refs),
        grid=grid,
        in_specs=[
            by_rows(near, size),
            by_rows(next_grad, size),
            by_rows(next_disp, size),
            by_rows(feat_left, size, (B, chan), (1, 0)),
            by_rows(next_left, size),
            by_rows(grad_first, size),
        ],
        out_specs=by_rows(out((rows, cols, chan), BF16), size),
        out_shape=out((rows, cols, chan), BF16),
        compiler_params=params,
        cost_estimate=cost(2 * rows * B * 2 * B * chan, 6 << 20),
        name="grad_right",
    )(near, next_grad, next_disp, feat_left, next_left, grad_first)
    return (new_hidden, grad_left, grad_right)


def solution(mesh):
    grid3 = P("rows", "cols", None)
    return jax.shard_map(
        per_device,
        mesh=mesh,
        in_specs=(grid3, grid3, grid3, P("rows", "cols"), P(), P(), P(), grid3),
        out_specs=(grid3, grid3, grid3),
        check_vma=False,
    )
```

```python
import math

import jax
import jax.numpy as jnp
from jax import lax
from jax.experimental import pallas as pl
from jax.experimental.pallas import tpu as pltpu
from jax.sharding import PartitionSpec as P

B = 128
HALO = 4
EDGE = 16
F32 = jnp.float32
BF16 = jnp.bfloat16
VMEM_LIMIT = 56 * 1024 * 1024


def shift(array, axis, by):
    size = lax.axis_size(axis)
    pairs = [(i, i + by) for i in range(size) if 0 <= i + by < size]
    return lax.ppermute(array, axis, pairs)


def dot_nt(a, b):
    return lax.dot_general(a, b, (((1,), (1,)), ((), ())), preferred_element_type=F32)


def dot(a, b):
    return jnp.dot(a, b, preferred_element_type=F32)


def iota(shape, dim):
    return lax.broadcasted_iota(jnp.int32, shape, dim)


def lane_gather(values, index):
    return jnp.take_along_axis(values, index, axis=1, mode="promise_in_bounds")


def sublane_gather(values, index):
    return jnp.take_along_axis(values, index, axis=0, mode="promise_in_bounds")


def down_lanes(row):
    return jnp.transpose(jnp.broadcast_to(row, (B, B)), (1, 0))


def pick_taps(far, near, disp, taps, radius, scale, first=0):
    count = far.shape[0]
    pixel = iota((count, B), 0) + first
    lane = iota((count, B), 1)
    merged = jnp.where(lane > pixel, far, near)
    level = disp + lane - radius
    usable = (level >= 0) & (level < B) & (lane < taps)
    picked = lane_gather(merged, (pixel - level) & (B - 1))
    return (jnp.where(usable, picked, 0.0) * scale).astype(BF16)


def silu(v):
    return v * jax.nn.sigmoid(v)


def edge_disp(values):
    return values[:, :B].astype(jnp.int32)


def right_corr_kernel(
    taps, radius, scale, left_ref, own_ref, disp_ref, edge_ref, weight_ref, mot_ref, pre_ref, pad_ref
):
    rows, _, chan = own_ref.shape
    pad_ref[...] = jnp.zeros_like(pad_ref)
    weight = weight_ref[...]
    for r in range(rows):
        edge = edge_ref[r]
        pad_ref[:EDGE] = edge[:, chan : 2 * chan]
        side = edge[:, :chan]
        scores = dot_nt(jnp.concatenate([left_ref[r], side], axis=0), own_ref[r])
        disp = down_lanes(disp_ref[r])
        main = pick_taps(scores[:B, :B], scores[:B, B:], disp, taps, radius, scale)
        disp = edge[:, 2 * chan + 2 * B :].astype(F32).astype(jnp.int32)
        beside = pick_taps(
            scores[B:, B:], dot_nt(side, pad_ref[...]), disp, taps, radius, scale
        )
        pre = dot(jnp.concatenate([main, beside], axis=0), weight)
        pre_ref[r] = pre[:B]
        mot_ref[r] = silu(pre).astype(BF16)


def left_corr_kernel(
    taps,
    radius,
    scale,
    left_ref,
    own_ref,
    before_ref,
    disp_ref,
    mot_right_ref,
    weight_ref,
    mot_ref,
    top_ref,
    low_ref,
    pre_ref,
    pad_ref,
):
    rows, _, chan = own_ref.shape
    step = pl.program_id(0)
    pad_ref[...] = jnp.zeros_like(pad_ref)
    weight = weight_ref[...]
    last = iota((EDGE, chan), 0) >= EDGE - HALO
    upper = iota((EDGE, B), 0) < EDGE // 2
    for r in range(rows):
        extra = before_ref[r, B:].astype(F32)
        pad_ref[B - EDGE :] = jnp.where(last, pltpu.roll(extra, 12, 0), 0.0).astype(BF16)
        side = jnp.where(last, pltpu.roll(extra, 8, 0), 0.0).astype(BF16)
        window = jnp.concatenate([before_ref[r, :B], own_ref[r]], axis=0)
        scores = dot_nt(jnp.concatenate([left_ref[r], side], axis=0), window)
        disp = down_lanes(disp_ref[r])
        main = pick_taps(scores[:B, :B], scores[:B, B:], disp, taps, radius, scale)
        disp = pltpu.roll(extra, 4, 0)[:, :B].astype(jnp.int32)
        beside = pick_taps(
            dot_nt(side, pad_ref[...]), scores[B:, :B], disp, taps, radius, scale, B - EDGE
        )
        pre = dot(jnp.concatenate([main, beside], axis=0), weight)
        pre_ref[r] = pre[:B]
        mot = silu(pre)
        mot_ref[r, :B] = mot[:B].astype(BF16)
        mot_ref[r, B : 2 * B] = mot_right_ref[r, :B]
        right_edge = mot_right_ref[r, B:].astype(F32)
        mot_ref[r, 2 * B :] = jnp.where(upper, right_edge, mot[B:]).astype(BF16)

    @pl.when(step == 0)
    def _():
        top_ref[...] = mot_ref[...]

    @pl.when(step == pl.num_programs(0) - 1)
    def _():
        low_ref[...] = mot_ref[...]


def shifted(value):
    return (
        pltpu.roll(value, 1, 0).astype(BF16),
        value.astype(BF16),
        pltpu.roll(value, value.shape[0] - 1, 0).astype(BF16),
    )


def store3(buf, row, value):
    for b, part in enumerate(shifted(value)):
        buf[row, :, b * B : (b + 1) * B] = part


def lanes(buf, rows, b):
    return jnp.concatenate([buf[r, :, b * B : (b + 1) * B] for r in rows], axis=0)


def patches(bufs, row_sets):
    return jnp.concatenate(
        [lanes(buf, rows, b) for rows in row_sets for b in range(3) for buf in bufs], axis=1
    )


def chunks(values, size):
    values = list(values)
    return [values[i : i + size] for i in range(0, len(values), size)]


CHUNK = 2


def gru_kernel(
    hid_ref,
    grad_ref,
    side_ref,
    hgt_ref,
    hgb_ref,
    mot_ref,
    mott_ref,
    motb_ref,
    prel_ref,
    prer_ref,
    disp_ref,
    wg_ref,
    wc_ref,
    wcb_ref,
    wgb_ref,
    mw_ref,
    nh_ref,
    pg_ref,
    tg_ref,
    h3_ref,
    m3_ref,
    r3_ref,
    c3_ref,
    h_ref,
    g_ref,
    up_ref,
    rs_ref,
    cb_ref,
):
    rows, own, _ = hid_ref.shape
    wide = own + EDGE
    total = rows + 2 * HALO
    inner = range(HALO, HALO + rows)

    for row in range(total):
        if row in inner:
            h_ref[row, :own] = hid_ref[row - HALO]
            h_ref[row, own:] = side_ref[row - HALO, :, :B]
            g_ref[row, :own] = grad_ref[row - HALO]
            g_ref[row, own:] = side_ref[row - HALO, :, B:]
            mot = mot_ref[row - HALO]
        elif row < HALO:
            h_ref[row] = hgt_ref[row, :, :B]
            g_ref[row] = hgt_ref[row, :, B:]
            mot = mott_ref[row]
        else:
            h_ref[row] = hgb_ref[row - HALO - rows, :, :B]
            g_ref[row] = hgb_ref[row - HALO - rows, :, B:]
            mot = motb_ref[row - HALO - rows]
        store3(h3_ref, row, h_ref[row].astype(F32))
        store3(m3_ref, row, mot.astype(F32))

    for group in chunks(range(1, total - 1), CHUNK * 2):
        lhs = patches((h3_ref, m3_ref), [[r + a - 1 for r in group] for a in range(3)])
        acc = jax.nn.sigmoid(dot(lhs, wg_ref[...]))
        for n, row in enumerate(group):
            gate = acc[n * wide : (n + 1) * wide]
            up_ref[row] = gate[:, :B]
            reset = gate[:, B:]
            rs_ref[row] = reset
            store3(r3_ref, row, reset * h_ref[row].astype(F32))

    for group in chunks(range(2, total - 2, 2), CHUNK * 2):
        lhs = patches((r3_ref, m3_ref), [[r + t - 1 for r in group] for t in range(4)])
        acc = jnp.tanh(dot(lhs, wc_ref[...]))
        for n, first in enumerate(group):
            for row in (first, first + 1):
                s = row - first
                cand = acc[n * wide : (n + 1) * wide, s * B : (s + 1) * B]
                hidden = h_ref[row].astype(F32)
                update = up_ref[row]
                if row in inner:
                    new = (1.0 - update) * hidden + update * cand
                    nh_ref[row - HALO] = new[:own].astype(BF16)
                gu = g_ref[row].astype(F32) * update
                store3(c3_ref, row, gu * (1.0 - cand * cand))
                store3(h3_ref, row, gu * (cand - hidden) * (1.0 - update))

    for group in chunks(range(3, total - 3), CHUNK * 2):
        lhs = patches((c3_ref,), [[r + a - 1 for r in group] for a in range(3)])
        acc = dot(lhs, wcb_ref[...])
        for n, row in enumerate(group):
            back = acc[n * wide : (n + 1) * wide]
            reset = rs_ref[row]
            store3(m3_ref, row, back[:, :B] * h_ref[row].astype(F32) * reset * (1.0 - reset))
            if row in inner:
                cb_ref[row - HALO] = back[:own, B:]

    for group in chunks(range(HALO, HALO + rows, 2), CHUNK * 2):
        lhs = patches((h3_ref, m3_ref), [[r + t - 1 for r in group] for t in range(4)])
        acc = dot(lhs, wgb_ref[...])
        for n, first in enumerate(group):
            for row in (first - HALO, first + 1 - HALO):
                s = row + HALO - first
                back = acc[n * wide : n * wide + own, s * B : (s + 1) * B]
                pre = jnp.concatenate([prel_ref[row], prer_ref[row]], axis=0)
                sig = jax.nn.sigmoid(pre)
                grad = (cb_ref[row] + back) * sig * (1.0 + pre * (1.0 - sig))
                grad = grad.astype(BF16)
                pg_ref[row] = grad
                tap = dot_nt(mw_ref[...], grad[:B])
                level = jnp.broadcast_to(disp_ref[row, :, :B].astype(F32), tap.shape)
                tg_ref[row] = jnp.where(iota(tap.shape, 0) == 15, level, tap).astype(BF16)


def spread(grad, disp, taps, radius):
    pixel = iota((B, B), 0)
    lane = iota((B, B), 1)
    tap = ((pixel - lane) & (B - 1)) - disp + radius
    ok = (tap >= 0) & (tap < taps)
    value = jnp.where(ok, lane_gather(grad, tap & (B - 1)), 0.0)
    far = jnp.where(lane > pixel, value, 0.0).astype(BF16)
    near = jnp.where(lane > pixel, 0.0, value).astype(BF16)
    return far, near


def spread_t(grad, disp, taps, radius):
    column = iota((B, B), 0)
    pixel = iota((B, B), 1)
    tap = ((pixel - column) & (B - 1)) - disp + radius
    value = jnp.zeros((B, B), F32)
    for k in range(taps):
        value = jnp.where(tap == k, grad[k : k + 1], value)
    far = jnp.where(column > pixel, value, 0.0).astype(BF16)
    near = jnp.where(column > pixel, 0.0, value).astype(BF16)
    return far, near


def grads_kernel(
    taps,
    radius,
    scale,
    pg_ref,
    left_ref,
    own_ref,
    before_ref,
    disp_ref,
    weight_ref,
    weight_t_ref,
    gl_ref,
    gr_ref,
    near_ref,
):
    rows = left_ref.shape[0]
    weight = weight_ref[...]
    weight_t = weight_t_ref[...]
    for r in range(rows):
        grads = dot(pg_ref[r], weight).astype(BF16).astype(F32)
        grads_t = dot_nt(weight_t, pg_ref[r]).astype(BF16).astype(F32)
        parts = []
        parts_t = []
        for block in range(2):
            at = slice(block * B, (block + 1) * B)
            row = disp_ref[r, :, at]
            parts.append(spread(grads[at], down_lanes(row), taps, radius))
            parts_t.append(spread_t(grads_t[:, at], row, taps, radius))
        window = jnp.concatenate([before_ref[r, :B], own_ref[r, :B]], axis=0)
        gl_ref[r, :B] = (dot(jnp.concatenate(parts[0], axis=1), window) * scale).astype(BF16)
        gl_ref[r, B:] = (dot(jnp.concatenate(parts[1], axis=1), own_ref[r]) * scale).astype(BF16)
        sg = jnp.concatenate([parts_t[0][1], parts_t[1][0]], axis=1)
        gr_ref[r] = (dot(sg, left_ref[r]) * scale).astype(BF16)
        near_ref[r] = parts_t[1][1]


def last_kernel(taps, radius, scale, near_ref, grad_ref, left_ref, next_ref, first_ref, gr_ref):
    del first_ref
    rows = left_ref.shape[0]
    for r in range(rows):
        grad = grad_ref[r].astype(F32)
        disp = grad[15:16].astype(jnp.int32)
        far, _ = spread_t(grad, disp, taps, radius)
        sg = jnp.concatenate([near_ref[r], far], axis=1)
        window = jnp.concatenate([left_ref[r], next_ref[r]], axis=0)
        gr_ref[r] = (dot(sg, window) * scale).astype(BF16)


def whole(array):
    nd = array.ndim
    return pl.BlockSpec(array.shape, lambda i: (0,) * nd)


def by_rows(array, size, block=None, at=None):
    block = tuple(array.shape[1:]) if block is None else block
    at = (0,) * len(block) if at is None else at
    return pl.BlockSpec((size,) + block, lambda i: (i,) + at)


def cost(flops, bytes_accessed):
    return pl.CostEstimate(flops=flops, bytes_accessed=bytes_accessed, transcendentals=0)


def paired(weight):
    rows = [
        jnp.pad(weight, ((0, 1), (0, 0), (0, 0))),
        jnp.pad(weight, ((1, 0), (0, 0), (0, 0))),
    ]
    return jnp.concatenate(rows, axis=2).reshape(-1, 2 * B)


def flipped(weight):
    return jnp.transpose(weight[::-1, ::-1], (0, 1, 3, 2))


def per_device(
    feat_left, feat_right, hidden, disparity, motion_weight, gate_weight, cand_weight, grad_hidden
):
    rows, cols, chan = feat_left.shape
    taps = motion_weight.shape[0]
    radius = taps // 2
    scale = 1.0 / math.sqrt(chan)
    args = (taps, radius, scale)
    size = 4
    grid = (rows // size,)
    wide = cols + EDGE
    params = pltpu.CompilerParams(vmem_limit_bytes=VMEM_LIMIT)
    shape = jax.ShapeDtypeStruct

    level = disparity.astype(BF16)[:, :, None]
    before = shift(
        jnp.concatenate(
            [
                feat_right[:, cols - B :],
                feat_right[:, cols - B - HALO : cols - B],
                feat_left[:, cols - HALO :],
                jnp.broadcast_to(level[:, cols - HALO :], (rows, HALO, chan)),
                jnp.zeros((rows, HALO, chan), BF16),
            ],
            axis=1,
        ),
        "cols",
        1,
    )
    from_right = shift(
        jnp.concatenate(
            [
                feat_left[:, :HALO],
                feat_right[:, :HALO],
                hidden[:, :HALO],
                grad_hidden[:, :HALO],
                jnp.broadcast_to(level[:, :HALO], (rows, HALO, B)),
            ],
            axis=2,
        ),
        "cols",
        -1,
    )
    from_left = shift(
        jnp.concatenate([hidden[:, cols - HALO :], grad_hidden[:, cols - HALO :]], axis=2), "cols", 1
    )
    edge = jnp.pad(from_right, ((0, 0), (0, EDGE - HALO), (0, 0)))
    side = jnp.concatenate(
        [
            from_right[:, :, 2 * chan : 2 * chan + 2 * B],
            jnp.zeros((rows, EDGE - 2 * HALO, 2 * B), BF16),
            from_left,
        ],
        axis=1,
    )

    def rim(at):
        own = jnp.concatenate([hidden[at : at + HALO], grad_hidden[at : at + HALO]], axis=2)
        return jnp.concatenate([own, side[at : at + HALO]], axis=1)

    hg_top = shift(rim(rows - HALO), "rows", 1)
    hg_low = shift(rim(0), "rows", -1)

    wg = gate_weight.reshape(-1, 2 * B)
    wc = paired(cand_weight.reshape(3, 6 * B, B))
    wcb = flipped(cand_weight).reshape(-1, 2 * B)
    wgb = paired(flipped(gate_weight[:, :, B:]).reshape(3, 6 * B, B))
    mw = jnp.pad(motion_weight, ((0, B - taps), (0, 0)))
    mw_t = jnp.pad(motion_weight.T, ((0, 0), (0, B - taps)))
    mw16 = jnp.pad(motion_weight, ((0, 16 - taps), (0, 0)))
    disp3 = disparity[:, None, :]

    pad = [pltpu.VMEM((B, chan), BF16)]
    lookup_cost = cost(2 * rows * B * 2 * B * chan, 6 << 20)
    right_shapes = (shape((rows, B + EDGE, B), BF16), shape((rows, B, B), F32))
    mot_right, pre_right = pl.pallas_call(
        lambda *refs: right_corr_kernel(*args, *refs),
        grid=grid,
        in_specs=[
            by_rows(feat_left, size, (B, chan), (1, 0)),
            by_rows(feat_right, size),
            by_rows(disp3, size, (1, B), (0, 1)),
            by_rows(edge, size),
            whole(mw),
        ],
        out_specs=[by_rows(s, size) for s in right_shapes],
        out_shape=right_shapes,
        scratch_shapes=pad,
        compiler_params=params,
        cost_estimate=lookup_cost,
        name="corr_right",
    )(feat_left, feat_right, disp3, edge, mw)

    mot_shape = shape((rows, wide, B), BF16)
    rim_shape = shape((HALO, wide, B), BF16)
    motion, mot_first, mot_last, pre_left = pl.pallas_call(
        lambda *refs: left_corr_kernel(*args, *refs),
        grid=grid,
        in_specs=[
            by_rows(feat_left, size, (B, chan), (0, 0)),
            by_rows(feat_right, size, (B, chan), (0, 0)),
            by_rows(before, size),
            by_rows(disp3, size, (1, B), (0, 0)),
            by_rows(mot_right, size),
            whole(mw),
        ],
        out_specs=[
            by_rows(mot_shape, size),
            whole(rim_shape),
            whole(rim_shape),
            by_rows(right_shapes[1], size),
        ],
        out_shape=(mot_shape, rim_shape, rim_shape, right_shapes[1]),
        scratch_shapes=pad,
        compiler_params=params,
        cost_estimate=lookup_cost,
        name="corr_left",
    )(feat_left, feat_right, before, disp3, mot_right, mw)
    mot_top = shift(mot_last, "rows", 1)
    mot_low = shift(mot_first, "rows", -1)
    first_left, _ = lax.optimization_barrier((feat_left[:, :B], motion))
    next_left = shift(first_left, "cols", -1)

    total = rows + 2 * HALO
    own_shape = shape((rows, cols, B), BF16)
    operands = (
        hidden,
        grad_hidden,
        side,
        hg_top,
        hg_low,
        motion,
        mot_top,
        mot_low,
        pre_left,
        pre_right,
        disp3,
        wg,
        wc,
        wcb,
        wgb,
        mw16,
    )
    vmem = pl.BlockSpec(memory_space=pltpu.VMEM)
    new_hidden, pre_grad, tap_grad = pl.pallas_call(
        gru_kernel,
        in_specs=[vmem] * len(operands),
        out_specs=[vmem] * 3,
        out_shape=(own_shape, own_shape, shape((rows, 16, B), BF16)),
        scratch_shapes=[pltpu.VMEM((total, wide, 3 * B), BF16)] * 4
        + [pltpu.VMEM((total, wide, B), BF16)] * 2
        + [pltpu.VMEM((total, wide, B), F32)] * 2
        + [pltpu.VMEM((rows, cols, B), F32)],
        compiler_params=params,
        cost_estimate=cost(2 * 22 * wide * 256 * 256 * 24, 16 << 20),
        name="gru",
    )(*operands)
    next_grad = shift(tap_grad, "cols", -1)

    feat_shape = shape((rows, cols, chan), BF16)
    near_shape = shape((rows, B, B), BF16)
    grad_left, grad_first, near = pl.pallas_call(
        lambda *refs: grads_kernel(*args, *refs),
        grid=grid,
        in_specs=[
            by_rows(pre_grad, size),
            by_rows(feat_left, size),
            by_rows(feat_right, size),
            by_rows(before, size),
            by_rows(disp3, size),
            whole(mw_t),
            whole(mw16),
        ],
        out_specs=[
            by_rows(feat_shape, size),
            by_rows(feat_shape, size, (B, chan), (0, 0)),
            by_rows(near_shape, size),
        ],
        out_shape=(feat_shape, feat_shape, near_shape),
        compiler_params=params,
        cost_estimate=cost(2 * rows * B * 2 * B * chan * 4, 12 << 20),
        name="grads",
    )(pre_grad, feat_left, feat_right, before, disp3, mw_t, mw16)
    grad_right = pl.pallas_call(
        lambda *refs: last_kernel(*args, *refs),
        grid=grid,
        in_specs=[
            by_rows(near, size),
            by_rows(next_grad, size),
            by_rows(feat_left, size, (B, chan), (1, 0)),
            by_rows(next_left, size),
            pl.BlockSpec(memory_space=pl.ANY),
        ],
        out_specs=by_rows(feat_shape, size, (B, chan), (1, 0)),
        out_shape=feat_shape,
        input_output_aliases={4: 0},
        compiler_params=params,
        cost_estimate=cost(2 * rows * B * 2 * B * chan, 4 << 20),
        name="grad_right",
    )(near, next_grad, feat_left, next_left, grad_first)
    return (new_hidden, grad_left, grad_right)


def solution(mesh):
    grid3 = P("rows", "cols", None)
    return jax.shard_map(
        per_device,
        mesh=mesh,
        in_specs=(grid3, grid3, grid3, P("rows", "cols"), P(), P(), P(), grid3),
        out_specs=(grid3, grid3, grid3),
        check_vma=False,
    )
```

```python
import math

import jax
import jax.numpy as jnp
from jax import lax
from jax.experimental import pallas as pl
from jax.experimental.pallas import tpu as pltpu
from jax.sharding import PartitionSpec as P

B = 128
HALO = 4
EDGE = 16
F32 = jnp.float32
BF16 = jnp.bfloat16
ROWS = 4
SMALL_VMEM = 16 * 1024 * 1024
GRU_VMEM = 56 * 1024 * 1024


def shift(array, axis, by):
    size = lax.axis_size(axis)
    pairs = [(i, i + by) for i in range(size) if 0 <= i + by < size]
    return lax.ppermute(array, axis, pairs)


def dot_nt(a, b):
    return lax.dot_general(a, b, (((1,), (1,)), ((), ())), preferred_element_type=F32)


def dot(a, b):
    return jnp.dot(a, b, preferred_element_type=F32)


def iota(shape, dim):
    return lax.broadcasted_iota(jnp.int32, shape, dim)


def lane_gather(values, index):
    return jnp.take_along_axis(values, index, axis=1, mode="promise_in_bounds")


def down_lanes(row):
    return jnp.transpose(jnp.broadcast_to(row, (B, B)), (1, 0))


def pick_taps(far, near, disp, taps, radius, scale, first=0):
    count = far.shape[0]
    pixel = iota((count, B), 0) + first
    lane = iota((count, B), 1)
    merged = jnp.where(lane > pixel, far, near)
    level = disp + lane - radius
    usable = (level >= 0) & (level < B) & (lane < taps)
    picked = lane_gather(merged, (pixel - level) & (B - 1))
    return (jnp.where(usable, picked, 0.0) * scale).astype(BF16)


def silu(v):
    return v * jax.nn.sigmoid(v)


def level_columns(disp_ref, at):
    return jnp.transpose(disp_ref[:, at : at + B].astype(F32), (1, 0))


def level_row(disp_ref, row, at):
    levels = disp_ref[:, at : at + B]
    return jnp.sum(jnp.where(iota(levels.shape, 0) == row, levels, 0), axis=0, keepdims=True)


def pack_left_kernel(left_ref, own_ref, hid_ref, grad_ref, disp_ref, out_ref):
    rows, _, chan = left_ref.shape
    levels = level_columns(disp_ref, 0)
    for r in range(rows):
        out_ref[r, :, :chan] = left_ref[r, :HALO]
        out_ref[r, :, chan : 2 * chan] = own_ref[r, :HALO]
        out_ref[r, :, 2 * chan : 2 * chan + B] = hid_ref[r, :HALO]
        out_ref[r, :, 2 * chan + B : 2 * chan + 2 * B] = grad_ref[r, :HALO]
        level = jnp.broadcast_to(levels[:8, r : r + 1], (8, B))
        out_ref[r, :, 2 * chan + 2 * B :] = level.astype(BF16)[:HALO]


def pack_right_kernel(
    start, own_ref, beside_ref, left_ref, hid_ref, grad_ref, disp_ref, out_ref
):
    rows, _, chan = own_ref.shape
    first = start + pl.program_id(0) * rows
    low = iota((8, chan), 0) < HALO
    for r in range(rows):
        out_ref[r, :B] = own_ref[r]
        beside = pltpu.roll(beside_ref[r].astype(F32), HALO, 0)
        upper = jnp.where(low, beside, left_ref[r].astype(F32))
        row = level_row(disp_ref, first + r, disp_ref.shape[1] - B).astype(F32)
        level = jnp.transpose(jnp.broadcast_to(row, (8, B)), (1, 0))[B - 8 :, :1]
        level = pltpu.roll(jnp.broadcast_to(level, (8, chan)), HALO, 0)
        hg = jnp.concatenate([hid_ref[r], grad_ref[r]], axis=1).astype(F32)
        out_ref[r, B:] = jnp.concatenate([upper, jnp.where(low, level, hg)], axis=0).astype(BF16)


def rim_kernel(
    hid_first_ref, grad_first_ref, hid_last_ref, grad_last_ref, side_ref, first_ref, last_ref, edge_ref, pad_ref
):
    rows = side_ref.shape[0]
    own = hid_first_ref.shape[1]
    chan = (side_ref.shape[2] - 3 * B) // 2
    pad_ref[...] = jnp.zeros_like(pad_ref)
    for r in range(rows):
        pad_ref[:HALO] = side_ref[r, :, 2 * chan : 2 * chan + 2 * B].astype(F32)
        edge_ref[r] = pad_ref[...].astype(BF16)
    for r in range(HALO):
        for out, hid, grad, row in (
            (first_ref, hid_first_ref, grad_first_ref, r),
            (last_ref, hid_last_ref, grad_last_ref, rows - HALO + r),
        ):
            out[r, :own, :B] = hid[r]
            out[r, :own, B:] = grad[r]
            out[r, own:] = edge_ref[row]


def taps_matrix(weight_ref, pad_ref):
    pad_ref[...] = jnp.zeros_like(pad_ref)
    pad_ref[: weight_ref.shape[0]] = weight_ref[...]
    return pad_ref[...]


def right_corr_kernel(
    taps,
    radius,
    scale,
    left_ref,
    own_ref,
    disp_ref,
    edge_ref,
    weight_ref,
    mot_ref,
    pre_ref,
    pad_ref,
    mw_ref,
    side_ref,
):
    rows, _, chan = own_ref.shape
    first = pl.program_id(0) * rows
    pad_ref[...] = jnp.zeros_like(pad_ref)
    side_ref[...] = jnp.zeros_like(side_ref)
    weight = taps_matrix(weight_ref, mw_ref)
    for r in range(rows):
        side_ref[r, :HALO] = edge_ref[r].astype(F32)
        edge = side_ref[r]
        pad_ref[r, :EDGE] = edge[:, chan : 2 * chan].astype(BF16)
        side = edge[:, :chan].astype(BF16)
        scores = dot_nt(jnp.concatenate([left_ref[r], side], axis=0), own_ref[r])
        disp = down_lanes(level_row(disp_ref, first + r, B))
        main = pick_taps(scores[:B, :B], scores[:B, B:], disp, taps, radius, scale)
        disp = edge[:, 2 * chan + 2 * B :].astype(jnp.int32)
        beside = pick_taps(
            scores[B:, B:], dot_nt(side, pad_ref[r]), disp, taps, radius, scale
        )
        pre = dot(jnp.concatenate([main, beside], axis=0), weight)
        pre_ref[r] = pre[:B]
        mot_ref[r] = silu(pre).astype(BF16)


def left_corr_kernel(
    taps,
    radius,
    scale,
    start,
    rim_step,
    left_ref,
    own_ref,
    before_ref,
    disp_ref,
    mot_right_ref,
    weight_ref,
    mot_ref,
    pre_ref,
    hg_ref,
    rim_ref,
    pad_ref,
    mw_ref,
):
    rows, _, chan = own_ref.shape
    step = pl.program_id(0)
    first = start + step * rows
    pad_ref[...] = jnp.zeros_like(pad_ref)
    weight = taps_matrix(weight_ref, mw_ref)
    last = iota((EDGE, chan), 0) >= EDGE - HALO
    upper = iota((EDGE, B), 0) < EDGE // 2
    wide = mot_ref.shape[1]
    for r in range(rows):
        extra = before_ref[r, B:].astype(F32)
        pad_ref[r, B - EDGE :] = jnp.where(last, pltpu.roll(extra, 12, 0), 0.0).astype(BF16)
        side = jnp.where(last, pltpu.roll(extra, 8, 0), 0.0).astype(BF16)
        window = jnp.concatenate([before_ref[r, :B], own_ref[r]], axis=0)
        scores = dot_nt(jnp.concatenate([left_ref[r], side], axis=0), window)
        disp = down_lanes(level_row(disp_ref, first + r, 0))
        main = pick_taps(scores[:B, :B], scores[:B, B:], disp, taps, radius, scale)
        disp = pltpu.roll(extra, 4, 0)[:, :B].astype(jnp.int32)
        beside = pick_taps(
            dot_nt(side, pad_ref[r]), scores[B:, :B], disp, taps, radius, scale, B - EDGE
        )
        pre = dot(jnp.concatenate([main, beside], axis=0), weight)
        pre_ref[r] = pre[:B]
        mot = silu(pre)
        mot_ref[r, :B] = mot[:B].astype(BF16)
        mot_ref[r, B : 2 * B] = mot_right_ref[r, :B]
        right_edge = mot_right_ref[r, B:].astype(F32)
        mot_ref[r, 2 * B :] = jnp.where(upper, right_edge, mot[B:]).astype(BF16)
        hg_ref[r] = jnp.where(last, extra, 0.0).astype(BF16)

    @pl.when(step == rim_step)
    def _():
        for r in range(rows):
            rim_ref[r, :wide] = mot_ref[r]
            hg = hg_ref[r].astype(F32)
            rim_ref[r, wide:] = (hg[:, :B] + pltpu.roll(hg[:, B:], EDGE // 2, 0)).astype(BF16)


def shifted(value):
    return (
        pltpu.roll(value, 1, 0).astype(BF16),
        value.astype(BF16),
        pltpu.roll(value, value.shape[0] - 1, 0).astype(BF16),
    )


def store3(buf, row, value):
    for b, part in enumerate(shifted(value)):
        buf[row, :, b * B : (b + 1) * B] = part


def lanes(buf, rows, b):
    return jnp.concatenate([buf[r, :, b * B : (b + 1) * B] for r in rows], axis=0)


def patches(bufs, row_sets):
    return jnp.concatenate(
        [lanes(buf, rows, b) for rows in row_sets for b in range(3) for buf in bufs], axis=1
    )


def chunks(values, size):
    values = list(values)
    return [values[i : i + size] for i in range(0, len(values), size)]


CHUNK = 4


def gru_kernel(
    hid_hbm,
    grad_hbm,
    hgt_hbm,
    hgb_hbm,
    mota_hbm,
    motb_hbm,
    gate_hbm,
    cand_hbm,
    prela_hbm,
    prelb_hbm,
    prer_hbm,
    right_ref,
    lefta_ref,
    leftb_ref,
    mott_ref,
    motl_ref,
    disp_ref,
    mw_ref,
    nh_hbm,
    pg_hbm,
    tg_ref,
    h3_ref,
    m3_ref,
    r3_ref,
    c3_ref,
    h_ref,
    g_ref,
    up_ref,
    rs_ref,
    cb_ref,
    hid_ref,
    grad_ref,
    hgt_ref,
    hgb_ref,
    mota_ref,
    motb_ref,
    wg_ref,
    cw_ref,
    prel_ref,
    prer_ref,
    wc_ref,
    wcb_ref,
    wgb_ref,
    nh_ref,
    pg_ref,
    sems,
):
    rows, own, _ = hid_ref.shape
    half = rows // 2
    wide = own + EDGE
    total = rows + 2 * HALO
    inner = range(HALO, HALO + rows)
    moves = (
        (hid_hbm, hid_ref),
        (hgt_hbm, hgt_ref),
        (hgb_hbm, hgb_ref),
        (mota_hbm, mota_ref),
        (motb_hbm, motb_ref),
        (grad_hbm, grad_ref),
        (gate_hbm, wg_ref),
        (cand_hbm, cw_ref),
        (prela_hbm, prel_ref.at[:half]),
        (prelb_hbm, prel_ref.at[half:]),
        (prer_hbm, prer_ref),
    )
    copies = [pltpu.make_async_copy(s, d, sems.at[n]) for n, (s, d) in enumerate(moves)]
    for copy in copies:
        copy.start()
    wc_ref[9 * B * 2 :, :B] = jnp.zeros((6 * B, B), BF16)
    wc_ref[: 6 * B, B:] = jnp.zeros((6 * B, B), BF16)
    wgb_ref[:B, 18 * B :] = jnp.zeros((B, 6 * B), BF16)
    wgb_ref[B:, : 6 * B] = jnp.zeros((B, 6 * B), BF16)
    for copy in copies[:6]:
        copy.wait()

    upper = iota((EDGE, B), 0) < EDGE // 2
    last = iota((EDGE, B), 0) >= EDGE - HALO

    def join(first, second):
        return jnp.where(upper, first.astype(F32), second.astype(F32)).astype(BF16)

    for row in range(total):
        if row in inner:
            n = row - HALO
            left = lefta_ref[n] if n < half else leftb_ref[n - half]
            h_ref[row, :own] = hid_ref[n]
            h_ref[row, own:] = join(right_ref[n, :, :B], left[:, :B])
            g_ref[row, :own] = grad_ref[n]
            g_ref[row, own:] = join(right_ref[n, :, B:], left[:, B:])
            mot = mota_ref[n] if n < half else motb_ref[n - half]
        else:
            top = row < HALO
            n = row if top else row - HALO - rows
            hg = hgt_ref[n] if top else hgb_ref[n]
            mot = mott_ref[n] if top else motl_ref[n]
            left = mot[wide:].astype(F32)
            mot = mot[:wide]
            h_ref[row, :own] = hg[:own, :B]
            h_ref[row, own:] = join(hg[own:, :B], jnp.where(last, left, 0.0))
            g_ref[row, :own] = hg[:own, B:]
            left = jnp.where(last, pltpu.roll(left, EDGE // 2, 0), 0.0)
            g_ref[row, own:] = join(hg[own:, B:], left)
        store3(h3_ref, row, h_ref[row].astype(F32))
        store3(m3_ref, row, mot.astype(F32))

    copies[6].wait()
    for group in chunks(range(1, total - 1), CHUNK):
        lhs = patches((h3_ref, m3_ref), [[r + a - 1 for r in group] for a in range(3)])
        acc = jax.nn.sigmoid(dot(lhs, wg_ref[...]))
        for n, row in enumerate(group):
            gate = acc[n * wide : (n + 1) * wide]
            up_ref[row] = gate[:, :B]
            reset = gate[:, B:]
            rs_ref[row] = reset
            store3(r3_ref, row, reset * h_ref[row].astype(F32))

    copies[7].wait()
    wc_ref[: 18 * B, :B] = cw_ref[...]
    wc_ref[6 * B :, B:] = cw_ref[...]
    for n in range(9):
        at = (8 - n) * 2 * B
        wcb_ref[:, n * B : (n + 1) * B] = cw_ref[at : at + 2 * B]
        for s in range(2):
            col = (n + 3 * s) * 2 * B
            wgb_ref[s * B : (s + 1) * B, col : col + 2 * B] = wg_ref[at + B : at + 2 * B]

    for group in chunks(range(2, total - 2, 2), CHUNK):
        lhs = patches((r3_ref, m3_ref), [[r + t - 1 for r in group] for t in range(4)])
        acc = jnp.tanh(dot(lhs, wc_ref[...]))
        for n, first in enumerate(group):
            for row in (first, first + 1):
                s = row - first
                cand = acc[n * wide : (n + 1) * wide, s * B : (s + 1) * B]
                hidden = h_ref[row].astype(F32)
                update = up_ref[row]
                if row in inner:
                    new = (1.0 - update) * hidden + update * cand
                    nh_ref[row - HALO] = new[:own].astype(BF16)
                gu = g_ref[row].astype(F32) * update
                store3(c3_ref, row, gu * (1.0 - cand * cand))
                store3(h3_ref, row, gu * (cand - hidden) * (1.0 - update))
    new_copy = pltpu.make_async_copy(nh_ref, nh_hbm, sems.at[len(moves)])
    new_copy.start()

    for group in chunks(range(3, total - 3), CHUNK):
        lhs = patches((c3_ref,), [[r + a - 1 for r in group] for a in range(3)])
        acc = dot_nt(lhs, wcb_ref[...])
        for n, row in enumerate(group):
            back = acc[n * wide : (n + 1) * wide]
            reset = rs_ref[row]
            store3(m3_ref, row, back[:, :B] * h_ref[row].astype(F32) * reset * (1.0 - reset))
            if row in inner:
                cb_ref[row - HALO] = back[:own, B:]

    for copy in copies[8:]:
        copy.wait()
    pieces = []
    for group in chunks(range(HALO, HALO + rows, 2), CHUNK):
        lhs = patches((h3_ref, m3_ref), [[r + t - 1 for r in group] for t in range(4)])
        acc = dot_nt(lhs, wgb_ref[...])
        for n, first in enumerate(group):
            for row in (first - HALO, first + 1 - HALO):
                s = row + HALO - first
                back = acc[n * wide : n * wide + own, s * B : (s + 1) * B]
                pre = jnp.concatenate([prel_ref[row], prer_ref[row]], axis=0)
                sig = jax.nn.sigmoid(pre)
                grad = (cb_ref[row] + back) * sig * (1.0 + pre * (1.0 - sig))
                grad = grad.astype(BF16)
                pg_ref[row] = grad
                tap = dot_nt(mw_ref[...], grad[:B])
                level = jnp.broadcast_to(disp_ref[row : row + 1, :B].astype(F32), tap.shape)
                tg_ref[row] = jnp.where(iota(tap.shape, 0) == 15, level, tap).astype(BF16)
        done = pl.ds(group[0] - HALO, 2 * len(group))
        at = len(moves) + 1 + len(pieces)
        piece = pltpu.make_async_copy(pg_ref.at[done], pg_hbm.at[done], sems.at[at])
        piece.start()
        pieces.append(piece)
    new_copy.wait()
    for piece in pieces:
        piece.wait()


def spread(grad, disp, taps, radius):
    pixel = iota((B, B), 0)
    lane = iota((B, B), 1)
    tap = ((pixel - lane) & (B - 1)) - disp + radius
    ok = (tap >= 0) & (tap < taps)
    value = jnp.where(ok, lane_gather(grad, tap & (B - 1)), 0.0)
    far = jnp.where(lane > pixel, value, 0.0).astype(BF16)
    near = jnp.where(lane > pixel, 0.0, value).astype(BF16)
    return far, near


def spread_t(grad, disp, taps, radius):
    column = iota((B, B), 0)
    pixel = iota((B, B), 1)
    tap = ((pixel - column) & (B - 1)) - disp + radius
    value = jnp.zeros((B, B), F32)
    for k in range(taps):
        value = jnp.where(tap == k, grad[k : k + 1], value)
    far = jnp.where(column > pixel, value, 0.0).astype(BF16)
    near = jnp.where(column > pixel, 0.0, value).astype(BF16)
    return far, near


def grads_kernel(
    taps,
    radius,
    scale,
    pg_ref,
    left_ref,
    own_ref,
    before_a_ref,
    before_b_ref,
    disp_ref,
    weight_ref,
    gl_ref,
    gr_ref,
    near_ref,
    mw_ref,
):
    rows = left_ref.shape[0]
    step = pl.program_id(0)
    head = step < pl.num_programs(0) // 2
    weight_t = weight_ref[...]
    weight = taps_matrix(weight_ref, mw_ref)
    for r in range(rows):
        grads = dot_nt(pg_ref[r], weight).astype(BF16).astype(F32)
        grads_t = dot_nt(weight_t, pg_ref[r]).astype(BF16).astype(F32)
        parts = []
        parts_t = []
        for block in range(2):
            at = slice(block * B, (block + 1) * B)
            row = level_row(disp_ref, step * rows + r, block * B)
            parts.append(spread(grads[at], down_lanes(row), taps, radius))
            parts_t.append(spread_t(grads_t[:, at], row, taps, radius))
        before = jnp.where(head, before_a_ref[r, :B], before_b_ref[r, :B])
        window = jnp.concatenate([before, own_ref[r, :B]], axis=0)
        gl_ref[r, :B] = (dot(jnp.concatenate(parts[0], axis=1), window) * scale).astype(BF16)
        gl_ref[r, B:] = (dot(jnp.concatenate(parts[1], axis=1), own_ref[r]) * scale).astype(BF16)
        sg = jnp.concatenate([parts_t[0][1], parts_t[1][0]], axis=1)
        gr_ref[r] = (dot(sg, left_ref[r]) * scale).astype(BF16)
        near_ref[r] = parts_t[1][1]


def last_kernel(taps, radius, scale, near_ref, grad_ref, left_ref, next_ref, first_ref, gr_ref):
    del first_ref
    rows = left_ref.shape[0]
    for r in range(rows):
        grad = grad_ref[r].astype(F32)
        disp = grad[15:16].astype(jnp.int32)
        far, _ = spread_t(grad, disp, taps, radius)
        sg = jnp.concatenate([near_ref[r], far], axis=1)
        window = jnp.concatenate([left_ref[r], next_ref[r]], axis=0)
        gr_ref[r] = (dot(sg, window) * scale).astype(BF16)


def whole(array):
    nd = array.ndim
    return pl.BlockSpec(array.shape, lambda i: (0,) * nd)


def by_rows(array, size, block=None, at=None):
    block = tuple(array.shape[1:]) if block is None else block
    at = (0,) * len(block) if at is None else at
    return pl.BlockSpec((size,) + block, lambda i: (i,) + at)


def cost(flops, bytes_accessed):
    return pl.CostEstimate(flops=flops, bytes_accessed=bytes_accessed, transcendentals=0)


def block(shape, *at):
    return pl.BlockSpec(shape, lambda i: (i + at[0],) + at[1:])


def per_device(
    feat_left, feat_right, hidden, disparity, motion_weight, gate_weight, cand_weight, grad_hidden
):
    rows, cols, chan = feat_left.shape
    taps = motion_weight.shape[0]
    radius = taps // 2
    scale = 1.0 / math.sqrt(chan)
    args = (taps, radius, scale)
    size = ROWS
    steps = rows // size
    half = rows // 2
    wide = cols + EDGE
    packed = 2 * chan + 3 * B
    params = pltpu.CompilerParams(vmem_limit_bytes=SMALL_VMEM)
    shape = jax.ShapeDtypeStruct
    vmem = pl.BlockSpec(memory_space=pltpu.VMEM)
    last8 = cols // 8 - 1

    from_right = shift(
        pl.pallas_call(
            pack_left_kernel,
            grid=(1,),
            in_specs=[
                block((rows, 8, chan), 0, 0, 0),
                block((rows, 8, chan), 0, 0, 0),
                block((rows, 8, B), 0, 0, 0),
                block((rows, 8, B), 0, 0, 0),
                whole(disparity),
            ],
            out_specs=whole(shape((rows, HALO, packed), BF16)),
            out_shape=shape((rows, HALO, packed), BF16),
            compiler_params=params,
            cost_estimate=cost(1 << 16, 1 << 18),
            name="pack_left",
        )(feat_left, feat_right, hidden, grad_hidden, disparity),
        "cols",
        -1,
    )

    def features_before(start):
        at = start // size
        out = shape((half, B + EDGE, chan), BF16)
        return shift(
            pl.pallas_call(
                lambda *refs: pack_right_kernel(start, *refs),
                grid=(half // size,),
                in_specs=[
                    block((size, B, chan), at, cols // B - 1, 0),
                    block((size, 8, chan), at, (cols - B) // 8 - 1, 0),
                    block((size, 8, chan), at, last8, 0),
                    block((size, 8, B), at, last8, 0),
                    block((size, 8, B), at, last8, 0),
                    whole(disparity),
                ],
                out_specs=by_rows(out, size),
                out_shape=out,
                compiler_params=params,
                cost_estimate=cost(1 << 16, 2 << 20),
                name="pack_right",
            )(feat_right, feat_right, feat_left, hidden, grad_hidden, disparity),
            "cols",
            1,
        )

    before = [features_before(0), features_before(half)]

    rim = shape((HALO, wide, 2 * B), BF16)
    edge_shape = shape((rows, EDGE, 2 * B), BF16)
    first_rim, last_rim, edge = pl.pallas_call(
        rim_kernel,
        grid=(1,),
        in_specs=[
            block((HALO, cols, B), 0, 0, 0),
            block((HALO, cols, B), 0, 0, 0),
            block((HALO, cols, B), rows // HALO - 1, 0, 0),
            block((HALO, cols, B), rows // HALO - 1, 0, 0),
            whole(from_right),
        ],
        out_specs=[whole(rim), whole(rim), whole(edge_shape)],
        out_shape=(rim, rim, edge_shape),
        scratch_shapes=[pltpu.VMEM((EDGE, 2 * B), F32)],
        compiler_params=params,
        cost_estimate=cost(1 << 16, 2 << 20),
        name="rims",
    )(hidden, grad_hidden, hidden, grad_hidden, from_right)
    hg_top = shift(last_rim, "rows", 1)
    hg_low = shift(first_rim, "rows", -1)

    mw16 = jnp.pad(motion_weight, ((0, 16 - taps), (0, 0)))
    pads = [pltpu.VMEM((size, B, chan), BF16), pltpu.VMEM((B, B), BF16)]
    right_shapes = (shape((rows, B + EDGE, B), BF16), shape((rows, B, B), F32))
    mot_right, pre_right = pl.pallas_call(
        lambda *refs: right_corr_kernel(*args, *refs),
        grid=(steps,),
        in_specs=[
            block((size, B, chan), 0, 1, 0),
            by_rows(feat_right, size),
            whole(disparity),
            by_rows(from_right, size),
            whole(mw16),
        ],
        out_specs=[by_rows(s, size) for s in right_shapes],
        out_shape=right_shapes,
        scratch_shapes=pads + [pltpu.VMEM((size, EDGE, packed), F32)],
        compiler_params=params,
        cost_estimate=cost(2 * rows * B * 2 * B * chan, 6 << 20),
        name="corr_right",
    )(feat_left, feat_right, disparity, from_right, mw16)

    def left_lookup(start, before, rim_step):
        at = start // size
        shapes = (
            shape((half, wide, B), BF16),
            shape((half, B, B), F32),
            shape((half, EDGE, 2 * B), BF16),
            shape((HALO, wide + EDGE, B), BF16),
        )
        return pl.pallas_call(
            lambda *refs: left_corr_kernel(*args, start, rim_step, *refs),
            grid=(half // size,),
            in_specs=[
                block((size, B, chan), at, 0, 0),
                block((size, B, chan), at, 0, 0),
                by_rows(before, size),
                whole(disparity),
                block((size, B + EDGE, B), at, 0, 0),
                whole(mw16),
            ],
            out_specs=[by_rows(s, size) for s in shapes[:3]] + [whole(shapes[3])],
            out_shape=shapes,
            scratch_shapes=pads,
            compiler_params=params,
            cost_estimate=cost(rows * B * 2 * B * chan, 3 << 20),
            name="corr_left",
        )(feat_left, feat_right, before, disparity, mot_right, mw16)

    mot_a, pre_a, left_a, rim_a = left_lookup(0, before[0], 0)
    mot_low = shift(rim_a, "rows", -1)
    mot_b, pre_b, left_b, rim_b = left_lookup(half, before[1], half // size - 1)
    mot_top = shift(rim_b, "rows", 1)
    first_left, _ = lax.optimization_barrier((feat_left[:, :B], mot_b))
    next_left = shift(first_left, "cols", -1)

    total = rows + 2 * HALO
    own_shape = shape((rows, cols, B), BF16)
    big = (
        hidden,
        grad_hidden,
        hg_top,
        hg_low,
        mot_a,
        mot_b,
        gate_weight.reshape(-1, 2 * B),
        cand_weight.reshape(-1, B),
        pre_a,
        pre_b,
        pre_right,
    )
    small = (edge, left_a, left_b, mot_top, mot_low, disparity, mw16)
    anywhere = pl.BlockSpec(memory_space=pl.ANY)
    new_hidden, pre_grad, tap_grad = pl.pallas_call(
        gru_kernel,
        in_specs=[anywhere] * len(big) + [vmem] * len(small),
        out_specs=[anywhere, anywhere, vmem],
        out_shape=(own_shape, own_shape, shape((rows, 16, B), BF16)),
        scratch_shapes=[pltpu.VMEM((total, wide, 3 * B), BF16)] * 4
        + [pltpu.VMEM((total, wide, B), BF16)] * 2
        + [pltpu.VMEM((total, wide, B), F32)] * 2
        + [pltpu.VMEM((rows, cols, B), F32)]
        + [pltpu.VMEM(a.shape, BF16) for a in big[:8]]
        + [pltpu.VMEM((rows, B, B), F32)] * 2
        + [
            pltpu.VMEM((24 * B, 2 * B), BF16),
            pltpu.VMEM((2 * B, 9 * B), BF16),
            pltpu.VMEM((2 * B, 24 * B), BF16),
            pltpu.VMEM((rows, cols, B), BF16),
            pltpu.VMEM((rows, cols, B), BF16),
            pltpu.SemaphoreType.DMA((len(big) + 1 + rows,)),
        ],
        compiler_params=pltpu.CompilerParams(vmem_limit_bytes=GRU_VMEM),
        cost_estimate=cost(2 * 22 * wide * 256 * 256 * 24, 16 << 20),
        name="gru",
    )(*big, *small)
    next_grad = shift(tap_grad, "cols", -1)

    feat_shape = shape((rows, cols, chan), BF16)
    near_shape = shape((rows, B, B), BF16)
    mid = steps // 2
    grad_left, grad_first, near = pl.pallas_call(
        lambda *refs: grads_kernel(*args, *refs),
        grid=(steps,),
        in_specs=[
            by_rows(pre_grad, size),
            by_rows(feat_left, size),
            by_rows(feat_right, size),
            pl.BlockSpec((size, B + EDGE, chan), lambda i: (jnp.minimum(i, mid - 1), 0, 0)),
            pl.BlockSpec((size, B + EDGE, chan), lambda i: (jnp.maximum(i - mid, 0), 0, 0)),
            whole(disparity),
            whole(mw16),
        ],
        out_specs=[
            by_rows(feat_shape, size),
            block((size, B, chan), 0, 0, 0),
            by_rows(near_shape, size),
        ],
        out_shape=(feat_shape, feat_shape, near_shape),
        scratch_shapes=[pltpu.VMEM((B, B), BF16)],
        compiler_params=params,
        cost_estimate=cost(2 * rows * B * 2 * B * chan * 4, 12 << 20),
        name="grads",
    )(pre_grad, feat_left, feat_right, before[0], before[1], disparity, mw16)
    grad_right = pl.pallas_call(
        lambda *refs: last_kernel(*args, *refs),
        grid=(steps,),
        in_specs=[
            by_rows(near, size),
            by_rows(next_grad, size),
            block((size, B, chan), 0, 1, 0),
            by_rows(next_left, size),
            anywhere,
        ],
        out_specs=block((size, B, chan), 0, 1, 0),
        out_shape=feat_shape,
        input_output_aliases={4: 0},
        compiler_params=params,
        cost_estimate=cost(2 * rows * B * 2 * B * chan, 4 << 20),
        name="grad_right",
    )(near, next_grad, feat_left, next_left, grad_first)
    return (new_hidden, grad_left, grad_right)


def solution(mesh):
    grid3 = P("rows", "cols", None)
    return jax.shard_map(
        per_device,
        mesh=mesh,
        in_specs=(grid3, grid3, grid3, P("rows", "cols"), P(), P(), P(), grid3),
        out_specs=(grid3, grid3, grid3),
        check_vma=False,
    )
```

```python
import math

import jax
import jax.numpy as jnp
from jax import lax
from jax.experimental import pallas as pl
from jax.experimental.pallas import tpu as pltpu
from jax.sharding import PartitionSpec as P

B = 128
HALO = 4
EDGE = 16
F32 = jnp.float32
BF16 = jnp.bfloat16
ROWS = 4
SMALL_VMEM = 16 * 1024 * 1024
GRU_VMEM = 32 * 1024 * 1024
GATES_VMEM = 12 * 1024 * 1024
PACK_VMEM = 60 * 1024 * 1024


def shift(array, axis, by):
    size = lax.axis_size(axis)
    pairs = [(i, i + by) for i in range(size) if 0 <= i + by < size]
    return lax.ppermute(array, axis, pairs)


def dot_nt(a, b):
    return lax.dot_general(a, b, (((1,), (1,)), ((), ())), preferred_element_type=F32)


def dot(a, b):
    return jnp.dot(a, b, preferred_element_type=F32)


def iota(shape, dim):
    return lax.broadcasted_iota(jnp.int32, shape, dim)


def lane_gather(values, index):
    return jnp.take_along_axis(values, index, axis=1, mode="promise_in_bounds")


def down_lanes(row):
    return jnp.transpose(jnp.broadcast_to(row, (B, B)), (1, 0))


def pick_taps(far, near, disp, taps, radius, scale, first=0):
    count = far.shape[0]
    pixel = iota((count, B), 0) + first
    lane = iota((count, B), 1)
    merged = jnp.where(lane > pixel, far, near)
    level = disp + lane - radius
    usable = (level >= 0) & (level < B) & (lane < taps)
    picked = lane_gather(merged, (pixel - level) & (B - 1))
    return (jnp.where(usable, picked, 0.0) * scale).astype(BF16)


def silu(v):
    return v * jax.nn.sigmoid(v)


def level_columns(disp_ref, at):
    return jnp.transpose(disp_ref[:, at : at + B].astype(F32), (1, 0))


def level_row(disp_ref, row, at):
    levels = disp_ref[:, at : at + B]
    return jnp.sum(jnp.where(iota(levels.shape, 0) == row, levels, 0), axis=0, keepdims=True)


def pack_small_kernel(
    left_ref, own_ref, hid_ref, grad_ref, hid_last_ref, grad_last_ref, disp_ref, out_ref, last_ref
):
    rows, _, chan = left_ref.shape
    levels = jnp.transpose(disp_ref[:, :B].astype(F32), (1, 0))
    for r in range(rows):
        out_ref[r, :, :chan] = left_ref[r, :HALO]
        out_ref[r, :, chan : 2 * chan] = own_ref[r, :HALO]
        out_ref[r, :, 2 * chan : 2 * chan + B] = hid_ref[r, :HALO]
        out_ref[r, :, 2 * chan + B : 2 * chan + 2 * B] = grad_ref[r, :HALO]
        level = jnp.broadcast_to(levels[:8, r : r + 1], (8, B))
        out_ref[r, :, 2 * chan + 2 * B :] = level.astype(BF16)[:HALO]
        hg = jnp.concatenate([hid_last_ref[r], grad_last_ref[r]], axis=1).astype(F32)
        last_ref[r] = pltpu.roll(hg, HALO, 0)[:HALO].astype(BF16)


def pack_right_kernel(start, own_ref, beside_ref, left_ref, disp_ref, out_ref):
    rows, _, chan = own_ref.shape
    first = start + pl.program_id(0) * rows
    low = iota((8, chan), 0) < HALO
    for r in range(rows):
        out_ref[r, :B] = own_ref[r]
        beside = pltpu.roll(beside_ref[r].astype(F32), HALO, 0)
        upper = jnp.where(low, beside, left_ref[r].astype(F32))
        row = level_row(disp_ref, first + r, disp_ref.shape[1] - B).astype(F32)
        level = jnp.transpose(jnp.broadcast_to(row, (8, B)), (1, 0))[B - 8 :, :1]
        level = pltpu.roll(jnp.broadcast_to(level, (8, chan)), HALO, 0)
        out_ref[r, B:] = jnp.concatenate([upper, jnp.where(low, level, 0.0)], axis=0).astype(BF16)


def rim_kernel(
    hid_first_ref,
    grad_first_ref,
    hid_last_ref,
    grad_last_ref,
    right_ref,
    left_ref,
    first_ref,
    last_ref,
    edge_ref,
    pad_ref,
):
    rows = right_ref.shape[0]
    own = hid_first_ref.shape[1]
    chan = (right_ref.shape[2] - 3 * B) // 2
    pad_ref[...] = jnp.zeros_like(pad_ref)
    for r in range(rows):
        pad_ref[:HALO] = right_ref[r, :, 2 * chan : 2 * chan + 2 * B].astype(F32)
        pad_ref[8 : 8 + HALO] = left_ref[r].astype(F32)
        value = pad_ref[...]
        low = pltpu.roll(value[8:], HALO, 0)
        edge_ref[r] = jnp.concatenate([value[:8], low], axis=0).astype(BF16)
    for r in range(HALO):
        for out, hid, grad, row in (
            (first_ref, hid_first_ref, grad_first_ref, r),
            (last_ref, hid_last_ref, grad_last_ref, rows - HALO + r),
        ):
            out[r, :own, :B] = hid[r]
            out[r, :own, B:] = grad[r]
            out[r, own:] = edge_ref[row]


def taps_matrix(weight_ref, pad_ref):
    pad_ref[...] = jnp.zeros_like(pad_ref)
    pad_ref[: weight_ref.shape[0]] = weight_ref[...]
    return pad_ref[...]


def right_corr_kernel(
    taps,
    radius,
    scale,
    left_ref,
    own_ref,
    disp_ref,
    edge_ref,
    weight_ref,
    mot_ref,
    pre_ref,
    pad_ref,
    mw_ref,
    side_ref,
):
    rows, _, chan = own_ref.shape
    first = pl.program_id(0) * rows
    pad_ref[...] = jnp.zeros_like(pad_ref)
    side_ref[...] = jnp.zeros_like(side_ref)
    weight = taps_matrix(weight_ref, mw_ref)
    for r in range(rows):
        side_ref[r, :HALO] = edge_ref[r].astype(F32)
        edge = side_ref[r]
        pad_ref[r, :EDGE] = edge[:, chan : 2 * chan].astype(BF16)
        side = edge[:, :chan].astype(BF16)
        scores = dot_nt(jnp.concatenate([left_ref[r], side], axis=0), own_ref[r])
        disp = down_lanes(level_row(disp_ref, first + r, B))
        main = pick_taps(scores[:B, :B], scores[:B, B:], disp, taps, radius, scale)
        disp = edge[:, 2 * chan + 2 * B :].astype(jnp.int32)
        beside = pick_taps(
            scores[B:, B:], dot_nt(side, pad_ref[r]), disp, taps, radius, scale
        )
        pre = dot(jnp.concatenate([main, beside], axis=0), weight)
        pre_ref[r] = pre[:B]
        mot_ref[r] = silu(pre).astype(BF16)


def left_corr_kernel(
    taps,
    radius,
    scale,
    start,
    rim_step,
    left_ref,
    own_ref,
    before_ref,
    disp_ref,
    mot_right_ref,
    weight_ref,
    mot_ref,
    pre_ref,
    rim_ref,
    pad_ref,
    mw_ref,
):
    rows, _, chan = own_ref.shape
    step = pl.program_id(0)
    first = start + step * rows
    pad_ref[...] = jnp.zeros_like(pad_ref)
    weight = taps_matrix(weight_ref, mw_ref)
    last = iota((EDGE, chan), 0) >= EDGE - HALO
    upper = iota((EDGE, B), 0) < EDGE // 2
    for r in range(rows):
        extra = before_ref[r, B:].astype(F32)
        pad_ref[r, B - EDGE :] = jnp.where(last, pltpu.roll(extra, 12, 0), 0.0).astype(BF16)
        side = jnp.where(last, pltpu.roll(extra, 8, 0), 0.0).astype(BF16)
        window = jnp.concatenate([before_ref[r, :B], own_ref[r]], axis=0)
        scores = dot_nt(jnp.concatenate([left_ref[r], side], axis=0), window)
        disp = down_lanes(level_row(disp_ref, first + r, 0))
        main = pick_taps(scores[:B, :B], scores[:B, B:], disp, taps, radius, scale)
        disp = pltpu.roll(extra, 4, 0)[:, :B].astype(jnp.int32)
        beside = pick_taps(
            dot_nt(side, pad_ref[r]), scores[B:, :B], disp, taps, radius, scale, B - EDGE
        )
        pre = dot(jnp.concatenate([main, beside], axis=0), weight)
        pre_ref[r] = pre[:B]
        mot = silu(pre)
        mot_ref[r, :B] = mot[:B].astype(BF16)
        mot_ref[r, B : 2 * B] = mot_right_ref[r, :B]
        right_edge = mot_right_ref[r, B:].astype(F32)
        mot_ref[r, 2 * B :] = jnp.where(upper, right_edge, mot[B:]).astype(BF16)

    @pl.when(step == rim_step)
    def _():
        rim_ref[...] = mot_ref[...]


def shifted(value):
    return (
        pltpu.roll(value, 1, 0).astype(BF16),
        value.astype(BF16),
        pltpu.roll(value, value.shape[0] - 1, 0).astype(BF16),
    )


def store3(buf, row, value):
    for b, part in enumerate(shifted(value)):
        buf[row, :, b * B : (b + 1) * B] = part


def lanes(buf, rows, b):
    return jnp.concatenate([buf[r, :, b * B : (b + 1) * B] for r in rows], axis=0)


def patches(bufs, row_sets):
    return jnp.concatenate(
        [lanes(buf, rows, b) for rows in row_sets for b in range(3) for buf in bufs], axis=1
    )


def chunks(values, size):
    values = list(values)
    return [values[i : i + size] for i in range(0, len(values), size)]


CHUNK = 4


def gates_hidden_kernel(
    hid_ref,
    grad_ref,
    hgt_ref,
    hgb_ref,
    edge_ref,
    gate_ref,
    cand_ref,
    h_ref,
    g_ref,
    gh_ref,
    wgm_ref,
    wc_ref,
    wcb_ref,
    wgb_ref,
    h3_ref,
    wgh_ref,
):
    rows, own, _ = hid_ref.shape
    wide = own + EDGE
    total = rows + 2 * HALO
    for row in range(total):
        n = row - HALO
        if 0 <= n < rows:
            h_ref[row, :own] = hid_ref[n]
            h_ref[row, own:] = edge_ref[n, :, :B]
            g_ref[row, :own] = grad_ref[n]
            g_ref[row, own:] = edge_ref[n, :, B:]
        else:
            hg = hgt_ref[row] if n < 0 else hgb_ref[n - rows]
            h_ref[row] = hg[:, :B]
            g_ref[row] = hg[:, B:]
        store3(h3_ref, row, h_ref[row].astype(F32))
    zeros = jnp.zeros((6 * B, B), BF16)
    wc_ref[18 * B :, :B] = zeros
    wc_ref[: 6 * B, B:] = zeros
    wc_ref[: 18 * B, :B] = cand_ref[...]
    wc_ref[6 * B :, B:] = cand_ref[...]
    wgb_ref[:B, 18 * B :] = jnp.zeros((B, 6 * B), BF16)
    wgb_ref[B:, : 6 * B] = jnp.zeros((B, 6 * B), BF16)
    for n in range(9):
        wgh_ref[n * B : (n + 1) * B] = gate_ref[2 * n * B : (2 * n + 1) * B]
        wgm_ref[n * B : (n + 1) * B] = gate_ref[(2 * n + 1) * B : (2 * n + 2) * B]
        at = (8 - n) * 2 * B
        wcb_ref[:, n * B : (n + 1) * B] = cand_ref[at : at + 2 * B]
        for s in range(2):
            col = (n + 3 * s) * 2 * B
            wgb_ref[s * B : (s + 1) * B, col : col + 2 * B] = gate_ref[at + B : at + 2 * B]
    for group in chunks(range(1, total - 1), CHUNK):
        lhs = patches((h3_ref,), [[r + a - 1 for r in group] for a in range(3)])
        acc = dot(lhs, wgh_ref[...])
        for n, row in enumerate(group):
            gh_ref[row - 1] = acc[n * wide : (n + 1) * wide]


def gru_kernel(
    mota_ref,
    motb_ref,
    wgm_ref,
    h_ref,
    gates_ref,
    g_ref,
    wc_ref,
    wcb_ref,
    wgb_ref,
    prela_ref,
    prelb_ref,
    prer_ref,
    mott_ref,
    motl_ref,
    disp_ref,
    mw_ref,
    nh_ref,
    pg_ref,
    tg_ref,
    gh_ref,
    u3_ref,
    m3_ref,
    r3_ref,
    c3_ref,
    cb_ref,
):
    rows, own, _ = nh_ref.shape
    half = rows // 2
    wide = own + EDGE
    total = rows + 2 * HALO
    inner = range(HALO, HALO + rows)
    gate_groups = chunks(range(1, total - 1), CHUNK)
    for row in range(total):
        n = row - HALO
        if n < 0:
            mot = mott_ref[row]
        elif n >= rows:
            mot = motl_ref[n - rows]
        else:
            mot = mota_ref[n] if n < half else motb_ref[n - half]
        store3(m3_ref, row, mot.astype(F32))

    for group in gate_groups:
        lhs = patches((m3_ref,), [[r + a - 1 for r in group] for a in range(3)])
        acc = dot(lhs, wgm_ref[...])
        for n, row in enumerate(group):
            gate = jax.nn.sigmoid(acc[n * wide : (n + 1) * wide] + gates_ref[row - 1])
            gh_ref[row - 1] = gate
            store3(r3_ref, row, gate[:, B:] * h_ref[row].astype(F32))

    for group in chunks(range(2, total - 2, 2), CHUNK):
        lhs = patches((r3_ref, m3_ref), [[r + t - 1 for r in group] for t in range(4)])
        acc = jnp.tanh(dot(lhs, wc_ref[...]))
        for n, top in enumerate(group):
            for row in (top, top + 1):
                s = row - top
                cand = acc[n * wide : (n + 1) * wide, s * B : (s + 1) * B]
                hidden = h_ref[row].astype(F32)
                update = gh_ref[row - 1, :, :B]
                if row in inner:
                    new = (1.0 - update) * hidden + update * cand
                    nh_ref[row - HALO] = new[:own].astype(BF16)
                gu = g_ref[row].astype(F32) * update
                store3(c3_ref, row, gu * (1.0 - cand * cand))
                store3(u3_ref, row, gu * (cand - hidden) * (1.0 - update))

    for group in chunks(range(3, total - 3), CHUNK):
        lhs = patches((c3_ref,), [[r + a - 1 for r in group] for a in range(3)])
        acc = dot_nt(lhs, wcb_ref[...])
        for n, row in enumerate(group):
            back = acc[n * wide : (n + 1) * wide]
            reset = gh_ref[row - 1, :, B:]
            store3(m3_ref, row, back[:, :B] * h_ref[row].astype(F32) * reset * (1.0 - reset))
            if row in inner:
                cb_ref[row - HALO] = back[:own, B:]

    for group in chunks(range(HALO, HALO + rows, 2), CHUNK):
        lhs = patches((u3_ref, m3_ref), [[r + t - 1 for r in group] for t in range(4)])
        acc = dot_nt(lhs, wgb_ref[...])
        for n, top in enumerate(group):
            for row in (top - HALO, top + 1 - HALO):
                s = row + HALO - top
                back = acc[n * wide : n * wide + own, s * B : (s + 1) * B]
                prel = prela_ref[row] if row < half else prelb_ref[row - half]
                pre = jnp.concatenate([prel, prer_ref[row]], axis=0)
                sig = jax.nn.sigmoid(pre)
                grad = (cb_ref[row] + back) * sig * (1.0 + pre * (1.0 - sig))
                grad = grad.astype(BF16)
                pg_ref[row] = grad
                tap = dot_nt(mw_ref[...], grad[:B])
                level = jnp.broadcast_to(disp_ref[row : row + 1, :B].astype(F32), tap.shape)
                tg_ref[row] = jnp.where(iota(tap.shape, 0) == 15, level, tap).astype(BF16)


def spread(grad, disp, taps, radius):
    pixel = iota((B, B), 0)
    lane = iota((B, B), 1)
    tap = ((pixel - lane) & (B - 1)) - disp + radius
    ok = (tap >= 0) & (tap < taps)
    value = jnp.where(ok, lane_gather(grad, tap & (B - 1)), 0.0)
    far = jnp.where(lane > pixel, value, 0.0).astype(BF16)
    near = jnp.where(lane > pixel, 0.0, value).astype(BF16)
    return far, near


def spread_t(grad, disp, taps, radius):
    column = iota((B, B), 0)
    pixel = iota((B, B), 1)
    tap = ((pixel - column) & (B - 1)) - disp + radius
    value = jnp.zeros((B, B), F32)
    for k in range(taps):
        value = jnp.where(tap == k, grad[k : k + 1], value)
    far = jnp.where(column > pixel, value, 0.0).astype(BF16)
    near = jnp.where(column > pixel, 0.0, value).astype(BF16)
    return far, near


def grads_kernel(
    taps,
    radius,
    scale,
    pg_ref,
    left_ref,
    own_ref,
    before_a_ref,
    before_b_ref,
    disp_ref,
    weight_ref,
    gl_ref,
    gr_ref,
    near_ref,
    mw_ref,
):
    rows = left_ref.shape[0]
    step = pl.program_id(0)
    head = step < pl.num_programs(0) // 2
    weight_t = weight_ref[...]
    weight = taps_matrix(weight_ref, mw_ref)
    for r in range(rows):
        grads = dot_nt(pg_ref[r], weight).astype(BF16).astype(F32)
        grads_t = dot_nt(weight_t, pg_ref[r]).astype(BF16).astype(F32)
        parts = []
        parts_t = []
        for block in range(2):
            at = slice(block * B, (block + 1) * B)
            row = level_row(disp_ref, step * rows + r, block * B)
            parts.append(spread(grads[at], down_lanes(row), taps, radius))
            parts_t.append(spread_t(grads_t[:, at], row, taps, radius))
        before = jnp.where(head, before_a_ref[r, :B], before_b_ref[r, :B])
        window = jnp.concatenate([before, own_ref[r, :B]], axis=0)
        gl_ref[r, :B] = (dot(jnp.concatenate(parts[0], axis=1), window) * scale).astype(BF16)
        gl_ref[r, B:] = (dot(jnp.concatenate(parts[1], axis=1), own_ref[r]) * scale).astype(BF16)
        sg = jnp.concatenate([parts_t[0][1], parts_t[1][0]], axis=1)
        gr_ref[r] = (dot(sg, left_ref[r]) * scale).astype(BF16)
        near_ref[r] = parts_t[1][1]


def last_kernel(taps, radius, scale, near_ref, grad_ref, left_ref, next_ref, first_ref, gr_ref):
    del first_ref
    rows = left_ref.shape[0]
    for r in range(rows):
        grad = grad_ref[r].astype(F32)
        disp = grad[15:16].astype(jnp.int32)
        far, _ = spread_t(grad, disp, taps, radius)
        sg = jnp.concatenate([near_ref[r], far], axis=1)
        window = jnp.concatenate([left_ref[r], next_ref[r]], axis=0)
        gr_ref[r] = (dot(sg, window) * scale).astype(BF16)


def whole(array):
    nd = array.ndim
    return pl.BlockSpec(array.shape, lambda i: (0,) * nd)


def by_rows(array, size, block=None, at=None):
    block = tuple(array.shape[1:]) if block is None else block
    at = (0,) * len(block) if at is None else at
    return pl.BlockSpec((size,) + block, lambda i: (i,) + at)


def cost(flops, bytes_accessed):
    return pl.CostEstimate(flops=flops, bytes_accessed=bytes_accessed, transcendentals=0)


def block(shape, *at):
    return pl.BlockSpec(shape, lambda i: (i + at[0],) + at[1:])


def per_device(
    feat_left, feat_right, hidden, disparity, motion_weight, gate_weight, cand_weight, grad_hidden
):
    rows, cols, chan = feat_left.shape
    taps = motion_weight.shape[0]
    radius = taps // 2
    scale = 1.0 / math.sqrt(chan)
    args = (taps, radius, scale)
    size = ROWS
    steps = rows // size
    half = rows // 2
    wide = cols + EDGE
    packed = 2 * chan + 3 * B
    params = pltpu.CompilerParams(vmem_limit_bytes=SMALL_VMEM)
    shape = jax.ShapeDtypeStruct
    vmem = pl.BlockSpec(memory_space=pltpu.VMEM)
    last8 = cols // 8 - 1
    pack_params = pltpu.CompilerParams(vmem_limit_bytes=PACK_VMEM)

    small_shapes = (shape((rows, HALO, packed), BF16), shape((rows, HALO, 2 * B), BF16))
    to_left, to_right = pl.pallas_call(
        pack_small_kernel,
        grid=(1,),
        in_specs=[
            block((rows, 8, chan), 0, 0, 0),
            block((rows, 8, chan), 0, 0, 0),
            block((rows, 8, B), 0, 0, 0),
            block((rows, 8, B), 0, 0, 0),
            block((rows, 8, B), 0, last8, 0),
            block((rows, 8, B), 0, last8, 0),
            whole(disparity),
        ],
        out_specs=[whole(s) for s in small_shapes],
        out_shape=small_shapes,
        compiler_params=pack_params,
        cost_estimate=cost(1 << 16, 1 << 18),
        name="pack_small",
    )(feat_left, feat_right, hidden, grad_hidden, hidden, grad_hidden, disparity)
    from_right = shift(to_left, "cols", -1)
    from_left = shift(to_right, "cols", 1)

    def features_for_right(start):
        at = start // size
        out = shape((half, B + EDGE, chan), BF16)
        return pl.pallas_call(
            lambda *refs: pack_right_kernel(start, *refs),
            grid=(half // size,),
            in_specs=[
                block((size, B, chan), at, cols // B - 1, 0),
                block((size, 8, chan), at, (cols - B) // 8 - 1, 0),
                block((size, 8, chan), at, last8, 0),
                whole(disparity),
            ],
            out_specs=by_rows(out, size),
            out_shape=out,
            compiler_params=pack_params,
            cost_estimate=cost(1 << 16, 2 << 20),
            name="pack_right",
        )(feat_right, feat_right, feat_left, disparity)

    packs, from_right, from_left = lax.optimization_barrier(
        ([features_for_right(0), features_for_right(half)], from_right, from_left)
    )
    before = [shift(pack, "cols", 1) for pack in packs]

    rim = shape((HALO, wide, 2 * B), BF16)
    edge_shape = shape((rows, EDGE, 2 * B), BF16)
    first_rim, last_rim, edge = pl.pallas_call(
        rim_kernel,
        grid=(1,),
        in_specs=[
            block((HALO, cols, B), 0, 0, 0),
            block((HALO, cols, B), 0, 0, 0),
            block((HALO, cols, B), rows // HALO - 1, 0, 0),
            block((HALO, cols, B), rows // HALO - 1, 0, 0),
            whole(from_right),
            whole(from_left),
        ],
        out_specs=[whole(rim), whole(rim), whole(edge_shape)],
        out_shape=(rim, rim, edge_shape),
        scratch_shapes=[pltpu.VMEM((EDGE, 2 * B), F32)],
        compiler_params=params,
        cost_estimate=cost(1 << 16, 2 << 20),
        name="rims",
    )(hidden, grad_hidden, hidden, grad_hidden, from_right, from_left)
    hg_top = shift(last_rim, "rows", 1)
    hg_low = shift(first_rim, "rows", -1)

    mw16 = jnp.pad(motion_weight, ((0, 16 - taps), (0, 0)))
    pads = [pltpu.VMEM((size, B, chan), BF16), pltpu.VMEM((B, B), BF16)]
    right_shapes = (shape((rows, B + EDGE, B), BF16), shape((rows, B, B), F32))
    mot_right, pre_right = pl.pallas_call(
        lambda *refs: right_corr_kernel(*args, *refs),
        grid=(steps,),
        in_specs=[
            block((size, B, chan), 0, 1, 0),
            by_rows(feat_right, size),
            whole(disparity),
            by_rows(from_right, size),
            whole(mw16),
        ],
        out_specs=[by_rows(s, size) for s in right_shapes],
        out_shape=right_shapes,
        scratch_shapes=pads + [pltpu.VMEM((size, EDGE, packed), F32)],
        compiler_params=params,
        cost_estimate=cost(2 * rows * B * 2 * B * chan, 6 << 20),
        name="corr_right",
    )(feat_left, feat_right, disparity, from_right, mw16)

    def left_lookup(start, before, rim_step):
        at = start // size
        shapes = (
            shape((half, wide, B), BF16),
            shape((half, B, B), F32),
            shape((HALO, wide, B), BF16),
        )
        return pl.pallas_call(
            lambda *refs: left_corr_kernel(*args, start, rim_step, *refs),
            grid=(half // size,),
            in_specs=[
                block((size, B, chan), at, 0, 0),
                block((size, B, chan), at, 0, 0),
                by_rows(before, size),
                whole(disparity),
                block((size, B + EDGE, B), at, 0, 0),
                whole(mw16),
            ],
            out_specs=[by_rows(s, size) for s in shapes[:2]] + [whole(shapes[2])],
            out_shape=shapes,
            scratch_shapes=pads,
            compiler_params=params,
            cost_estimate=cost(rows * B * 2 * B * chan, 3 << 20),
            name="corr_left",
        )(feat_left, feat_right, before, disparity, mot_right, mw16)

    mot_a, pre_a, rim_a = left_lookup(0, before[0], 0)
    mot_low = shift(rim_a, "rows", -1)
    mot_b, pre_b, rim_b = left_lookup(half, before[1], half // size - 1)
    mot_top = shift(rim_b, "rows", 1)
    first_left, _ = lax.optimization_barrier((feat_left[:, :B], mot_b))
    next_left = shift(first_left, "cols", -1)

    total = rows + 2 * HALO
    own_shape = shape((rows, cols, B), BF16)
    halo_shape = shape((total, wide, B), BF16)
    gate_shape = shape((total - 2, wide, 2 * B), F32)
    weight_shapes = [
        shape((9 * B, 2 * B), BF16),
        shape((24 * B, 2 * B), BF16),
        shape((2 * B, 9 * B), BF16),
        shape((2 * B, 24 * B), BF16),
    ]
    hid_operands = (
        hidden,
        grad_hidden,
        hg_top,
        hg_low,
        edge,
        gate_weight.reshape(-1, 2 * B),
        cand_weight.reshape(-1, B),
    )
    hid_shapes = (halo_shape, halo_shape, gate_shape, *weight_shapes)
    hid, grad, gates, wgm, wc, wcb, wgb = pl.pallas_call(
        gates_hidden_kernel,
        in_specs=[vmem] * len(hid_operands),
        out_specs=[vmem] * len(hid_shapes),
        out_shape=hid_shapes,
        scratch_shapes=[
            pltpu.VMEM((total, wide, 3 * B), BF16),
            pltpu.VMEM((9 * B, 2 * B), BF16),
        ],
        compiler_params=pltpu.CompilerParams(vmem_limit_bytes=GATES_VMEM),
        cost_estimate=cost(2 * 22 * wide * 9 * B * 2 * B, 16 << 20),
        name="gates_hidden",
    )(*hid_operands)
    big = (mot_a, mot_b, wgm, hid, gates, grad, wc, wcb, wgb, pre_a, pre_b, pre_right)
    small = (mot_top, mot_low, disparity, mw16)
    anywhere = pl.BlockSpec(memory_space=pl.ANY)
    new_hidden, pre_grad, tap_grad, _ = pl.pallas_call(
        gru_kernel,
        in_specs=[vmem] * (len(big) + len(small)),
        out_specs=[vmem] * 4,
        out_shape=(own_shape, own_shape, shape((rows, 16, B), BF16), gate_shape),
        input_output_aliases={4: 3},
        scratch_shapes=[pltpu.VMEM((total, wide, 3 * B), BF16)] * 4
        + [pltpu.VMEM((rows, cols, B), F32)],
        compiler_params=pltpu.CompilerParams(vmem_limit_bytes=GRU_VMEM),
        cost_estimate=cost(2 * 22 * wide * 256 * 256 * 20, 16 << 20),
        name="gru",
    )(*big, *small)
    next_grad = shift(tap_grad, "cols", -1)

    feat_shape = shape((rows, cols, chan), BF16)
    near_shape = shape((rows, B, B), BF16)
    mid = steps // 2
    grad_left, grad_first, near = pl.pallas_call(
        lambda *refs: grads_kernel(*args, *refs),
        grid=(steps,),
        in_specs=[
            by_rows(pre_grad, size),
            by_rows(feat_left, size),
            by_rows(feat_right, size),
            pl.BlockSpec((size, B + EDGE, chan), lambda i: (jnp.minimum(i, mid - 1), 0, 0)),
            pl.BlockSpec((size, B + EDGE, chan), lambda i: (jnp.maximum(i - mid, 0), 0, 0)),
            whole(disparity),
            whole(mw16),
        ],
        out_specs=[
            by_rows(feat_shape, size),
            block((size, B, chan), 0, 0, 0),
            by_rows(near_shape, size),
        ],
        out_shape=(feat_shape, feat_shape, near_shape),
        scratch_shapes=[pltpu.VMEM((B, B), BF16)],
        compiler_params=params,
        cost_estimate=cost(2 * rows * B * 2 * B * chan * 4, 12 << 20),
        name="grads",
    )(pre_grad, feat_left, feat_right, before[0], before[1], disparity, mw16)
    grad_right = pl.pallas_call(
        lambda *refs: last_kernel(*args, *refs),
        grid=(steps,),
        in_specs=[
            by_rows(near, size),
            by_rows(next_grad, size),
            block((size, B, chan), 0, 1, 0),
            by_rows(next_left, size),
            anywhere,
        ],
        out_specs=block((size, B, chan), 0, 1, 0),
        out_shape=feat_shape,
        input_output_aliases={4: 0},
        compiler_params=params,
        cost_estimate=cost(2 * rows * B * 2 * B * chan, 4 << 20),
        name="grad_right",
    )(near, next_grad, feat_left, next_left, grad_first)
    return (new_hidden, grad_left, grad_right)


def solution(mesh):
    grid3 = P("rows", "cols", None)
    return jax.shard_map(
        per_device,
        mesh=mesh,
        in_specs=(grid3, grid3, grid3, P("rows", "cols"), P(), P(), P(), grid3),
        out_specs=(grid3, grid3, grid3),
        check_vma=False,
    )
```

```python
import math

import jax
import jax.numpy as jnp
from jax import lax
from jax.experimental import pallas as pl
from jax.experimental.pallas import tpu as pltpu
from jax.sharding import PartitionSpec as P

B = 128
HALO = 4
EDGE = 16
F32 = jnp.float32
BF16 = jnp.bfloat16
ROWS = 4
SMALL_VMEM = 16 * 1024 * 1024
GRU_VMEM = 36 * 1024 * 1024
GATES_VMEM = 12 * 1024 * 1024
PACK_VMEM = 60 * 1024 * 1024


def shift(array, axis, by):
    size = lax.axis_size(axis)
    pairs = [(i, i + by) for i in range(size) if 0 <= i + by < size]
    return lax.ppermute(array, axis, pairs)


def dot_nt(a, b):
    return lax.dot_general(a, b, (((1,), (1,)), ((), ())), preferred_element_type=F32)


def dot(a, b):
    return jnp.dot(a, b, preferred_element_type=F32)


def iota(shape, dim):
    return lax.broadcasted_iota(jnp.int32, shape, dim)


def lane_gather(values, index):
    return jnp.take_along_axis(values, index, axis=1, mode="promise_in_bounds")


def down_lanes(row):
    return jnp.transpose(jnp.broadcast_to(row, (B, B)), (1, 0))


def pick_taps(far, near, disp, taps, radius, scale, first=0):
    count = far.shape[0]
    pixel = iota((count, B), 0) + first
    lane = iota((count, B), 1)
    merged = jnp.where(lane > pixel, far, near)
    level = disp + lane - radius
    usable = (level >= 0) & (level < B) & (lane < taps)
    picked = lane_gather(merged, (pixel - level) & (B - 1))
    return (jnp.where(usable, picked, 0.0) * scale).astype(BF16)


def silu(v):
    return v * jax.nn.sigmoid(v)


def level_columns(disp_ref, at):
    return jnp.transpose(disp_ref[:, at : at + B].astype(F32), (1, 0))


def level_row(disp_ref, row, at):
    levels = disp_ref[:, at : at + B]
    return jnp.sum(jnp.where(iota(levels.shape, 0) == row, levels, 0), axis=0, keepdims=True)


def pack_small_kernel(
    left_ref,
    own_ref,
    hid_ref,
    grad_ref,
    beside_ref,
    left_last_ref,
    hid_last_ref,
    grad_last_ref,
    disp_ref,
    out_ref,
    last_ref,
):
    rows, _, chan = left_ref.shape
    levels = jnp.transpose(disp_ref[:, :B].astype(F32), (1, 0))
    last_levels = jnp.transpose(disp_ref[:, disp_ref.shape[1] - B :].astype(F32), (1, 0))
    low = iota((8, chan), 0) < HALO
    for r in range(rows):
        out_ref[r, :, :chan] = left_ref[r, :HALO]
        out_ref[r, :, chan : 2 * chan] = own_ref[r, :HALO]
        out_ref[r, :, 2 * chan : 2 * chan + B] = hid_ref[r, :HALO]
        out_ref[r, :, 2 * chan + B : 2 * chan + 2 * B] = grad_ref[r, :HALO]
        level = jnp.broadcast_to(levels[:8, r : r + 1], (8, B))
        out_ref[r, :, 2 * chan + 2 * B :] = level.astype(BF16)[:HALO]
        beside = pltpu.roll(beside_ref[r].astype(F32), HALO, 0)
        upper = jnp.where(low, beside, left_last_ref[r].astype(F32))
        level = jnp.broadcast_to(last_levels[B - 8 :, r : r + 1], (8, chan))
        hg = jnp.concatenate([hid_last_ref[r], grad_last_ref[r]], axis=1).astype(F32)
        lower = jnp.where(low, pltpu.roll(level, HALO, 0), hg)
        last_ref[r] = jnp.concatenate([upper, lower], axis=0).astype(BF16)


def rim_kernel(
    hid_first_ref,
    grad_first_ref,
    hid_last_ref,
    grad_last_ref,
    right_ref,
    left_ref,
    first_ref,
    last_ref,
    edge_ref,
    pad_ref,
):
    rows = right_ref.shape[0]
    own = hid_first_ref.shape[1]
    chan = (right_ref.shape[2] - 3 * B) // 2
    pad_ref[...] = jnp.zeros_like(pad_ref)
    last = iota(pad_ref.shape, 0) >= EDGE - HALO
    for r in range(rows):
        pad_ref[:HALO] = right_ref[r, :, 2 * chan : 2 * chan + 2 * B].astype(F32)
        edge_ref[r] = jnp.where(last, left_ref[r].astype(F32), pad_ref[...]).astype(BF16)
    for r in range(HALO):
        for out, hid, grad, row in (
            (first_ref, hid_first_ref, grad_first_ref, r),
            (last_ref, hid_last_ref, grad_last_ref, rows - HALO + r),
        ):
            out[r, :own, :B] = hid[r]
            out[r, :own, B:] = grad[r]
            out[r, own:] = edge_ref[row]


def taps_matrix(weight_ref, pad_ref):
    pad_ref[...] = jnp.zeros_like(pad_ref)
    pad_ref[: weight_ref.shape[0]] = weight_ref[...]
    return pad_ref[...]


def right_corr_kernel(
    taps,
    radius,
    scale,
    left_ref,
    own_ref,
    disp_ref,
    edge_ref,
    weight_ref,
    mot_ref,
    pre_ref,
    pad_ref,
    mw_ref,
    side_ref,
):
    rows, _, chan = own_ref.shape
    first = pl.program_id(0) * rows
    pad_ref[...] = jnp.zeros_like(pad_ref)
    side_ref[...] = jnp.zeros_like(side_ref)
    weight = taps_matrix(weight_ref, mw_ref)
    for r in range(rows):
        side_ref[r, :HALO] = edge_ref[r].astype(F32)
        edge = side_ref[r]
        pad_ref[r, :EDGE] = edge[:, chan : 2 * chan].astype(BF16)
        side = edge[:, :chan].astype(BF16)
        scores = dot_nt(jnp.concatenate([left_ref[r], side], axis=0), own_ref[r])
        disp = down_lanes(level_row(disp_ref, first + r, B))
        main = pick_taps(scores[:B, :B], scores[:B, B:], disp, taps, radius, scale)
        disp = edge[:, 2 * chan + 2 * B :].astype(jnp.int32)
        beside = pick_taps(
            scores[B:, B:], dot_nt(side, pad_ref[r]), disp, taps, radius, scale
        )
        pre = dot(jnp.concatenate([main, beside], axis=0), weight)
        pre_ref[r] = pre[:B]
        mot_ref[r] = silu(pre).astype(BF16)


def left_corr_kernel(
    taps,
    radius,
    scale,
    start,
    rim_step,
    left_ref,
    own_ref,
    before_ref,
    extra_ref,
    disp_ref,
    mot_right_ref,
    weight_ref,
    mot_ref,
    pre_ref,
    rim_ref,
    pad_ref,
    mw_ref,
):
    rows, _, chan = own_ref.shape
    step = pl.program_id(0)
    first = start + step * rows
    pad_ref[...] = jnp.zeros_like(pad_ref)
    weight = taps_matrix(weight_ref, mw_ref)
    last = iota((EDGE, chan), 0) >= EDGE - HALO
    upper = iota((EDGE, B), 0) < EDGE // 2
    for r in range(rows):
        extra = extra_ref[r].astype(F32)
        pad_ref[r, B - EDGE :] = jnp.where(last, pltpu.roll(extra, 12, 0), 0.0).astype(BF16)
        side = jnp.where(last, pltpu.roll(extra, 8, 0), 0.0).astype(BF16)
        window = jnp.concatenate([before_ref[r], own_ref[r]], axis=0)
        scores = dot_nt(jnp.concatenate([left_ref[r], side], axis=0), window)
        disp = down_lanes(level_row(disp_ref, first + r, 0))
        main = pick_taps(scores[:B, :B], scores[:B, B:], disp, taps, radius, scale)
        disp = pltpu.roll(extra, 4, 0)[:, :B].astype(jnp.int32)
        beside = pick_taps(
            dot_nt(side, pad_ref[r]), scores[B:, :B], disp, taps, radius, scale, B - EDGE
        )
        pre = dot(jnp.concatenate([main, beside], axis=0), weight)
        pre_ref[r] = pre[:B]
        mot = silu(pre)
        mot_ref[r, :B] = mot[:B].astype(BF16)
        mot_ref[r, B : 2 * B] = mot_right_ref[r, :B]
        right_edge = mot_right_ref[r, B:].astype(F32)
        mot_ref[r, 2 * B :] = jnp.where(upper, right_edge, mot[B:]).astype(BF16)

    @pl.when(step == rim_step)
    def _():
        rim_ref[...] = mot_ref[...]


def shifted(value):
    return (
        pltpu.roll(value, 1, 0).astype(BF16),
        value.astype(BF16),
        pltpu.roll(value, value.shape[0] - 1, 0).astype(BF16),
    )


def store3(buf, row, value):
    for b, part in enumerate(shifted(value)):
        buf[row, :, b * B : (b + 1) * B] = part


def lanes(buf, rows, b):
    return jnp.concatenate([buf[r, :, b * B : (b + 1) * B] for r in rows], axis=0)


def patches(bufs, row_sets):
    return jnp.concatenate(
        [lanes(buf, rows, b) for rows in row_sets for b in range(3) for buf in bufs], axis=1
    )


def chunks(values, size):
    values = list(values)
    return [values[i : i + size] for i in range(0, len(values), size)]


CHUNK = 4


def join_columns(buf, row, own_row, edge_row):
    own = own_row.shape[0]
    buf[row, :own] = own_row
    buf[row, own:] = edge_row


def gates_hidden_kernel(
    hid_ref,
    edge_ref,
    gate_ref,
    cand_ref,
    gh_ref,
    wgm_ref,
    wc_ref,
    wcb_ref,
    wgb_ref,
    h_ref,
    h3_ref,
    wgh_ref,
):
    rows, own, _ = hid_ref.shape
    wide = own + EDGE
    for row in range(rows):
        join_columns(h_ref, 0, hid_ref[row], edge_ref[row, :, :B])
        store3(h3_ref, row, h_ref[0].astype(F32))
    zeros = jnp.zeros((6 * B, B), BF16)
    wc_ref[18 * B :, :B] = zeros
    wc_ref[: 6 * B, B:] = zeros
    wc_ref[: 18 * B, :B] = cand_ref[...]
    wc_ref[6 * B :, B:] = cand_ref[...]
    wgb_ref[:B, 18 * B :] = jnp.zeros((B, 6 * B), BF16)
    wgb_ref[B:, : 6 * B] = jnp.zeros((B, 6 * B), BF16)
    for n in range(9):
        wgh_ref[n * B : (n + 1) * B] = gate_ref[2 * n * B : (2 * n + 1) * B]
        wgm_ref[n * B : (n + 1) * B] = gate_ref[(2 * n + 1) * B : (2 * n + 2) * B]
        at = (8 - n) * 2 * B
        wcb_ref[:, n * B : (n + 1) * B] = cand_ref[at : at + 2 * B]
        for s in range(2):
            col = (n + 3 * s) * 2 * B
            wgb_ref[s * B : (s + 1) * B, col : col + 2 * B] = gate_ref[at + B : at + 2 * B]
    for group in chunks(range(1, rows - 1), CHUNK):
        lhs = patches((h3_ref,), [[r + a - 1 for r in group] for a in range(3)])
        acc = dot(lhs, wgh_ref[...])
        for n, row in enumerate(group):
            gh_ref[row - 1] = acc[n * wide : (n + 1) * wide]


def gru_kernel(
    hid_ref,
    grad_ref,
    hgt_ref,
    hgb_ref,
    edge_ref,
    mota_ref,
    motb_ref,
    mott_ref,
    motl_ref,
    wg_ref,
    wgm_ref,
    gates_ref,
    wc_ref,
    wcb_ref,
    wgb_ref,
    prela_ref,
    prelb_ref,
    prer_ref,
    disp_ref,
    mw_ref,
    nh_ref,
    pg_ref,
    tg_ref,
    u3_ref,
    m3_ref,
    r3_ref,
    c3_ref,
    cb_ref,
    h_ref,
    g_ref,
    gh_ref,
):
    rows, own, _ = nh_ref.shape
    half = rows // 2
    wide = own + EDGE
    total = rows + 2 * HALO
    inner = range(HALO, HALO + rows)
    known = range(HALO + 1, HALO + rows - 1)
    for row in range(total):
        n = row - HALO
        if n < 0 or n >= rows:
            hg = hgt_ref[row] if n < 0 else hgb_ref[n - rows]
            mot = mott_ref[row] if n < 0 else motl_ref[n - rows]
            h_ref[row] = hg[:, :B]
            g_ref[row] = hg[:, B:]
        else:
            mot = mota_ref[n] if n < half else motb_ref[n - half]
            join_columns(h_ref, row, hid_ref[n], edge_ref[n, :, :B])
            join_columns(g_ref, row, grad_ref[n], edge_ref[n, :, B:])
        store3(m3_ref, row, mot.astype(F32))
        if row <= known[0] or row >= known[-1]:
            store3(u3_ref, row, h_ref[row].astype(F32))

    def gate(row, value):
        value = jax.nn.sigmoid(value)
        gh_ref[row - 1] = value
        store3(r3_ref, row, value[:, B:] * h_ref[row].astype(F32))

    for group in (list(range(1, known[0])), list(range(known[-1] + 1, total - 1))):
        lhs = patches((u3_ref, m3_ref), [[r + a - 1 for r in group] for a in range(3)])
        acc = dot(lhs, wg_ref[...])
        for n, row in enumerate(group):
            gate(row, acc[n * wide : (n + 1) * wide])
    for group in chunks(known, CHUNK):
        lhs = patches((m3_ref,), [[r + a - 1 for r in group] for a in range(3)])
        acc = dot(lhs, wgm_ref[...])
        for n, row in enumerate(group):
            gate(row, acc[n * wide : (n + 1) * wide] + gates_ref[row - known[0]])

    for group in chunks(range(2, total - 2, 2), CHUNK):
        lhs = patches((r3_ref, m3_ref), [[r + t - 1 for r in group] for t in range(4)])
        acc = jnp.tanh(dot(lhs, wc_ref[...]))
        for n, top in enumerate(group):
            for row in (top, top + 1):
                s = row - top
                cand = acc[n * wide : (n + 1) * wide, s * B : (s + 1) * B]
                hidden = h_ref[row].astype(F32)
                update = gh_ref[row - 1, :, :B]
                if row in inner:
                    new = (1.0 - update) * hidden + update * cand
                    nh_ref[row - HALO] = new[:own].astype(BF16)
                gu = g_ref[row].astype(F32) * update
                store3(c3_ref, row, gu * (1.0 - cand * cand))
                store3(u3_ref, row, gu * (cand - hidden) * (1.0 - update))

    for group in chunks(range(3, total - 3), CHUNK):
        lhs = patches((c3_ref,), [[r + a - 1 for r in group] for a in range(3)])
        acc = dot_nt(lhs, wcb_ref[...])
        for n, row in enumerate(group):
            back = acc[n * wide : (n + 1) * wide]
            reset = gh_ref[row - 1, :, B:]
            store3(m3_ref, row, back[:, :B] * h_ref[row].astype(F32) * reset * (1.0 - reset))
            if row in inner:
                cb_ref[row - HALO] = back[:own, B:]

    for group in chunks(range(HALO, HALO + rows, 2), CHUNK):
        lhs = patches((u3_ref, m3_ref), [[r + t - 1 for r in group] for t in range(4)])
        acc = dot_nt(lhs, wgb_ref[...])
        for n, top in enumerate(group):
            for row in (top - HALO, top + 1 - HALO):
                s = row + HALO - top
                back = acc[n * wide : n * wide + own, s * B : (s + 1) * B]
                prel = prela_ref[row] if row < half else prelb_ref[row - half]
                pre = jnp.concatenate([prel, prer_ref[row]], axis=0)
                sig = jax.nn.sigmoid(pre)
                grad = (cb_ref[row] + back) * sig * (1.0 + pre * (1.0 - sig))
                grad = grad.astype(BF16)
                pg_ref[row] = grad
                tap = dot_nt(mw_ref[...], grad[:B])
                level = jnp.broadcast_to(disp_ref[row : row + 1, :B].astype(F32), tap.shape)
                tg_ref[row] = jnp.where(iota(tap.shape, 0) == 15, level, tap).astype(BF16)


def spread(grad, disp, taps, radius):
    pixel = iota((B, B), 0)
    lane = iota((B, B), 1)
    tap = ((pixel - lane) & (B - 1)) - disp + radius
    ok = (tap >= 0) & (tap < taps)
    value = jnp.where(ok, lane_gather(grad, tap & (B - 1)), 0.0)
    far = jnp.where(lane > pixel, value, 0.0).astype(BF16)
    near = jnp.where(lane > pixel, 0.0, value).astype(BF16)
    return far, near


def spread_t(grad, disp, taps, radius):
    column = iota((B, B), 0)
    pixel = iota((B, B), 1)
    tap = ((pixel - column) & (B - 1)) - disp + radius
    value = jnp.zeros((B, B), F32)
    for k in range(taps):
        value = jnp.where(tap == k, grad[k : k + 1], value)
    far = jnp.where(column > pixel, value, 0.0).astype(BF16)
    near = jnp.where(column > pixel, 0.0, value).astype(BF16)
    return far, near


def grads_kernel(
    taps,
    radius,
    scale,
    pg_ref,
    left_ref,
    own_ref,
    before_a_ref,
    before_b_ref,
    disp_ref,
    weight_ref,
    gl_ref,
    gr_ref,
    near_ref,
    mw_ref,
):
    rows = left_ref.shape[0]
    step = pl.program_id(0)
    head = step < pl.num_programs(0) // 2
    weight_t = weight_ref[...]
    weight = taps_matrix(weight_ref, mw_ref)
    for r in range(rows):
        grads = dot_nt(pg_ref[r], weight).astype(BF16).astype(F32)
        grads_t = dot_nt(weight_t, pg_ref[r]).astype(BF16).astype(F32)
        parts = []
        parts_t = []
        for block in range(2):
            at = slice(block * B, (block + 1) * B)
            row = level_row(disp_ref, step * rows + r, block * B)
            parts.append(spread(grads[at], down_lanes(row), taps, radius))
            parts_t.append(spread_t(grads_t[:, at], row, taps, radius))
        before = jnp.where(head, before_a_ref[r], before_b_ref[r])
        window = jnp.concatenate([before, own_ref[r, :B]], axis=0)
        gl_ref[r, :B] = (dot(jnp.concatenate(parts[0], axis=1), window) * scale).astype(BF16)
        gl_ref[r, B:] = (dot(jnp.concatenate(parts[1], axis=1), own_ref[r]) * scale).astype(BF16)
        sg = jnp.concatenate([parts_t[0][1], parts_t[1][0]], axis=1)
        gr_ref[r] = (dot(sg, left_ref[r]) * scale).astype(BF16)
        near_ref[r] = parts_t[1][1]


def last_kernel(taps, radius, scale, near_ref, grad_ref, left_ref, next_ref, first_ref, gr_ref):
    del first_ref
    rows = left_ref.shape[0]
    for r in range(rows):
        grad = grad_ref[r].astype(F32)
        disp = grad[15:16].astype(jnp.int32)
        far, _ = spread_t(grad, disp, taps, radius)
        sg = jnp.concatenate([near_ref[r], far], axis=1)
        window = jnp.concatenate([left_ref[r], next_ref[r]], axis=0)
        gr_ref[r] = (dot(sg, window) * scale).astype(BF16)


def whole(array):
    nd = array.ndim
    return pl.BlockSpec(array.shape, lambda i: (0,) * nd)


def by_rows(array, size, block=None, at=None):
    block = tuple(array.shape[1:]) if block is None else block
    at = (0,) * len(block) if at is None else at
    return pl.BlockSpec((size,) + block, lambda i: (i,) + at)


def cost(flops, bytes_accessed):
    return pl.CostEstimate(flops=flops, bytes_accessed=bytes_accessed, transcendentals=0)


def block(shape, *at):
    return pl.BlockSpec(shape, lambda i: (i + at[0],) + at[1:])


def per_device(
    feat_left, feat_right, hidden, disparity, motion_weight, gate_weight, cand_weight, grad_hidden
):
    rows, cols, chan = feat_left.shape
    taps = motion_weight.shape[0]
    radius = taps // 2
    scale = 1.0 / math.sqrt(chan)
    args = (taps, radius, scale)
    size = ROWS
    steps = rows // size
    half = rows // 2
    wide = cols + EDGE
    packed = 2 * chan + 3 * B
    params = pltpu.CompilerParams(vmem_limit_bytes=SMALL_VMEM)
    shape = jax.ShapeDtypeStruct
    vmem = pl.BlockSpec(memory_space=pltpu.VMEM)
    last8 = cols // 8 - 1
    pack_params = pltpu.CompilerParams(vmem_limit_bytes=PACK_VMEM)

    small_shapes = (shape((rows, HALO, packed), BF16), shape((rows, EDGE, chan), BF16))
    to_left, to_right = pl.pallas_call(
        pack_small_kernel,
        grid=(1,),
        in_specs=[
            block((rows, 8, chan), 0, 0, 0),
            block((rows, 8, chan), 0, 0, 0),
            block((rows, 8, B), 0, 0, 0),
            block((rows, 8, B), 0, 0, 0),
            block((rows, 8, chan), 0, (cols - B) // 8 - 1, 0),
            block((rows, 8, chan), 0, last8, 0),
            block((rows, 8, B), 0, last8, 0),
            block((rows, 8, B), 0, last8, 0),
            whole(disparity),
        ],
        out_specs=[whole(s) for s in small_shapes],
        out_shape=small_shapes,
        compiler_params=pack_params,
        cost_estimate=cost(1 << 16, 1 << 18),
        name="pack_small",
    )(
        feat_left,
        feat_right,
        hidden,
        grad_hidden,
        feat_right,
        feat_left,
        hidden,
        grad_hidden,
        disparity,
    )
    from_right = shift(to_left, "cols", -1)
    from_left = shift(to_right, "cols", 1)
    features = feat_right[:, cols - B :]
    second, from_right, from_left = lax.optimization_barrier(
        (features[half:], from_right, from_left)
    )
    before = [shift(features[:half], "cols", 1), shift(second, "cols", 1)]

    rim = shape((HALO, wide, 2 * B), BF16)
    edge_shape = shape((rows, EDGE, 2 * B), BF16)
    first_rim, last_rim, edge = pl.pallas_call(
        rim_kernel,
        grid=(1,),
        in_specs=[
            block((HALO, cols, B), 0, 0, 0),
            block((HALO, cols, B), 0, 0, 0),
            block((HALO, cols, B), rows // HALO - 1, 0, 0),
            block((HALO, cols, B), rows // HALO - 1, 0, 0),
            whole(from_right),
            whole(from_left),
        ],
        out_specs=[whole(rim), whole(rim), whole(edge_shape)],
        out_shape=(rim, rim, edge_shape),
        scratch_shapes=[pltpu.VMEM((EDGE, 2 * B), F32)],
        compiler_params=params,
        cost_estimate=cost(1 << 16, 2 << 20),
        name="rims",
    )(hidden, grad_hidden, hidden, grad_hidden, from_right, from_left)
    hg_top = shift(last_rim, "rows", 1)
    hg_low = shift(first_rim, "rows", -1)

    mw16 = jnp.pad(motion_weight, ((0, 16 - taps), (0, 0)))
    pads = [pltpu.VMEM((size, B, chan), BF16), pltpu.VMEM((B, B), BF16)]
    right_shapes = (shape((rows, B + EDGE, B), BF16), shape((rows, B, B), F32))
    mot_right, pre_right = pl.pallas_call(
        lambda *refs: right_corr_kernel(*args, *refs),
        grid=(steps,),
        in_specs=[
            block((size, B, chan), 0, 1, 0),
            by_rows(feat_right, size),
            whole(disparity),
            by_rows(from_right, size),
            whole(mw16),
        ],
        out_specs=[by_rows(s, size) for s in right_shapes],
        out_shape=right_shapes,
        scratch_shapes=pads + [pltpu.VMEM((size, EDGE, packed), F32)],
        compiler_params=params,
        cost_estimate=cost(2 * rows * B * 2 * B * chan, 6 << 20),
        name="corr_right",
    )(feat_left, feat_right, disparity, from_right, mw16)

    def left_lookup(start, before, rim_step):
        at = start // size
        shapes = (
            shape((half, wide, B), BF16),
            shape((half, B, B), F32),
            shape((HALO, wide, B), BF16),
        )
        return pl.pallas_call(
            lambda *refs: left_corr_kernel(*args, start, rim_step, *refs),
            grid=(half // size,),
            in_specs=[
                block((size, B, chan), at, 0, 0),
                block((size, B, chan), at, 0, 0),
                by_rows(before, size),
                block((size, EDGE, chan), at, 0, 0),
                whole(disparity),
                block((size, B + EDGE, B), at, 0, 0),
                whole(mw16),
            ],
            out_specs=[by_rows(s, size) for s in shapes[:2]] + [whole(shapes[2])],
            out_shape=shapes,
            scratch_shapes=pads,
            compiler_params=params,
            cost_estimate=cost(rows * B * 2 * B * chan, 3 << 20),
            name="corr_left",
        )(feat_left, feat_right, before, from_left, disparity, mot_right, mw16)

    mot_a, pre_a, rim_a = left_lookup(0, before[0], 0)
    mot_low = shift(rim_a, "rows", -1)
    mot_b, pre_b, rim_b = left_lookup(half, before[1], half // size - 1)
    mot_top = shift(rim_b, "rows", 1)
    first_left, _ = lax.optimization_barrier((feat_left[:, :B], mot_b))
    next_left = shift(first_left, "cols", -1)

    total = rows + 2 * HALO
    own_shape = shape((rows, cols, B), BF16)
    gate_shape = shape((rows - 2, wide, 2 * B), F32)
    weight_shapes = [
        shape((9 * B, 2 * B), BF16),
        shape((24 * B, 2 * B), BF16),
        shape((2 * B, 9 * B), BF16),
        shape((2 * B, 24 * B), BF16),
    ]
    wg = gate_weight.reshape(-1, 2 * B)
    hid_operands = (hidden, edge, wg, cand_weight.reshape(-1, B))
    hid_shapes = (gate_shape, *weight_shapes)
    gates, wgm, wc, wcb, wgb = pl.pallas_call(
        gates_hidden_kernel,
        in_specs=[vmem] * len(hid_operands),
        out_specs=[vmem] * len(hid_shapes),
        out_shape=hid_shapes,
        scratch_shapes=[
            pltpu.VMEM((1, wide, B), BF16),
            pltpu.VMEM((rows, wide, 3 * B), BF16),
            pltpu.VMEM((9 * B, 2 * B), BF16),
        ],
        compiler_params=pltpu.CompilerParams(vmem_limit_bytes=GATES_VMEM),
        cost_estimate=cost(2 * 22 * wide * 9 * B * 2 * B, 16 << 20),
        name="gates_hidden",
    )(*hid_operands)
    operands = (
        hidden,
        grad_hidden,
        hg_top,
        hg_low,
        edge,
        mot_a,
        mot_b,
        mot_top,
        mot_low,
        wg,
        wgm,
        gates,
        wc,
        wcb,
        wgb,
        pre_a,
        pre_b,
        pre_right,
        disparity,
        mw16,
    )
    anywhere = pl.BlockSpec(memory_space=pl.ANY)
    halo_buffer = pltpu.VMEM((total, wide, B), BF16)
    new_hidden, pre_grad, tap_grad = pl.pallas_call(
        gru_kernel,
        in_specs=[vmem] * len(operands),
        out_specs=[vmem] * 3,
        out_shape=(own_shape, own_shape, shape((rows, 16, B), BF16)),
        scratch_shapes=[pltpu.VMEM((total, wide, 3 * B), BF16)] * 4
        + [pltpu.VMEM((rows, cols, B), F32), halo_buffer, halo_buffer]
        + [pltpu.VMEM((total - 2, wide, 2 * B), F32)],
        compiler_params=pltpu.CompilerParams(vmem_limit_bytes=GRU_VMEM),
        cost_estimate=cost(2 * 22 * wide * 256 * 256 * 20, 16 << 20),
        name="gru",
    )(*operands)
    next_grad = shift(tap_grad, "cols", -1)

    feat_shape = shape((rows, cols, chan), BF16)
    near_shape = shape((rows, B, B), BF16)
    mid = steps // 2
    grad_left, grad_first, near = pl.pallas_call(
        lambda *refs: grads_kernel(*args, *refs),
        grid=(steps,),
        in_specs=[
            by_rows(pre_grad, size),
            by_rows(feat_left, size),
            by_rows(feat_right, size),
            pl.BlockSpec((size, B, chan), lambda i: (jnp.minimum(i, mid - 1), 0, 0)),
            pl.BlockSpec((size, B, chan), lambda i: (jnp.maximum(i - mid, 0), 0, 0)),
            whole(disparity),
            whole(mw16),
        ],
        out_specs=[
            by_rows(feat_shape, size),
            block((size, B, chan), 0, 0, 0),
            by_rows(near_shape, size),
        ],
        out_shape=(feat_shape, feat_shape, near_shape),
        scratch_shapes=[pltpu.VMEM((B, B), BF16)],
        compiler_params=params,
        cost_estimate=cost(2 * rows * B * 2 * B * chan * 4, 12 << 20),
        name="grads",
    )(pre_grad, feat_left, feat_right, before[0], before[1], disparity, mw16)
    grad_right = pl.pallas_call(
        lambda *refs: last_kernel(*args, *refs),
        grid=(steps,),
        in_specs=[
            by_rows(near, size),
            by_rows(next_grad, size),
            block((size, B, chan), 0, 1, 0),
            by_rows(next_left, size),
            anywhere,
        ],
        out_specs=block((size, B, chan), 0, 1, 0),
        out_shape=feat_shape,
        input_output_aliases={4: 0},
        compiler_params=params,
        cost_estimate=cost(2 * rows * B * 2 * B * chan, 4 << 20),
        name="grad_right",
    )(near, next_grad, feat_left, next_left, grad_first)
    return (new_hidden, grad_left, grad_right)


def solution(mesh):
    grid3 = P("rows", "cols", None)
    return jax.shard_map(
        per_device,
        mesh=mesh,
        in_specs=(grid3, grid3, grid3, P("rows", "cols"), P(), P(), P(), grid3),
        out_specs=(grid3, grid3, grid3),
        check_vma=False,
    )
```

```python
import math

import jax
import jax.numpy as jnp
from jax import lax
from jax.experimental import pallas as pl
from jax.experimental.pallas import tpu as pltpu
from jax.sharding import PartitionSpec as P

B = 128
HALO = 4
EDGE = 16
F32 = jnp.float32
BF16 = jnp.bfloat16
ROWS = 4
SMALL_VMEM = 16 * 1024 * 1024
GRU_VMEM = 36 * 1024 * 1024
GATES_VMEM = 12 * 1024 * 1024
PACK_VMEM = 60 * 1024 * 1024


def shift(array, axis, by):
    size = lax.axis_size(axis)
    pairs = [(i, i + by) for i in range(size) if 0 <= i + by < size]
    return lax.ppermute(array, axis, pairs)


def dot_nt(a, b):
    return lax.dot_general(a, b, (((1,), (1,)), ((), ())), preferred_element_type=F32)


def dot(a, b):
    return jnp.dot(a, b, preferred_element_type=F32)


def iota(shape, dim):
    return lax.broadcasted_iota(jnp.int32, shape, dim)


def lane_gather(values, index):
    return jnp.take_along_axis(values, index, axis=1, mode="promise_in_bounds")


def down_lanes(row):
    return jnp.transpose(jnp.broadcast_to(row, (B, B)), (1, 0))


def pick_taps(far, near, disp, taps, radius, scale, first=0):
    count = far.shape[0]
    pixel = iota((count, B), 0) + first
    lane = iota((count, B), 1)
    merged = jnp.where(lane > pixel, far, near)
    level = disp + lane - radius
    usable = (level >= 0) & (level < B) & (lane < taps)
    picked = lane_gather(merged, (pixel - level) & (B - 1))
    return (jnp.where(usable, picked, 0.0) * scale).astype(BF16)


def silu(v):
    return v * jax.nn.sigmoid(v)


def level_columns(disp_ref, at):
    return jnp.transpose(disp_ref[:, at : at + B].astype(F32), (1, 0))


def level_row(disp_ref, row, at):
    levels = disp_ref[:, at : at + B]
    return jnp.sum(jnp.where(iota(levels.shape, 0) == row, levels, 0), axis=0, keepdims=True)


def pack_small_kernel(
    left_ref,
    own_ref,
    hid_ref,
    grad_ref,
    beside_ref,
    left_last_ref,
    hid_last_ref,
    grad_last_ref,
    features_ref,
    disp_ref,
    out_ref,
    last_ref,
):
    rows, _, chan = left_ref.shape
    half = features_ref.shape[0]
    for r in range(half):
        last_ref[r * B : (r + 1) * B] = features_ref[r]
    levels = jnp.transpose(disp_ref[:, :B].astype(F32), (1, 0))
    last_levels = jnp.transpose(disp_ref[:, disp_ref.shape[1] - B :].astype(F32), (1, 0))
    low = iota((8, chan), 0) < HALO
    for r in range(rows):
        out_ref[r, :, :chan] = left_ref[r, :HALO]
        out_ref[r, :, chan : 2 * chan] = own_ref[r, :HALO]
        out_ref[r, :, 2 * chan : 2 * chan + B] = hid_ref[r, :HALO]
        out_ref[r, :, 2 * chan + B : 2 * chan + 2 * B] = grad_ref[r, :HALO]
        level = jnp.broadcast_to(levels[:8, r : r + 1], (8, B))
        out_ref[r, :, 2 * chan + 2 * B :] = level.astype(BF16)[:HALO]
        beside = pltpu.roll(beside_ref[r].astype(F32), HALO, 0)
        upper = jnp.where(low, beside, left_last_ref[r].astype(F32))
        level = jnp.broadcast_to(last_levels[B - 8 :, r : r + 1], (8, chan))
        hg = jnp.concatenate([hid_last_ref[r], grad_last_ref[r]], axis=1).astype(F32)
        lower = jnp.where(low, pltpu.roll(level, HALO, 0), hg)
        at = half * B + r * EDGE
        last_ref[at : at + EDGE] = jnp.concatenate([upper, lower], axis=0).astype(BF16)


def join_columns(buf, row, own_row, edge_row):
    own = own_row.shape[0]
    buf[row, :own] = own_row
    buf[row, own:] = edge_row


def rim_kernel(
    hid_first_ref,
    grad_first_ref,
    hid_last_ref,
    grad_last_ref,
    right_ref,
    left_ref,
    first_ref,
    last_ref,
    edge_ref,
    pad_ref,
):
    rows = right_ref.shape[0]
    own = hid_first_ref.shape[1]
    chan = left_ref.shape[1]
    pad_ref[...] = jnp.zeros_like(pad_ref)
    last = iota(pad_ref.shape, 0) >= EDGE - HALO
    for r in range(rows):
        pad_ref[:HALO] = right_ref[r, :, 2 * chan : 2 * chan + 2 * B].astype(F32)
        left = left_ref[r * EDGE : (r + 1) * EDGE].astype(F32)
        edge_ref[r] = jnp.where(last, left, pad_ref[...]).astype(BF16)
    for r in range(HALO):
        join_columns(first_ref, r, hid_first_ref[r], edge_ref[r, :, :B])
        join_columns(last_ref, r, hid_last_ref[r], edge_ref[rows - HALO + r, :, :B])
    for r in range(HALO // 2):
        join_columns(first_ref, HALO + r, grad_first_ref[r], edge_ref[r, :, B:])
        row = HALO - HALO // 2 + r
        join_columns(last_ref, HALO + r, grad_last_ref[row], edge_ref[rows - HALO + row, :, B:])


def taps_matrix(weight_ref, pad_ref):
    pad_ref[...] = jnp.zeros_like(pad_ref)
    pad_ref[: weight_ref.shape[0]] = weight_ref[...]
    return pad_ref[...]


def right_corr_kernel(
    taps,
    radius,
    scale,
    left_ref,
    own_ref,
    disp_ref,
    edge_ref,
    weight_ref,
    mot_ref,
    pre_ref,
    pad_ref,
    mw_ref,
    side_ref,
):
    rows, _, chan = own_ref.shape
    first = pl.program_id(0) * rows
    pad_ref[...] = jnp.zeros_like(pad_ref)
    side_ref[...] = jnp.zeros_like(side_ref)
    weight = taps_matrix(weight_ref, mw_ref)
    for r in range(rows):
        side_ref[r, :HALO] = edge_ref[r].astype(F32)
        edge = side_ref[r]
        pad_ref[r, :EDGE] = edge[:, chan : 2 * chan].astype(BF16)
        side = edge[:, :chan].astype(BF16)
        scores = dot_nt(jnp.concatenate([left_ref[r], side], axis=0), own_ref[r])
        disp = down_lanes(level_row(disp_ref, first + r, B))
        main = pick_taps(scores[:B, :B], scores[:B, B:], disp, taps, radius, scale)
        disp = edge[:, 2 * chan + 2 * B :].astype(jnp.int32)
        beside = pick_taps(
            scores[B:, B:], dot_nt(side, pad_ref[r]), disp, taps, radius, scale
        )
        pre = dot(jnp.concatenate([main, beside], axis=0), weight)
        pre_ref[r] = pre[:B]
        mot_ref[r] = silu(pre).astype(BF16)


def left_corr_kernel(
    taps,
    radius,
    scale,
    start,
    rim_step,
    left_ref,
    own_ref,
    before_ref,
    extra_ref,
    disp_ref,
    mot_right_ref,
    weight_ref,
    mot_ref,
    pre_ref,
    rim_ref,
    pad_ref,
    mw_ref,
):
    rows, _, chan = own_ref.shape
    step = pl.program_id(0)
    first = start + step * rows
    pad_ref[...] = jnp.zeros_like(pad_ref)
    weight = taps_matrix(weight_ref, mw_ref)
    last = iota((EDGE, chan), 0) >= EDGE - HALO
    upper = iota((EDGE, B), 0) < EDGE // 2
    for r in range(rows):
        extra = extra_ref[r * EDGE : (r + 1) * EDGE].astype(F32)
        pad_ref[r, B - EDGE :] = jnp.where(last, pltpu.roll(extra, 12, 0), 0.0).astype(BF16)
        side = jnp.where(last, pltpu.roll(extra, 8, 0), 0.0).astype(BF16)
        window = jnp.concatenate([before_ref[r * B : (r + 1) * B], own_ref[r]], axis=0)
        scores = dot_nt(jnp.concatenate([left_ref[r], side], axis=0), window)
        disp = down_lanes(level_row(disp_ref, first + r, 0))
        main = pick_taps(scores[:B, :B], scores[:B, B:], disp, taps, radius, scale)
        disp = pltpu.roll(extra, 4, 0)[:, :B].astype(jnp.int32)
        beside = pick_taps(
            dot_nt(side, pad_ref[r]), scores[B:, :B], disp, taps, radius, scale, B - EDGE
        )
        pre = dot(jnp.concatenate([main, beside], axis=0), weight)
        pre_ref[r] = pre[:B]
        mot = silu(pre)
        mot_ref[r, :B] = mot[:B].astype(BF16)
        mot_ref[r, B : 2 * B] = mot_right_ref[r, :B]
        right_edge = mot_right_ref[r, B:].astype(F32)
        mot_ref[r, 2 * B :] = jnp.where(upper, right_edge, mot[B:]).astype(BF16)

    @pl.when(step == rim_step)
    def _():
        rim_ref[...] = mot_ref[...]


def shifted(value):
    return (
        pltpu.roll(value, 1, 0).astype(BF16),
        value.astype(BF16),
        pltpu.roll(value, value.shape[0] - 1, 0).astype(BF16),
    )


def store3(buf, row, value):
    for b, part in enumerate(shifted(value)):
        buf[row, :, b * B : (b + 1) * B] = part


def lanes(buf, rows, b):
    return jnp.concatenate([buf[r, :, b * B : (b + 1) * B] for r in rows], axis=0)


def patches(bufs, row_sets):
    return jnp.concatenate(
        [lanes(buf, rows, b) for rows in row_sets for b in range(3) for buf in bufs], axis=1
    )


def chunks(values, size):
    values = list(values)
    return [values[i : i + size] for i in range(0, len(values), size)]


CHUNK = 4


def gates_hidden_kernel(
    hid_ref,
    edge_ref,
    gate_ref,
    cand_ref,
    gh_ref,
    wgm_ref,
    wc_ref,
    wcb_ref,
    wgb_ref,
    h_ref,
    h3_ref,
    wgh_ref,
):
    rows, own, _ = hid_ref.shape
    wide = own + EDGE
    for row in range(rows):
        join_columns(h_ref, 0, hid_ref[row], edge_ref[row, :, :B])
        store3(h3_ref, row, h_ref[0].astype(F32))
    zeros = jnp.zeros((6 * B, B), BF16)
    wc_ref[18 * B :, :B] = zeros
    wc_ref[: 6 * B, B:] = zeros
    wc_ref[: 18 * B, :B] = cand_ref[...]
    wc_ref[6 * B :, B:] = cand_ref[...]
    wgb_ref[:B, 18 * B :] = jnp.zeros((B, 6 * B), BF16)
    wgb_ref[B:, : 6 * B] = jnp.zeros((B, 6 * B), BF16)
    for n in range(9):
        wgh_ref[n * B : (n + 1) * B] = gate_ref[2 * n * B : (2 * n + 1) * B]
        wgm_ref[n * B : (n + 1) * B] = gate_ref[(2 * n + 1) * B : (2 * n + 2) * B]
        at = (8 - n) * 2 * B
        wcb_ref[:, n * B : (n + 1) * B] = cand_ref[at : at + 2 * B]
        for s in range(2):
            col = (n + 3 * s) * 2 * B
            wgb_ref[s * B : (s + 1) * B, col : col + 2 * B] = gate_ref[at + B : at + 2 * B]
    for group in chunks(range(1, rows - 1), CHUNK):
        lhs = patches((h3_ref,), [[r + a - 1 for r in group] for a in range(3)])
        acc = dot(lhs, wgh_ref[...])
        for n, row in enumerate(group):
            gh_ref[row - 1] = acc[n * wide : (n + 1) * wide]


def gru_kernel(
    hid_ref,
    grad_ref,
    hgt_ref,
    hgb_ref,
    edge_ref,
    mota_ref,
    motb_ref,
    mott_ref,
    motl_ref,
    wg_ref,
    wgm_ref,
    gates_ref,
    wc_ref,
    wcb_ref,
    wgb_ref,
    prela_ref,
    prelb_ref,
    prer_ref,
    disp_ref,
    mw_ref,
    nh_ref,
    pg_ref,
    tg_ref,
    u3_ref,
    m3_ref,
    r3_ref,
    c3_ref,
    cb_ref,
    h_ref,
    g_ref,
    gh_ref,
):
    rows, own, _ = nh_ref.shape
    half = rows // 2
    wide = own + EDGE
    total = rows + 2 * HALO
    inner = range(HALO, HALO + rows)
    known = range(HALO + 1, HALO + rows - 1)
    for row in range(total):
        n = row - HALO
        if n < 0 or n >= rows:
            hg = hgt_ref[row] if n < 0 else hgb_ref[n - rows]
            mot = mott_ref[row] if n < 0 else motl_ref[n - rows]
            h_ref[row] = hg
        else:
            mot = mota_ref[n] if n < half else motb_ref[n - half]
            join_columns(h_ref, row, hid_ref[n], edge_ref[n, :, :B])
            join_columns(g_ref, row, grad_ref[n], edge_ref[n, :, B:])
        store3(m3_ref, row, mot.astype(F32))
        if row <= known[0] or row >= known[-1]:
            store3(u3_ref, row, h_ref[row].astype(F32))

    for n in range(HALO // 2):
        g_ref[HALO - HALO // 2 + n] = hgt_ref[HALO + n]
        g_ref[HALO + rows + n] = hgb_ref[HALO + n]

    def gate(row, value):
        value = jax.nn.sigmoid(value)
        gh_ref[row - 1] = value
        store3(r3_ref, row, value[:, B:] * h_ref[row].astype(F32))

    for group in (list(range(1, known[0])), list(range(known[-1] + 1, total - 1))):
        lhs = patches((u3_ref, m3_ref), [[r + a - 1 for r in group] for a in range(3)])
        acc = dot(lhs, wg_ref[...])
        for n, row in enumerate(group):
            gate(row, acc[n * wide : (n + 1) * wide])
    for group in chunks(known, CHUNK):
        lhs = patches((m3_ref,), [[r + a - 1 for r in group] for a in range(3)])
        acc = dot(lhs, wgm_ref[...])
        for n, row in enumerate(group):
            gate(row, acc[n * wide : (n + 1) * wide] + gates_ref[row - known[0]])

    for group in chunks(range(2, total - 2, 2), CHUNK):
        lhs = patches((r3_ref, m3_ref), [[r + t - 1 for r in group] for t in range(4)])
        acc = jnp.tanh(dot(lhs, wc_ref[...]))
        for n, top in enumerate(group):
            for row in (top, top + 1):
                s = row - top
                cand = acc[n * wide : (n + 1) * wide, s * B : (s + 1) * B]
                hidden = h_ref[row].astype(F32)
                update = gh_ref[row - 1, :, :B]
                if row in inner:
                    new = (1.0 - update) * hidden + update * cand
                    nh_ref[row - HALO] = new[:own].astype(BF16)
                gu = g_ref[row].astype(F32) * update
                store3(c3_ref, row, gu * (1.0 - cand * cand))
                store3(u3_ref, row, gu * (cand - hidden) * (1.0 - update))

    for group in chunks(range(3, total - 3), CHUNK):
        lhs = patches((c3_ref,), [[r + a - 1 for r in group] for a in range(3)])
        acc = dot_nt(lhs, wcb_ref[...])
        for n, row in enumerate(group):
            back = acc[n * wide : (n + 1) * wide]
            reset = gh_ref[row - 1, :, B:]
            store3(m3_ref, row, back[:, :B] * h_ref[row].astype(F32) * reset * (1.0 - reset))
            if row in inner:
                cb_ref[row - HALO] = back[:own, B:]

    for group in chunks(range(HALO, HALO + rows, 2), CHUNK):
        lhs = patches((u3_ref, m3_ref), [[r + t - 1 for r in group] for t in range(4)])
        acc = dot_nt(lhs, wgb_ref[...])
        for n, top in enumerate(group):
            for row in (top - HALO, top + 1 - HALO):
                s = row + HALO - top
                back = acc[n * wide : n * wide + own, s * B : (s + 1) * B]
                prel = prela_ref[row] if row < half else prelb_ref[row - half]
                pre = jnp.concatenate([prel, prer_ref[row]], axis=0)
                sig = jax.nn.sigmoid(pre)
                grad = (cb_ref[row] + back) * sig * (1.0 + pre * (1.0 - sig))
                grad = grad.astype(BF16)
                pg_ref[row] = grad
                tap = dot_nt(mw_ref[...], grad[:B])
                level = jnp.broadcast_to(disp_ref[row : row + 1, :B].astype(F32), tap.shape)
                tg_ref[row] = jnp.where(iota(tap.shape, 0) == 15, level, tap).astype(BF16)


def spread(grad, disp, taps, radius):
    pixel = iota((B, B), 0)
    lane = iota((B, B), 1)
    tap = ((pixel - lane) & (B - 1)) - disp + radius
    ok = (tap >= 0) & (tap < taps)
    value = jnp.where(ok, lane_gather(grad, tap & (B - 1)), 0.0)
    far = jnp.where(lane > pixel, value, 0.0).astype(BF16)
    near = jnp.where(lane > pixel, 0.0, value).astype(BF16)
    return far, near


def spread_t(grad, disp, taps, radius):
    column = iota((B, B), 0)
    pixel = iota((B, B), 1)
    tap = ((pixel - column) & (B - 1)) - disp + radius
    value = jnp.zeros((B, B), F32)
    for k in range(taps):
        value = jnp.where(tap == k, grad[k : k + 1], value)
    far = jnp.where(column > pixel, value, 0.0).astype(BF16)
    near = jnp.where(column > pixel, 0.0, value).astype(BF16)
    return far, near


def grads_kernel(
    taps,
    radius,
    scale,
    pg_ref,
    left_ref,
    own_ref,
    before_a_ref,
    before_b_ref,
    disp_ref,
    weight_ref,
    gl_ref,
    gr_ref,
    near_ref,
    mw_ref,
):
    rows = left_ref.shape[0]
    step = pl.program_id(0)
    head = step < pl.num_programs(0) // 2
    weight_t = weight_ref[...]
    weight = taps_matrix(weight_ref, mw_ref)
    for r in range(rows):
        grads = dot_nt(pg_ref[r], weight).astype(BF16).astype(F32)
        grads_t = dot_nt(weight_t, pg_ref[r]).astype(BF16).astype(F32)
        parts = []
        parts_t = []
        for block in range(2):
            at = slice(block * B, (block + 1) * B)
            row = level_row(disp_ref, step * rows + r, block * B)
            parts.append(spread(grads[at], down_lanes(row), taps, radius))
            parts_t.append(spread_t(grads_t[:, at], row, taps, radius))
        at = slice(r * B, (r + 1) * B)
        before = jnp.where(head, before_a_ref[at], before_b_ref[at])
        window = jnp.concatenate([before, own_ref[r, :B]], axis=0)
        gl_ref[r, :B] = (dot(jnp.concatenate(parts[0], axis=1), window) * scale).astype(BF16)
        gl_ref[r, B:] = (dot(jnp.concatenate(parts[1], axis=1), own_ref[r]) * scale).astype(BF16)
        sg = jnp.concatenate([parts_t[0][1], parts_t[1][0]], axis=1)
        gr_ref[r] = (dot(sg, left_ref[r]) * scale).astype(BF16)
        near_ref[r] = parts_t[1][1]


def last_kernel(taps, radius, scale, near_ref, grad_ref, left_ref, next_ref, first_ref, gr_ref):
    del first_ref
    rows = left_ref.shape[0]
    for r in range(rows):
        grad = grad_ref[r].astype(F32)
        disp = grad[15:16].astype(jnp.int32)
        far, _ = spread_t(grad, disp, taps, radius)
        sg = jnp.concatenate([near_ref[r], far], axis=1)
        window = jnp.concatenate([left_ref[r], next_ref[r]], axis=0)
        gr_ref[r] = (dot(sg, window) * scale).astype(BF16)


def whole(array):
    nd = array.ndim
    return pl.BlockSpec(array.shape, lambda i: (0,) * nd)


def by_rows(array, size, block=None, at=None):
    block = tuple(array.shape[1:]) if block is None else block
    at = (0,) * len(block) if at is None else at
    return pl.BlockSpec((size,) + block, lambda i: (i,) + at)


def cost(flops, bytes_accessed):
    return pl.CostEstimate(flops=flops, bytes_accessed=bytes_accessed, transcendentals=0)


def block(shape, *at):
    return pl.BlockSpec(shape, lambda i: (i + at[0],) + at[1:])


def per_device(
    feat_left, feat_right, hidden, disparity, motion_weight, gate_weight, cand_weight, grad_hidden
):
    rows, cols, chan = feat_left.shape
    taps = motion_weight.shape[0]
    radius = taps // 2
    scale = 1.0 / math.sqrt(chan)
    args = (taps, radius, scale)
    size = ROWS
    steps = rows // size
    half = rows // 2
    wide = cols + EDGE
    packed = 2 * chan + 3 * B
    params = pltpu.CompilerParams(vmem_limit_bytes=SMALL_VMEM)
    shape = jax.ShapeDtypeStruct
    vmem = pl.BlockSpec(memory_space=pltpu.VMEM)
    last8 = cols // 8 - 1
    pack_params = pltpu.CompilerParams(vmem_limit_bytes=PACK_VMEM)

    small_shapes = (shape((rows, HALO, packed), BF16), shape((half * B + rows * EDGE, chan), BF16))
    to_left, to_right = pl.pallas_call(
        pack_small_kernel,
        grid=(1,),
        in_specs=[
            block((rows, 8, chan), 0, 0, 0),
            block((rows, 8, chan), 0, 0, 0),
            block((rows, 8, B), 0, 0, 0),
            block((rows, 8, B), 0, 0, 0),
            block((rows, 8, chan), 0, (cols - B) // 8 - 1, 0),
            block((rows, 8, chan), 0, last8, 0),
            block((rows, 8, B), 0, last8, 0),
            block((rows, 8, B), 0, last8, 0),
            block((half, B, chan), 0, cols // B - 1, 0),
            whole(disparity),
        ],
        out_specs=[whole(s) for s in small_shapes],
        out_shape=small_shapes,
        compiler_params=pack_params,
        cost_estimate=cost(1 << 16, 1 << 18),
        name="pack_small",
    )(
        feat_left,
        feat_right,
        hidden,
        grad_hidden,
        feat_right,
        feat_left,
        hidden,
        grad_hidden,
        feat_right,
        disparity,
    )
    from_right = shift(to_left, "cols", -1)
    from_left = shift(to_right, "cols", 1)
    second, from_right = lax.optimization_barrier((feat_right[half:, cols - B :], from_right))
    mw16 = jnp.pad(motion_weight, ((0, 16 - taps), (0, 0)))
    pads = [pltpu.VMEM((size, B, chan), BF16), pltpu.VMEM((B, B), BF16)]
    right_shapes = (shape((rows, B + EDGE, B), BF16), shape((rows, B, B), F32))
    mot_right, pre_right = pl.pallas_call(
        lambda *refs: right_corr_kernel(*args, *refs),
        grid=(steps,),
        in_specs=[
            block((size, B, chan), 0, 1, 0),
            by_rows(feat_right, size),
            whole(disparity),
            by_rows(from_right, size),
            whole(mw16),
        ],
        out_specs=[by_rows(s, size) for s in right_shapes],
        out_shape=right_shapes,
        scratch_shapes=pads + [pltpu.VMEM((size, EDGE, packed), F32)],
        compiler_params=params,
        cost_estimate=cost(2 * rows * B * 2 * B * chan, 6 << 20),
        name="corr_right",
    )(feat_left, feat_right, disparity, from_right, mw16)
    from_left, mot_right = lax.optimization_barrier((from_left, mot_right))
    before = [from_left, shift(second, "cols", 1).reshape(half * B, chan)]

    rim = shape((HALO + HALO // 2, wide, B), BF16)
    edge_shape = shape((rows, EDGE, 2 * B), BF16)
    first_rim, last_rim, edge = pl.pallas_call(
        rim_kernel,
        grid=(1,),
        in_specs=[
            block((HALO, cols, B), 0, 0, 0),
            block((HALO, cols, B), 0, 0, 0),
            block((HALO, cols, B), rows // HALO - 1, 0, 0),
            block((HALO, cols, B), rows // HALO - 1, 0, 0),
            whole(from_right),
            block((rows * EDGE, chan), half * B // (rows * EDGE), 0),
        ],
        out_specs=[whole(rim), whole(rim), whole(edge_shape)],
        out_shape=(rim, rim, edge_shape),
        scratch_shapes=[pltpu.VMEM((EDGE, 2 * B), F32)],
        compiler_params=params,
        cost_estimate=cost(1 << 16, 2 << 20),
        name="rims",
    )(hidden, grad_hidden, hidden, grad_hidden, from_right, from_left)
    hg_top = shift(last_rim, "rows", 1)
    hg_low = shift(first_rim, "rows", -1)

    def left_lookup(start, before, rim_step):
        at = start // size
        shapes = (
            shape((half, wide, B), BF16),
            shape((half, B, B), F32),
            shape((HALO, wide, B), BF16),
        )
        return pl.pallas_call(
            lambda *refs: left_corr_kernel(*args, start, rim_step, *refs),
            grid=(half // size,),
            in_specs=[
                block((size, B, chan), at, 0, 0),
                block((size, B, chan), at, 0, 0),
                block((size * B, chan), 0, 0),
                block((size * EDGE, chan), half * B // (size * EDGE) + at, 0),
                whole(disparity),
                block((size, B + EDGE, B), at, 0, 0),
                whole(mw16),
            ],
            out_specs=[by_rows(s, size) for s in shapes[:2]] + [whole(shapes[2])],
            out_shape=shapes,
            scratch_shapes=pads,
            compiler_params=params,
            cost_estimate=cost(rows * B * 2 * B * chan, 3 << 20),
            name="corr_left",
        )(feat_left, feat_right, before, from_left, disparity, mot_right, mw16)

    mot_a, pre_a, rim_a = left_lookup(0, before[0], 0)
    mot_low = shift(rim_a, "rows", -1)
    before[1], mot_a = lax.optimization_barrier((before[1], mot_a))
    mot_b, pre_b, rim_b = left_lookup(half, before[1], half // size - 1)
    mot_top = shift(rim_b, "rows", 1)
    first_left, _ = lax.optimization_barrier((feat_left[:, :B], mot_b))
    next_left = shift(first_left, "cols", -1)

    total = rows + 2 * HALO
    own_shape = shape((rows, cols, B), BF16)
    gate_shape = shape((rows - 2, wide, 2 * B), F32)
    weight_shapes = [
        shape((9 * B, 2 * B), BF16),
        shape((24 * B, 2 * B), BF16),
        shape((2 * B, 9 * B), BF16),
        shape((2 * B, 24 * B), BF16),
    ]
    wg = gate_weight.reshape(-1, 2 * B)
    hid_operands = (hidden, edge, wg, cand_weight.reshape(-1, B))
    hid_shapes = (gate_shape, *weight_shapes)
    gates, wgm, wc, wcb, wgb = pl.pallas_call(
        gates_hidden_kernel,
        in_specs=[vmem] * len(hid_operands),
        out_specs=[vmem] * len(hid_shapes),
        out_shape=hid_shapes,
        scratch_shapes=[
            pltpu.VMEM((1, wide, B), BF16),
            pltpu.VMEM((rows, wide, 3 * B), BF16),
            pltpu.VMEM((9 * B, 2 * B), BF16),
        ],
        compiler_params=pltpu.CompilerParams(vmem_limit_bytes=GATES_VMEM),
        cost_estimate=cost(2 * 22 * wide * 9 * B * 2 * B, 16 << 20),
        name="gates_hidden",
    )(*hid_operands)
    operands = (
        hidden,
        grad_hidden,
        hg_top,
        hg_low,
        edge,
        mot_a,
        mot_b,
        mot_top,
        mot_low,
        wg,
        wgm,
        gates,
        wc,
        wcb,
        wgb,
        pre_a,
        pre_b,
        pre_right,
        disparity,
        mw16,
    )
    anywhere = pl.BlockSpec(memory_space=pl.ANY)
    halo_buffer = pltpu.VMEM((total, wide, B), BF16)
    new_hidden, pre_grad, tap_grad = pl.pallas_call(
        gru_kernel,
        in_specs=[vmem] * len(operands),
        out_specs=[vmem] * 3,
        out_shape=(own_shape, own_shape, shape((rows, 16, B), BF16)),
        scratch_shapes=[pltpu.VMEM((total, wide, 3 * B), BF16)] * 4
        + [pltpu.VMEM((rows, cols, B), F32), halo_buffer, halo_buffer]
        + [pltpu.VMEM((total - 2, wide, 2 * B), F32)],
        compiler_params=pltpu.CompilerParams(vmem_limit_bytes=GRU_VMEM),
        cost_estimate=cost(2 * 22 * wide * 256 * 256 * 20, 16 << 20),
        name="gru",
    )(*operands)
    next_grad = shift(tap_grad, "cols", -1)

    feat_shape = shape((rows, cols, chan), BF16)
    near_shape = shape((rows, B, B), BF16)
    mid = steps // 2
    grad_left, grad_first, near = pl.pallas_call(
        lambda *refs: grads_kernel(*args, *refs),
        grid=(steps,),
        in_specs=[
            by_rows(pre_grad, size),
            by_rows(feat_left, size),
            by_rows(feat_right, size),
            pl.BlockSpec((size * B, chan), lambda i: (jnp.minimum(i, mid - 1), 0)),
            pl.BlockSpec((size * B, chan), lambda i: (jnp.maximum(i - mid, 0), 0)),
            whole(disparity),
            whole(mw16),
        ],
        out_specs=[
            by_rows(feat_shape, size),
            block((size, B, chan), 0, 0, 0),
            by_rows(near_shape, size),
        ],
        out_shape=(feat_shape, feat_shape, near_shape),
        scratch_shapes=[pltpu.VMEM((B, B), BF16)],
        compiler_params=params,
        cost_estimate=cost(2 * rows * B * 2 * B * chan * 4, 12 << 20),
        name="grads",
    )(pre_grad, feat_left, feat_right, before[0], before[1], disparity, mw16)
    grad_right = pl.pallas_call(
        lambda *refs: last_kernel(*args, *refs),
        grid=(steps,),
        in_specs=[
            by_rows(near, size),
            by_rows(next_grad, size),
            block((size, B, chan), 0, 1, 0),
            by_rows(next_left, size),
            anywhere,
        ],
        out_specs=block((size, B, chan), 0, 1, 0),
        out_shape=feat_shape,
        input_output_aliases={4: 0},
        compiler_params=params,
        cost_estimate=cost(2 * rows * B * 2 * B * chan, 4 << 20),
        name="grad_right",
    )(near, next_grad, feat_left, next_left, grad_first)
    return (new_hidden, grad_left, grad_right)


def solution(mesh):
    grid3 = P("rows", "cols", None)
    return jax.shard_map(
        per_device,
        mesh=mesh,
        in_specs=(grid3, grid3, grid3, P("rows", "cols"), P(), P(), P(), grid3),
        out_specs=(grid3, grid3, grid3),
        check_vma=False,
    )
```

```python
import math

import jax
import jax.numpy as jnp
from jax import lax
from jax.experimental import pallas as pl
from jax.experimental.pallas import tpu as pltpu
from jax.sharding import PartitionSpec as P

B = 128
HALO = 4
EDGE = 16
F32 = jnp.float32
BF16 = jnp.bfloat16
ROWS = 4
SMALL_VMEM = 16 * 1024 * 1024
GRU_VMEM = 36 * 1024 * 1024
GATES_VMEM = 12 * 1024 * 1024
PACK_VMEM = 60 * 1024 * 1024


def shift(array, axis, by):
    size = lax.axis_size(axis)
    pairs = [(i, i + by) for i in range(size) if 0 <= i + by < size]
    return lax.ppermute(array, axis, pairs)


def dot_nt(a, b):
    return lax.dot_general(a, b, (((1,), (1,)), ((), ())), preferred_element_type=F32)


def dot(a, b):
    return jnp.dot(a, b, preferred_element_type=F32)


def iota(shape, dim):
    return lax.broadcasted_iota(jnp.int32, shape, dim)


def lane_gather(values, index):
    return jnp.take_along_axis(values, index, axis=1, mode="promise_in_bounds")


def down_lanes(row):
    return jnp.transpose(jnp.broadcast_to(row, (B, B)), (1, 0))


def pick_taps(far, near, disp, taps, radius, scale, first=0):
    count = far.shape[0]
    pixel = iota((count, B), 0) + first
    lane = iota((count, B), 1)
    merged = jnp.where(lane > pixel, far, near)
    level = disp + lane - radius
    usable = (level >= 0) & (level < B) & (lane < taps)
    picked = lane_gather(merged, (pixel - level) & (B - 1))
    return (jnp.where(usable, picked, 0.0) * scale).astype(BF16)


def silu(v):
    return v * jax.nn.sigmoid(v)


def level_columns(disp_ref, at):
    return jnp.transpose(disp_ref[:, at : at + B].astype(F32), (1, 0))


def level_row(disp_ref, row, at):
    levels = disp_ref[:, at : at + B]
    return jnp.sum(jnp.where(iota(levels.shape, 0) == row, levels, 0), axis=0, keepdims=True)


def pack_left_kernel(left_ref, own_ref, hid_ref, grad_ref, disp_ref, out_ref):
    rows, _, chan = left_ref.shape
    levels = jnp.transpose(disp_ref[:, :B].astype(F32), (1, 0))
    for r in range(rows):
        out_ref[r, :, :chan] = left_ref[r, :HALO]
        out_ref[r, :, chan : 2 * chan] = own_ref[r, :HALO]
        out_ref[r, :, 2 * chan : 2 * chan + B] = hid_ref[r, :HALO]
        out_ref[r, :, 2 * chan + B : 2 * chan + 2 * B] = grad_ref[r, :HALO]
        level = jnp.broadcast_to(levels[:8, r : r + 1], (8, B))
        out_ref[r, :, 2 * chan + 2 * B :] = level.astype(BF16)[:HALO]


def pack_right_kernel(
    beside_ref, left_last_ref, hid_last_ref, grad_last_ref, features_ref, disp_ref, last_ref
):
    rows, _, chan = beside_ref.shape
    half = features_ref.shape[0]
    last_levels = jnp.transpose(disp_ref[:, disp_ref.shape[1] - B :].astype(F32), (1, 0))
    low = iota((8, chan), 0) < HALO
    for r in range(half):
        last_ref[r * B : (r + 1) * B] = features_ref[r]
    for r in range(rows):
        beside = pltpu.roll(beside_ref[r].astype(F32), HALO, 0)
        upper = jnp.where(low, beside, left_last_ref[r].astype(F32))
        level = jnp.broadcast_to(last_levels[B - 8 :, r : r + 1], (8, chan))
        hg = jnp.concatenate([hid_last_ref[r], grad_last_ref[r]], axis=1).astype(F32)
        lower = jnp.where(low, pltpu.roll(level, HALO, 0), hg)
        at = half * B + r * EDGE
        last_ref[at : at + EDGE] = jnp.concatenate([upper, lower], axis=0).astype(BF16)


def join_columns(buf, row, own_row, edge_row):
    own = own_row.shape[0]
    buf[row, :own] = own_row
    buf[row, own:] = edge_row


def rim_kernel(
    hid_first_ref,
    grad_first_ref,
    hid_last_ref,
    grad_last_ref,
    right_ref,
    left_ref,
    first_ref,
    last_ref,
    edge_ref,
    pad_ref,
):
    rows = right_ref.shape[0]
    own = hid_first_ref.shape[1]
    chan = left_ref.shape[1]
    pad_ref[...] = jnp.zeros_like(pad_ref)
    last = iota(pad_ref.shape, 0) >= EDGE - HALO
    for r in range(rows):
        pad_ref[:HALO] = right_ref[r, :, 2 * chan : 2 * chan + 2 * B].astype(F32)
        left = left_ref[r * EDGE : (r + 1) * EDGE].astype(F32)
        edge_ref[r] = jnp.where(last, left, pad_ref[...]).astype(BF16)
    for r in range(HALO):
        join_columns(first_ref, r, hid_first_ref[r], edge_ref[r, :, :B])
        join_columns(last_ref, r, hid_last_ref[r], edge_ref[rows - HALO + r, :, :B])
    for r in range(HALO // 2):
        join_columns(first_ref, HALO + r, grad_first_ref[r], edge_ref[r, :, B:])
        row = HALO - HALO // 2 + r
        join_columns(last_ref, HALO + r, grad_last_ref[row], edge_ref[rows - HALO + row, :, B:])


def taps_matrix(weight_ref, pad_ref):
    pad_ref[...] = jnp.zeros_like(pad_ref)
    pad_ref[: weight_ref.shape[0]] = weight_ref[...]
    return pad_ref[...]


def right_corr_kernel(
    taps,
    radius,
    scale,
    left_ref,
    own_ref,
    disp_ref,
    edge_ref,
    weight_ref,
    mot_ref,
    pre_ref,
    pad_ref,
    mw_ref,
    side_ref,
):
    rows, _, chan = own_ref.shape
    first = pl.program_id(0) * rows
    pad_ref[...] = jnp.zeros_like(pad_ref)
    side_ref[...] = jnp.zeros_like(side_ref)
    weight = taps_matrix(weight_ref, mw_ref)
    for r in range(rows):
        side_ref[r, :HALO] = edge_ref[r].astype(F32)
        edge = side_ref[r]
        pad_ref[r, :EDGE] = edge[:, chan : 2 * chan].astype(BF16)
        side = edge[:, :chan].astype(BF16)
        scores = dot_nt(jnp.concatenate([left_ref[r], side], axis=0), own_ref[r])
        disp = down_lanes(level_row(disp_ref, first + r, B))
        main = pick_taps(scores[:B, :B], scores[:B, B:], disp, taps, radius, scale)
        disp = edge[:, 2 * chan + 2 * B :].astype(jnp.int32)
        beside = pick_taps(
            scores[B:, B:], dot_nt(side, pad_ref[r]), disp, taps, radius, scale
        )
        pre = dot(jnp.concatenate([main, beside], axis=0), weight)
        pre_ref[r] = pre[:B]
        mot_ref[r] = silu(pre).astype(BF16)


def left_corr_kernel(
    taps,
    radius,
    scale,
    start,
    rim_step,
    left_ref,
    own_ref,
    before_ref,
    extra_ref,
    disp_ref,
    mot_right_ref,
    weight_ref,
    mot_ref,
    pre_ref,
    rim_ref,
    pad_ref,
    mw_ref,
):
    rows, _, chan = own_ref.shape
    step = pl.program_id(0)
    first = start + step * rows
    pad_ref[...] = jnp.zeros_like(pad_ref)
    weight = taps_matrix(weight_ref, mw_ref)
    last = iota((EDGE, chan), 0) >= EDGE - HALO
    upper = iota((EDGE, B), 0) < EDGE // 2
    for r in range(rows):
        extra = extra_ref[r * EDGE : (r + 1) * EDGE].astype(F32)
        pad_ref[r, B - EDGE :] = jnp.where(last, pltpu.roll(extra, 12, 0), 0.0).astype(BF16)
        side = jnp.where(last, pltpu.roll(extra, 8, 0), 0.0).astype(BF16)
        window = jnp.concatenate([before_ref[r * B : (r + 1) * B], own_ref[r]], axis=0)
        scores = dot_nt(jnp.concatenate([left_ref[r], side], axis=0), window)
        disp = down_lanes(level_row(disp_ref, first + r, 0))
        main = pick_taps(scores[:B, :B], scores[:B, B:], disp, taps, radius, scale)
        disp = pltpu.roll(extra, 4, 0)[:, :B].astype(jnp.int32)
        beside = pick_taps(
            dot_nt(side, pad_ref[r]), scores[B:, :B], disp, taps, radius, scale, B - EDGE
        )
        pre = dot(jnp.concatenate([main, beside], axis=0), weight)
        pre_ref[r] = pre[:B]
        mot = silu(pre)
        mot_ref[r, :B] = mot[:B].astype(BF16)
        mot_ref[r, B : 2 * B] = mot_right_ref[r, :B]
        right_edge = mot_right_ref[r, B:].astype(F32)
        mot_ref[r, 2 * B :] = jnp.where(upper, right_edge, mot[B:]).astype(BF16)

    @pl.when(step == rim_step)
    def _():
        rim_ref[...] = mot_ref[...]


def shifted(value):
    return (
        pltpu.roll(value, 1, 0).astype(BF16),
        value.astype(BF16),
        pltpu.roll(value, value.shape[0] - 1, 0).astype(BF16),
    )


def store3(buf, row, value):
    for b, part in enumerate(shifted(value)):
        buf[row, :, b * B : (b + 1) * B] = part


def lanes(buf, rows, b):
    return jnp.concatenate([buf[r, :, b * B : (b + 1) * B] for r in rows], axis=0)


def patches(bufs, row_sets):
    return jnp.concatenate(
        [lanes(buf, rows, b) for rows in row_sets for b in range(3) for buf in bufs], axis=1
    )


def chunks(values, size):
    values = list(values)
    return [values[i : i + size] for i in range(0, len(values), size)]


CHUNK = 4


def gates_hidden_kernel(
    hid_ref,
    edge_ref,
    gate_ref,
    cand_ref,
    gh_ref,
    wgm_ref,
    wc_ref,
    wcb_ref,
    wgb_ref,
    h_ref,
    h3_ref,
    wgh_ref,
):
    rows, own, _ = hid_ref.shape
    wide = own + EDGE
    for row in range(rows):
        join_columns(h_ref, 0, hid_ref[row], edge_ref[row, :, :B])
        store3(h3_ref, row, h_ref[0].astype(F32))
    zeros = jnp.zeros((6 * B, B), BF16)
    wc_ref[18 * B :, :B] = zeros
    wc_ref[: 6 * B, B:] = zeros
    wc_ref[: 18 * B, :B] = cand_ref[...]
    wc_ref[6 * B :, B:] = cand_ref[...]
    wgb_ref[:B, 18 * B :] = jnp.zeros((B, 6 * B), BF16)
    wgb_ref[B:, : 6 * B] = jnp.zeros((B, 6 * B), BF16)
    for n in range(9):
        wgh_ref[n * B : (n + 1) * B] = gate_ref[2 * n * B : (2 * n + 1) * B]
        wgm_ref[n * B : (n + 1) * B] = gate_ref[(2 * n + 1) * B : (2 * n + 2) * B]
        at = (8 - n) * 2 * B
        wcb_ref[:, n * B : (n + 1) * B] = cand_ref[at : at + 2 * B]
        for s in range(2):
            col = (n + 3 * s) * 2 * B
            wgb_ref[s * B : (s + 1) * B, col : col + 2 * B] = gate_ref[at + B : at + 2 * B]
    for group in chunks(range(1, rows - 1), CHUNK):
        lhs = patches((h3_ref,), [[r + a - 1 for r in group] for a in range(3)])
        acc = dot(lhs, wgh_ref[...])
        for n, row in enumerate(group):
            gh_ref[row - 1] = acc[n * wide : (n + 1) * wide]


def gru_kernel(
    hid_ref,
    grad_ref,
    hgt_ref,
    hgb_ref,
    edge_ref,
    mota_ref,
    motb_ref,
    mott_ref,
    motl_ref,
    wg_ref,
    wgm_ref,
    gates_ref,
    wc_ref,
    wcb_ref,
    wgb_ref,
    prela_ref,
    prelb_ref,
    prer_ref,
    disp_ref,
    mw_ref,
    nh_ref,
    pg_ref,
    tg_ref,
    u3_ref,
    m3_ref,
    r3_ref,
    c3_ref,
    cb_ref,
    h_ref,
    g_ref,
    gh_ref,
):
    rows, own, _ = nh_ref.shape
    half = rows // 2
    wide = own + EDGE
    total = rows + 2 * HALO
    inner = range(HALO, HALO + rows)
    known = range(HALO + 1, HALO + rows - 1)
    for row in range(total):
        n = row - HALO
        if n < 0 or n >= rows:
            hg = hgt_ref[row] if n < 0 else hgb_ref[n - rows]
            mot = mott_ref[row] if n < 0 else motl_ref[n - rows]
            h_ref[row] = hg
        else:
            mot = mota_ref[n] if n < half else motb_ref[n - half]
            join_columns(h_ref, row, hid_ref[n], edge_ref[n, :, :B])
            join_columns(g_ref, row, grad_ref[n], edge_ref[n, :, B:])
        store3(m3_ref, row, mot.astype(F32))
        if row <= known[0] or row >= known[-1]:
            store3(u3_ref, row, h_ref[row].astype(F32))

    for n in range(HALO // 2):
        g_ref[HALO - HALO // 2 + n] = hgt_ref[HALO + n]
        g_ref[HALO + rows + n] = hgb_ref[HALO + n]

    def gate(row, value):
        value = jax.nn.sigmoid(value)
        gh_ref[row - 1] = value
        store3(r3_ref, row, value[:, B:] * h_ref[row].astype(F32))

    for group in (list(range(1, known[0])), list(range(known[-1] + 1, total - 1))):
        lhs = patches((u3_ref, m3_ref), [[r + a - 1 for r in group] for a in range(3)])
        acc = dot(lhs, wg_ref[...])
        for n, row in enumerate(group):
            gate(row, acc[n * wide : (n + 1) * wide])
    for group in chunks(known, CHUNK):
        lhs = patches((m3_ref,), [[r + a - 1 for r in group] for a in range(3)])
        acc = dot(lhs, wgm_ref[...])
        for n, row in enumerate(group):
            gate(row, acc[n * wide : (n + 1) * wide] + gates_ref[row - known[0]])

    for group in chunks(range(2, total - 2, 2), CHUNK):
        lhs = patches((r3_ref, m3_ref), [[r + t - 1 for r in group] for t in range(4)])
        acc = jnp.tanh(dot(lhs, wc_ref[...]))
        for n, top in enumerate(group):
            for row in (top, top + 1):
                s = row - top
                cand = acc[n * wide : (n + 1) * wide, s * B : (s + 1) * B]
                hidden = h_ref[row].astype(F32)
                update = gh_ref[row - 1, :, :B]
                if row in inner:
                    new = (1.0 - update) * hidden + update * cand
                    nh_ref[row - HALO] = new[:own].astype(BF16)
                gu = g_ref[row].astype(F32) * update
                store3(c3_ref, row, gu * (1.0 - cand * cand))
                store3(u3_ref, row, gu * (cand - hidden) * (1.0 - update))

    for group in chunks(range(3, total - 3), CHUNK):
        lhs = patches((c3_ref,), [[r + a - 1 for r in group] for a in range(3)])
        acc = dot_nt(lhs, wcb_ref[...])
        for n, row in enumerate(group):
            back = acc[n * wide : (n + 1) * wide]
            reset = gh_ref[row - 1, :, B:]
            store3(m3_ref, row, back[:, :B] * h_ref[row].astype(F32) * reset * (1.0 - reset))
            if row in inner:
                cb_ref[row - HALO] = back[:own, B:]

    for group in chunks(range(HALO, HALO + rows, 2), CHUNK):
        lhs = patches((u3_ref, m3_ref), [[r + t - 1 for r in group] for t in range(4)])
        acc = dot_nt(lhs, wgb_ref[...])
        for n, top in enumerate(group):
            for row in (top - HALO, top + 1 - HALO):
                s = row + HALO - top
                back = acc[n * wide : n * wide + own, s * B : (s + 1) * B]
                prel = prela_ref[row] if row < half else prelb_ref[row - half]
                pre = jnp.concatenate([prel, prer_ref[row]], axis=0)
                sig = jax.nn.sigmoid(pre)
                grad = (cb_ref[row] + back) * sig * (1.0 + pre * (1.0 - sig))
                grad = grad.astype(BF16)
                pg_ref[row] = grad
                tap = dot_nt(mw_ref[...], grad[:B])
                level = jnp.broadcast_to(disp_ref[row : row + 1, :B].astype(F32), tap.shape)
                tg_ref[row] = jnp.where(iota(tap.shape, 0) == 15, level, tap).astype(BF16)


def spread(grad, disp, taps, radius):
    pixel = iota((B, B), 0)
    lane = iota((B, B), 1)
    tap = ((pixel - lane) & (B - 1)) - disp + radius
    ok = (tap >= 0) & (tap < taps)
    value = jnp.where(ok, lane_gather(grad, tap & (B - 1)), 0.0)
    far = jnp.where(lane > pixel, value, 0.0).astype(BF16)
    near = jnp.where(lane > pixel, 0.0, value).astype(BF16)
    return far, near


def spread_t(grad, disp, taps, radius):
    column = iota((B, B), 0)
    pixel = iota((B, B), 1)
    tap = ((pixel - column) & (B - 1)) - disp + radius
    value = jnp.zeros((B, B), F32)
    for k in range(taps):
        value = jnp.where(tap == k, grad[k : k + 1], value)
    far = jnp.where(column > pixel, value, 0.0).astype(BF16)
    near = jnp.where(column > pixel, 0.0, value).astype(BF16)
    return far, near


def grads_kernel(
    taps,
    radius,
    scale,
    pg_ref,
    left_ref,
    own_ref,
    before_a_ref,
    before_b_ref,
    disp_ref,
    weight_ref,
    gl_ref,
    gr_ref,
    near_ref,
    mw_ref,
):
    rows = left_ref.shape[0]
    step = pl.program_id(0)
    head = step < pl.num_programs(0) // 2
    weight_t = weight_ref[...]
    weight = taps_matrix(weight_ref, mw_ref)
    for r in range(rows):
        grads = dot_nt(pg_ref[r], weight).astype(BF16).astype(F32)
        grads_t = dot_nt(weight_t, pg_ref[r]).astype(BF16).astype(F32)
        parts = []
        parts_t = []
        for block in range(2):
            at = slice(block * B, (block + 1) * B)
            row = level_row(disp_ref, step * rows + r, block * B)
            parts.append(spread(grads[at], down_lanes(row), taps, radius))
            parts_t.append(spread_t(grads_t[:, at], row, taps, radius))
        at = slice(r * B, (r + 1) * B)
        before = jnp.where(head, before_a_ref[at], before_b_ref[at])
        window = jnp.concatenate([before, own_ref[r, :B]], axis=0)
        gl_ref[r, :B] = (dot(jnp.concatenate(parts[0], axis=1), window) * scale).astype(BF16)
        gl_ref[r, B:] = (dot(jnp.concatenate(parts[1], axis=1), own_ref[r]) * scale).astype(BF16)
        sg = jnp.concatenate([parts_t[0][1], parts_t[1][0]], axis=1)
        gr_ref[r] = (dot(sg, left_ref[r]) * scale).astype(BF16)
        near_ref[r] = parts_t[1][1]


def last_kernel(taps, radius, scale, near_ref, grad_ref, left_ref, next_ref, first_ref, gr_ref):
    del first_ref
    rows = left_ref.shape[0]
    for r in range(rows):
        grad = grad_ref[r].astype(F32)
        disp = grad[15:16].astype(jnp.int32)
        far, _ = spread_t(grad, disp, taps, radius)
        sg = jnp.concatenate([near_ref[r], far], axis=1)
        window = jnp.concatenate([left_ref[r], next_ref[r]], axis=0)
        gr_ref[r] = (dot(sg, window) * scale).astype(BF16)


def whole(array):
    nd = array.ndim
    return pl.BlockSpec(array.shape, lambda i: (0,) * nd)


def by_rows(array, size, block=None, at=None):
    block = tuple(array.shape[1:]) if block is None else block
    at = (0,) * len(block) if at is None else at
    return pl.BlockSpec((size,) + block, lambda i: (i,) + at)


def cost(flops, bytes_accessed):
    return pl.CostEstimate(flops=flops, bytes_accessed=bytes_accessed, transcendentals=0)


def block(shape, *at):
    return pl.BlockSpec(shape, lambda i: (i + at[0],) + at[1:])


def per_device(
    feat_left, feat_right, hidden, disparity, motion_weight, gate_weight, cand_weight, grad_hidden
):
    rows, cols, chan = feat_left.shape
    taps = motion_weight.shape[0]
    radius = taps // 2
    scale = 1.0 / math.sqrt(chan)
    args = (taps, radius, scale)
    size = ROWS
    steps = rows // size
    half = rows // 2
    wide = cols + EDGE
    packed = 2 * chan + 3 * B
    params = pltpu.CompilerParams(vmem_limit_bytes=SMALL_VMEM)
    shape = jax.ShapeDtypeStruct
    vmem = pl.BlockSpec(memory_space=pltpu.VMEM)
    last8 = cols // 8 - 1
    pack_params = pltpu.CompilerParams(vmem_limit_bytes=PACK_VMEM)

    left_shape = shape((rows, HALO, packed), BF16)
    to_left = pl.pallas_call(
        pack_left_kernel,
        grid=(1,),
        in_specs=[
            block((rows, 8, chan), 0, 0, 0),
            block((rows, 8, chan), 0, 0, 0),
            block((rows, 8, B), 0, 0, 0),
            block((rows, 8, B), 0, 0, 0),
            whole(disparity),
        ],
        out_specs=whole(left_shape),
        out_shape=left_shape,
        compiler_params=pack_params,
        cost_estimate=cost(1 << 16, 1 << 18),
        name="pack_left",
    )(feat_left, feat_right, hidden, grad_hidden, disparity)
    from_right = shift(to_left, "cols", -1)
    right_shape = shape((half * B + rows * EDGE, chan), BF16)
    to_right = pl.pallas_call(
        pack_right_kernel,
        grid=(1,),
        in_specs=[
            block((rows, 8, chan), 0, (cols - B) // 8 - 1, 0),
            block((rows, 8, chan), 0, last8, 0),
            block((rows, 8, B), 0, last8, 0),
            block((rows, 8, B), 0, last8, 0),
            block((half, B, chan), 0, cols // B - 1, 0),
            whole(disparity),
        ],
        out_specs=whole(right_shape),
        out_shape=right_shape,
        compiler_params=pack_params,
        cost_estimate=cost(1 << 16, 1 << 20),
        name="pack_right",
    )(feat_right, feat_left, hidden, grad_hidden, feat_right, disparity)
    first, second, from_right = lax.optimization_barrier(
        (to_right, feat_right[half:, cols - B :], from_right)
    )
    from_left = shift(first, "cols", 1)
    second = shift(second, "cols", 1).reshape(half * B, chan)
    mw16 = jnp.pad(motion_weight, ((0, 16 - taps), (0, 0)))
    pads = [pltpu.VMEM((size, B, chan), BF16), pltpu.VMEM((B, B), BF16)]
    right_shapes = (shape((rows, B + EDGE, B), BF16), shape((rows, B, B), F32))
    mot_right, pre_right = pl.pallas_call(
        lambda *refs: right_corr_kernel(*args, *refs),
        grid=(steps,),
        in_specs=[
            block((size, B, chan), 0, 1, 0),
            by_rows(feat_right, size),
            whole(disparity),
            by_rows(from_right, size),
            whole(mw16),
        ],
        out_specs=[by_rows(s, size) for s in right_shapes],
        out_shape=right_shapes,
        scratch_shapes=pads + [pltpu.VMEM((size, EDGE, packed), F32)],
        compiler_params=params,
        cost_estimate=cost(2 * rows * B * 2 * B * chan, 6 << 20),
        name="corr_right",
    )(feat_left, feat_right, disparity, from_right, mw16)
    from_left, mot_right = lax.optimization_barrier((from_left, mot_right))
    before = [from_left, second]

    rim = shape((HALO + HALO // 2, wide, B), BF16)
    edge_shape = shape((rows, EDGE, 2 * B), BF16)
    first_rim, last_rim, edge = pl.pallas_call(
        rim_kernel,
        grid=(1,),
        in_specs=[
            block((HALO, cols, B), 0, 0, 0),
            block((HALO, cols, B), 0, 0, 0),
            block((HALO, cols, B), rows // HALO - 1, 0, 0),
            block((HALO, cols, B), rows // HALO - 1, 0, 0),
            whole(from_right),
            block((rows * EDGE, chan), half * B // (rows * EDGE), 0),
        ],
        out_specs=[whole(rim), whole(rim), whole(edge_shape)],
        out_shape=(rim, rim, edge_shape),
        scratch_shapes=[pltpu.VMEM((EDGE, 2 * B), F32)],
        compiler_params=params,
        cost_estimate=cost(1 << 16, 2 << 20),
        name="rims",
    )(hidden, grad_hidden, hidden, grad_hidden, from_right, from_left)
    hg_top = shift(last_rim, "rows", 1)
    hg_low = shift(first_rim, "rows", -1)

    def left_lookup(start, before, rim_step):
        at = start // size
        shapes = (
            shape((half, wide, B), BF16),
            shape((half, B, B), F32),
            shape((HALO, wide, B), BF16),
        )
        return pl.pallas_call(
            lambda *refs: left_corr_kernel(*args, start, rim_step, *refs),
            grid=(half // size,),
            in_specs=[
                block((size, B, chan), at, 0, 0),
                block((size, B, chan), at, 0, 0),
                block((size * B, chan), 0, 0),
                block((size * EDGE, chan), half * B // (size * EDGE) + at, 0),
                whole(disparity),
                block((size, B + EDGE, B), at, 0, 0),
                whole(mw16),
            ],
            out_specs=[by_rows(s, size) for s in shapes[:2]] + [whole(shapes[2])],
            out_shape=shapes,
            scratch_shapes=pads,
            compiler_params=params,
            cost_estimate=cost(rows * B * 2 * B * chan, 3 << 20),
            name="corr_left",
        )(feat_left, feat_right, before, from_left, disparity, mot_right, mw16)

    mot_a, pre_a, rim_a = left_lookup(0, before[0], 0)
    mot_low = shift(rim_a, "rows", -1)
    before[1], mot_a = lax.optimization_barrier((before[1], mot_a))
    mot_b, pre_b, rim_b = left_lookup(half, before[1], half // size - 1)
    mot_top = shift(rim_b, "rows", 1)
    first_left, _ = lax.optimization_barrier((feat_left[:, :B], mot_b))
    next_left = shift(first_left, "cols", -1)

    total = rows + 2 * HALO
    own_shape = shape((rows, cols, B), BF16)
    gate_shape = shape((rows - 2, wide, 2 * B), F32)
    weight_shapes = [
        shape((9 * B, 2 * B), BF16),
        shape((24 * B, 2 * B), BF16),
        shape((2 * B, 9 * B), BF16),
        shape((2 * B, 24 * B), BF16),
    ]
    wg = gate_weight.reshape(-1, 2 * B)
    hid_operands = (hidden, edge, wg, cand_weight.reshape(-1, B))
    hid_shapes = (gate_shape, *weight_shapes)
    gates, wgm, wc, wcb, wgb = pl.pallas_call(
        gates_hidden_kernel,
        in_specs=[vmem] * len(hid_operands),
        out_specs=[vmem] * len(hid_shapes),
        out_shape=hid_shapes,
        scratch_shapes=[
            pltpu.VMEM((1, wide, B), BF16),
            pltpu.VMEM((rows, wide, 3 * B), BF16),
            pltpu.VMEM((9 * B, 2 * B), BF16),
        ],
        compiler_params=pltpu.CompilerParams(vmem_limit_bytes=GATES_VMEM),
        cost_estimate=cost(2 * 22 * wide * 9 * B * 2 * B, 16 << 20),
        name="gates_hidden",
    )(*hid_operands)
    operands = (
        hidden,
        grad_hidden,
        hg_top,
        hg_low,
        edge,
        mot_a,
        mot_b,
        mot_top,
        mot_low,
        wg,
        wgm,
        gates,
        wc,
        wcb,
        wgb,
        pre_a,
        pre_b,
        pre_right,
        disparity,
        mw16,
    )
    anywhere = pl.BlockSpec(memory_space=pl.ANY)
    halo_buffer = pltpu.VMEM((total, wide, B), BF16)
    new_hidden, pre_grad, tap_grad = pl.pallas_call(
        gru_kernel,
        in_specs=[vmem] * len(operands),
        out_specs=[vmem] * 3,
        out_shape=(own_shape, own_shape, shape((rows, 16, B), BF16)),
        scratch_shapes=[pltpu.VMEM((total, wide, 3 * B), BF16)] * 4
        + [pltpu.VMEM((rows, cols, B), F32), halo_buffer, halo_buffer]
        + [pltpu.VMEM((total - 2, wide, 2 * B), F32)],
        compiler_params=pltpu.CompilerParams(vmem_limit_bytes=GRU_VMEM),
        cost_estimate=cost(2 * 22 * wide * 256 * 256 * 20, 16 << 20),
        name="gru",
    )(*operands)
    next_grad = shift(tap_grad, "cols", -1)

    feat_shape = shape((rows, cols, chan), BF16)
    near_shape = shape((rows, B, B), BF16)
    mid = steps // 2
    grad_left, grad_first, near = pl.pallas_call(
        lambda *refs: grads_kernel(*args, *refs),
        grid=(steps,),
        in_specs=[
            by_rows(pre_grad, size),
            by_rows(feat_left, size),
            by_rows(feat_right, size),
            pl.BlockSpec((size * B, chan), lambda i: (jnp.minimum(i, mid - 1), 0)),
            pl.BlockSpec((size * B, chan), lambda i: (jnp.maximum(i - mid, 0), 0)),
            whole(disparity),
            whole(mw16),
        ],
        out_specs=[
            by_rows(feat_shape, size),
            block((size, B, chan), 0, 0, 0),
            by_rows(near_shape, size),
        ],
        out_shape=(feat_shape, feat_shape, near_shape),
        scratch_shapes=[pltpu.VMEM((B, B), BF16)],
        compiler_params=params,
        cost_estimate=cost(2 * rows * B * 2 * B * chan * 4, 12 << 20),
        name="grads",
    )(pre_grad, feat_left, feat_right, before[0], before[1], disparity, mw16)
    grad_right = pl.pallas_call(
        lambda *refs: last_kernel(*args, *refs),
        grid=(steps,),
        in_specs=[
            by_rows(near, size),
            by_rows(next_grad, size),
            block((size, B, chan), 0, 1, 0),
            by_rows(next_left, size),
            anywhere,
        ],
        out_specs=block((size, B, chan), 0, 1, 0),
        out_shape=feat_shape,
        input_output_aliases={4: 0},
        compiler_params=params,
        cost_estimate=cost(2 * rows * B * 2 * B * chan, 4 << 20),
        name="grad_right",
    )(near, next_grad, feat_left, next_left, grad_first)
    return (new_hidden, grad_left, grad_right)


def solution(mesh):
    grid3 = P("rows", "cols", None)
    return jax.shard_map(
        per_device,
        mesh=mesh,
        in_specs=(grid3, grid3, grid3, P("rows", "cols"), P(), P(), P(), grid3),
        out_specs=(grid3, grid3, grid3),
        check_vma=False,
    )
```

```python
import math

import jax
import jax.numpy as jnp
from jax import lax
from jax.experimental import pallas as pl
from jax.experimental.pallas import tpu as pltpu
from jax.sharding import PartitionSpec as P

B = 128
HALO = 4
EDGE = 16
F32 = jnp.float32
BF16 = jnp.bfloat16
ROWS = 4
GRAD_ROWS = 8
SMALL_VMEM = 16 * 1024 * 1024
GRU_VMEM = 36 * 1024 * 1024
GATES_VMEM = 12 * 1024 * 1024
PACK_VMEM = 60 * 1024 * 1024


def shift(array, axis, by):
    size = lax.axis_size(axis)
    pairs = [(i, i + by) for i in range(size) if 0 <= i + by < size]
    return lax.ppermute(array, axis, pairs)


def dot_nt(a, b):
    return lax.dot_general(a, b, (((1,), (1,)), ((), ())), preferred_element_type=F32)


def dot(a, b):
    return jnp.dot(a, b, preferred_element_type=F32)


def iota(shape, dim):
    return lax.broadcasted_iota(jnp.int32, shape, dim)


def lane_gather(values, index):
    return jnp.take_along_axis(values, index, axis=1, mode="promise_in_bounds")


def down_lanes(row):
    return jnp.transpose(jnp.broadcast_to(row, (B, B)), (1, 0))


def pick_taps(far, near, disp, taps, radius, scale, first=0):
    count = far.shape[0]
    pixel = iota((count, B), 0) + first
    lane = iota((count, B), 1)
    merged = jnp.where(lane > pixel, far, near)
    level = disp + lane - radius
    usable = (level >= 0) & (level < B) & (lane < taps)
    picked = lane_gather(merged, (pixel - level) & (B - 1))
    return (jnp.where(usable, picked, 0.0) * scale).astype(BF16)


def silu(v):
    return v * jax.nn.sigmoid(v)


def level_columns(disp_ref, at):
    return jnp.transpose(disp_ref[:, at : at + B].astype(F32), (1, 0))


def level_row(disp_ref, row, at):
    levels = disp_ref[:, at : at + B]
    return jnp.sum(jnp.where(iota(levels.shape, 0) == row, levels, 0), axis=0, keepdims=True)


def pack_small_kernel(
    left_ref,
    own_ref,
    hid_ref,
    grad_ref,
    beside_ref,
    left_last_ref,
    hid_last_ref,
    grad_last_ref,
    disp_ref,
    out_ref,
    last_ref,
):
    rows, _, chan = left_ref.shape
    levels = jnp.transpose(disp_ref[:, :B].astype(F32), (1, 0))
    last_levels = jnp.transpose(disp_ref[:, disp_ref.shape[1] - B :].astype(F32), (1, 0))
    low = iota((8, chan), 0) < HALO
    for r in range(rows):
        out_ref[r, :, :chan] = left_ref[r, :HALO]
        out_ref[r, :, chan : 2 * chan] = own_ref[r, :HALO]
        out_ref[r, :, 2 * chan : 2 * chan + B] = hid_ref[r, :HALO]
        out_ref[r, :, 2 * chan + B : 2 * chan + 2 * B] = grad_ref[r, :HALO]
        level = jnp.broadcast_to(levels[:8, r : r + 1], (8, B))
        out_ref[r, :, 2 * chan + 2 * B :] = level.astype(BF16)[:HALO]
        beside = pltpu.roll(beside_ref[r].astype(F32), HALO, 0)
        upper = jnp.where(low, beside, left_last_ref[r].astype(F32))
        level = jnp.broadcast_to(last_levels[B - 8 :, r : r + 1], (8, chan))
        hg = jnp.concatenate([hid_last_ref[r], grad_last_ref[r]], axis=1).astype(F32)
        lower = jnp.where(low, pltpu.roll(level, HALO, 0), hg)
        last_ref[r] = jnp.concatenate([upper, lower], axis=0).astype(BF16)


def join_columns(buf, row, own_row, edge_row):
    own = own_row.shape[0]
    buf[row, :own] = own_row
    buf[row, own:] = edge_row


def rim_kernel(
    hid_first_ref,
    grad_first_ref,
    hid_last_ref,
    grad_last_ref,
    right_ref,
    left_ref,
    first_ref,
    last_ref,
    edge_ref,
    pad_ref,
):
    rows = right_ref.shape[0]
    chan = left_ref.shape[2]
    pad_ref[...] = jnp.zeros_like(pad_ref)
    last = iota(pad_ref.shape, 0) >= EDGE - HALO
    for r in range(rows):
        pad_ref[:HALO] = right_ref[r, :, 2 * chan : 2 * chan + 2 * B].astype(F32)
        edge_ref[r] = jnp.where(last, left_ref[r].astype(F32), pad_ref[...]).astype(BF16)
    for r in range(HALO):
        join_columns(first_ref, r, hid_first_ref[r], edge_ref[r, :, :B])
        join_columns(last_ref, r, hid_last_ref[r], edge_ref[rows - HALO + r, :, :B])
    for r in range(HALO // 2):
        join_columns(first_ref, HALO + r, grad_first_ref[r], edge_ref[r, :, B:])
        row = HALO - HALO // 2 + r
        join_columns(last_ref, HALO + r, grad_last_ref[row], edge_ref[rows - HALO + row, :, B:])


def taps_matrix(weight_ref, pad_ref):
    pad_ref[...] = jnp.zeros_like(pad_ref)
    pad_ref[: weight_ref.shape[0]] = weight_ref[...]
    return pad_ref[...]


def right_corr_kernel(
    taps,
    radius,
    scale,
    left_ref,
    own_ref,
    disp_ref,
    edge_ref,
    weight_ref,
    mot_ref,
    pre_ref,
    pad_ref,
    mw_ref,
    side_ref,
):
    rows, _, chan = own_ref.shape
    first = pl.program_id(0) * rows
    pad_ref[...] = jnp.zeros_like(pad_ref)
    side_ref[...] = jnp.zeros_like(side_ref)
    weight = taps_matrix(weight_ref, mw_ref)
    for r in range(rows):
        side_ref[r, :HALO] = edge_ref[r].astype(F32)
        edge = side_ref[r]
        pad_ref[r, :EDGE] = edge[:, chan : 2 * chan].astype(BF16)
        side = edge[:, :chan].astype(BF16)
        scores = dot_nt(jnp.concatenate([left_ref[r], side], axis=0), own_ref[r])
        disp = down_lanes(level_row(disp_ref, first + r, B))
        main = pick_taps(scores[:B, :B], scores[:B, B:], disp, taps, radius, scale)
        disp = edge[:, 2 * chan + 2 * B :].astype(jnp.int32)
        beside = pick_taps(
            scores[B:, B:], dot_nt(side, pad_ref[r]), disp, taps, radius, scale
        )
        pre = dot(jnp.concatenate([main, beside], axis=0), weight)
        pre_ref[r] = pre[:B]
        mot_ref[r] = silu(pre).astype(BF16)


def left_corr_kernel(
    taps,
    radius,
    scale,
    start,
    rim_step,
    left_ref,
    own_ref,
    before_ref,
    extra_ref,
    disp_ref,
    mot_right_ref,
    weight_ref,
    mot_ref,
    pre_ref,
    rim_ref,
    pad_ref,
    mw_ref,
):
    rows, _, chan = own_ref.shape
    step = pl.program_id(0)
    first = start + step * rows
    pad_ref[...] = jnp.zeros_like(pad_ref)
    weight = taps_matrix(weight_ref, mw_ref)
    last = iota((EDGE, chan), 0) >= EDGE - HALO
    upper = iota((EDGE, B), 0) < EDGE // 2
    for r in range(rows):
        extra = extra_ref[r].astype(F32)
        pad_ref[r, B - EDGE :] = jnp.where(last, pltpu.roll(extra, 12, 0), 0.0).astype(BF16)
        side = jnp.where(last, pltpu.roll(extra, 8, 0), 0.0).astype(BF16)
        window = jnp.concatenate([before_ref[r], own_ref[r]], axis=0)
        scores = dot_nt(jnp.concatenate([left_ref[r], side], axis=0), window)
        disp = down_lanes(level_row(disp_ref, first + r, 0))
        main = pick_taps(scores[:B, :B], scores[:B, B:], disp, taps, radius, scale)
        disp = pltpu.roll(extra, 4, 0)[:, :B].astype(jnp.int32)
        beside = pick_taps(
            dot_nt(side, pad_ref[r]), scores[B:, :B], disp, taps, radius, scale, B - EDGE
        )
        pre = dot(jnp.concatenate([main, beside], axis=0), weight)
        pre_ref[r] = pre[:B]
        mot = silu(pre)
        mot_ref[r, :B] = mot[:B].astype(BF16)
        mot_ref[r, B : 2 * B] = mot_right_ref[r, :B]
        right_edge = mot_right_ref[r, B:].astype(F32)
        mot_ref[r, 2 * B :] = jnp.where(upper, right_edge, mot[B:]).astype(BF16)

    @pl.when(step == rim_step)
    def _():
        rim_ref[...] = mot_ref[...]


def shifted(value):
    return (
        pltpu.roll(value, 1, 0).astype(BF16),
        value.astype(BF16),
        pltpu.roll(value, value.shape[0] - 1, 0).astype(BF16),
    )


def store3(buf, row, value):
    for b, part in enumerate(shifted(value)):
        buf[row, :, b * B : (b + 1) * B] = part


def lanes(buf, rows, b):
    return jnp.concatenate([buf[r, :, b * B : (b + 1) * B] for r in rows], axis=0)


def patches(bufs, row_sets):
    return jnp.concatenate(
        [lanes(buf, rows, b) for rows in row_sets for b in range(3) for buf in bufs], axis=1
    )


def chunks(values, size):
    values = list(values)
    return [values[i : i + size] for i in range(0, len(values), size)]


CHUNK = 4


def gates_hidden_kernel(
    hid_ref,
    edge_ref,
    gate_ref,
    cand_ref,
    gh_ref,
    wgm_ref,
    wc_ref,
    wcb_ref,
    wgb_ref,
    h_ref,
    h3_ref,
    wgh_ref,
):
    rows, own, _ = hid_ref.shape
    wide = own + EDGE
    for row in range(rows):
        join_columns(h_ref, 0, hid_ref[row], edge_ref[row, :, :B])
        store3(h3_ref, row, h_ref[0].astype(F32))
    zeros = jnp.zeros((6 * B, B), BF16)
    wc_ref[18 * B :, :B] = zeros
    wc_ref[: 6 * B, B:] = zeros
    wc_ref[: 18 * B, :B] = cand_ref[...]
    wc_ref[6 * B :, B:] = cand_ref[...]
    wgb_ref[:B, 18 * B :] = jnp.zeros((B, 6 * B), BF16)
    wgb_ref[B:, : 6 * B] = jnp.zeros((B, 6 * B), BF16)
    for n in range(9):
        wgh_ref[n * B : (n + 1) * B] = gate_ref[2 * n * B : (2 * n + 1) * B]
        wgm_ref[n * B : (n + 1) * B] = gate_ref[(2 * n + 1) * B : (2 * n + 2) * B]
        at = (8 - n) * 2 * B
        wcb_ref[:, n * B : (n + 1) * B] = cand_ref[at : at + 2 * B]
        for s in range(2):
            col = (n + 3 * s) * 2 * B
            wgb_ref[s * B : (s + 1) * B, col : col + 2 * B] = gate_ref[at + B : at + 2 * B]
    for group in chunks(range(1, rows - 1), CHUNK):
        lhs = patches((h3_ref,), [[r + a - 1 for r in group] for a in range(3)])
        acc = dot(lhs, wgh_ref[...])
        for n, row in enumerate(group):
            gh_ref[row - 1] = acc[n * wide : (n + 1) * wide]


def gru_kernel(
    hid_ref,
    grad_ref,
    hgt_ref,
    hgb_ref,
    edge_ref,
    mota_ref,
    motb_ref,
    mott_ref,
    motl_ref,
    wg_ref,
    wgm_ref,
    gates_ref,
    wc_ref,
    wcb_ref,
    wgb_ref,
    prela_ref,
    prelb_ref,
    prer_ref,
    disp_ref,
    mw_ref,
    nh_ref,
    pg_ref,
    tg_ref,
    u3_ref,
    m3_ref,
    r3_ref,
    c3_ref,
    cb_ref,
    h_ref,
    g_ref,
    gh_ref,
):
    rows, own, _ = nh_ref.shape
    half = rows // 2
    wide = own + EDGE
    total = rows + 2 * HALO
    inner = range(HALO, HALO + rows)
    known = range(HALO + 1, HALO + rows - 1)
    for row in range(total):
        n = row - HALO
        if n < 0 or n >= rows:
            hg = hgt_ref[row] if n < 0 else hgb_ref[n - rows]
            mot = mott_ref[row] if n < 0 else motl_ref[n - rows]
            h_ref[row] = hg
        else:
            mot = mota_ref[n] if n < half else motb_ref[n - half]
            join_columns(h_ref, row, hid_ref[n], edge_ref[n, :, :B])
            join_columns(g_ref, row, grad_ref[n], edge_ref[n, :, B:])
        store3(m3_ref, row, mot.astype(F32))
        if row <= known[0] or row >= known[-1]:
            store3(u3_ref, row, h_ref[row].astype(F32))

    for n in range(HALO // 2):
        g_ref[HALO - HALO // 2 + n] = hgt_ref[HALO + n]
        g_ref[HALO + rows + n] = hgb_ref[HALO + n]

    def gate(row, value):
        value = jax.nn.sigmoid(value)
        gh_ref[row - 1] = value
        store3(r3_ref, row, value[:, B:] * h_ref[row].astype(F32))

    for group in (list(range(1, known[0])), list(range(known[-1] + 1, total - 1))):
        lhs = patches((u3_ref, m3_ref), [[r + a - 1 for r in group] for a in range(3)])
        acc = dot(lhs, wg_ref[...])
        for n, row in enumerate(group):
            gate(row, acc[n * wide : (n + 1) * wide])
    for group in chunks(known, CHUNK):
        lhs = patches((m3_ref,), [[r + a - 1 for r in group] for a in range(3)])
        acc = dot(lhs, wgm_ref[...])
        for n, row in enumerate(group):
            gate(row, acc[n * wide : (n + 1) * wide] + gates_ref[row - known[0]])

    for group in chunks(range(2, total - 2, 2), CHUNK):
        lhs = patches((r3_ref, m3_ref), [[r + t - 1 for r in group] for t in range(4)])
        acc = jnp.tanh(dot(lhs, wc_ref[...]))
        for n, top in enumerate(group):
            for row in (top, top + 1):
                s = row - top
                cand = acc[n * wide : (n + 1) * wide, s * B : (s + 1) * B]
                hidden = h_ref[row].astype(F32)
                update = gh_ref[row - 1, :, :B]
                if row in inner:
                    new = (1.0 - update) * hidden + update * cand
                    nh_ref[row - HALO] = new[:own].astype(BF16)
                gu = g_ref[row].astype(F32) * update
                store3(c3_ref, row, gu * (1.0 - cand * cand))
                store3(u3_ref, row, gu * (cand - hidden) * (1.0 - update))

    for group in chunks(range(3, total - 3), CHUNK):
        lhs = patches((c3_ref,), [[r + a - 1 for r in group] for a in range(3)])
        acc = dot_nt(lhs, wcb_ref[...])
        for n, row in enumerate(group):
            back = acc[n * wide : (n + 1) * wide]
            reset = gh_ref[row - 1, :, B:]
            store3(m3_ref, row, back[:, :B] * h_ref[row].astype(F32) * reset * (1.0 - reset))
            if row in inner:
                cb_ref[row - HALO] = back[:own, B:]

    for group in chunks(range(HALO, HALO + rows, 2), CHUNK):
        lhs = patches((u3_ref, m3_ref), [[r + t - 1 for r in group] for t in range(4)])
        acc = dot_nt(lhs, wgb_ref[...])
        for n, top in enumerate(group):
            for row in (top - HALO, top + 1 - HALO):
                s = row + HALO - top
                back = acc[n * wide : n * wide + own, s * B : (s + 1) * B]
                prel = prela_ref[row] if row < half else prelb_ref[row - half]
                pre = jnp.concatenate([prel, prer_ref[row]], axis=0)
                sig = jax.nn.sigmoid(pre)
                grad = (cb_ref[row] + back) * sig * (1.0 + pre * (1.0 - sig))
                grad = grad.astype(BF16)
                pg_ref[row] = grad
                tap = dot_nt(mw_ref[...], grad[:B])
                level = jnp.broadcast_to(disp_ref[row : row + 1, :B].astype(F32), tap.shape)
                tg_ref[row] = jnp.where(iota(tap.shape, 0) == 15, level, tap).astype(BF16)


def spread(grad, disp, taps, radius):
    pixel = iota((B, B), 0)
    lane = iota((B, B), 1)
    tap = ((pixel - lane) & (B - 1)) - disp + radius
    ok = (tap >= 0) & (tap < taps)
    value = jnp.where(ok, lane_gather(grad, tap & (B - 1)), 0.0)
    far = jnp.where(lane > pixel, value, 0.0).astype(BF16)
    near = jnp.where(lane > pixel, 0.0, value).astype(BF16)
    return far, near


def spread_t(grad, disp, taps, radius):
    column = iota((B, B), 0)
    pixel = iota((B, B), 1)
    tap = ((pixel - column) & (B - 1)) - disp + radius
    value = jnp.zeros((B, B), F32)
    for k in range(taps):
        value = jnp.where(tap == k, grad[k : k + 1], value)
    far = jnp.where(column > pixel, value, 0.0).astype(BF16)
    near = jnp.where(column > pixel, 0.0, value).astype(BF16)
    return far, near


def grads_kernel(
    taps,
    radius,
    scale,
    pg_ref,
    left_ref,
    own_ref,
    before_a_ref,
    before_b_ref,
    disp_ref,
    weight_ref,
    gl_ref,
    gr_ref,
    near_ref,
    mw_ref,
):
    rows = left_ref.shape[0]
    step = pl.program_id(0)
    head = step < pl.num_programs(0) // 2
    weight_t = weight_ref[...]
    weight = taps_matrix(weight_ref, mw_ref)
    for r in range(rows):
        grads = dot_nt(pg_ref[r], weight).astype(BF16).astype(F32)
        grads_t = dot_nt(weight_t, pg_ref[r]).astype(BF16).astype(F32)
        parts = []
        parts_t = []
        for block in range(2):
            at = slice(block * B, (block + 1) * B)
            row = level_row(disp_ref, step * rows + r, block * B)
            parts.append(spread(grads[at], down_lanes(row), taps, radius))
            parts_t.append(spread_t(grads_t[:, at], row, taps, radius))
        before = jnp.where(head, before_a_ref[r], before_b_ref[r])
        window = jnp.concatenate([before, own_ref[r, :B]], axis=0)
        gl_ref[r, :B] = (dot(jnp.concatenate(parts[0], axis=1), window) * scale).astype(BF16)
        gl_ref[r, B:] = (dot(jnp.concatenate(parts[1], axis=1), own_ref[r]) * scale).astype(BF16)
        sg = jnp.concatenate([parts_t[0][1], parts_t[1][0]], axis=1)
        gr_ref[r] = (dot(sg, left_ref[r]) * scale).astype(BF16)
        near_ref[r] = parts_t[1][1]


def last_kernel(taps, radius, scale, near_ref, grad_ref, left_ref, next_ref, first_ref, gr_ref):
    del first_ref
    rows = left_ref.shape[0]
    for r in range(rows):
        grad = grad_ref[r].astype(F32)
        disp = grad[15:16].astype(jnp.int32)
        far, _ = spread_t(grad, disp, taps, radius)
        sg = jnp.concatenate([near_ref[r], far], axis=1)
        window = jnp.concatenate([left_ref[r], next_ref[r]], axis=0)
        gr_ref[r] = (dot(sg, window) * scale).astype(BF16)


def whole(array):
    nd = array.ndim
    return pl.BlockSpec(array.shape, lambda i: (0,) * nd)


def by_rows(array, size, block=None, at=None):
    block = tuple(array.shape[1:]) if block is None else block
    at = (0,) * len(block) if at is None else at
    return pl.BlockSpec((size,) + block, lambda i: (i,) + at)


def cost(flops, bytes_accessed):
    return pl.CostEstimate(flops=flops, bytes_accessed=bytes_accessed, transcendentals=0)


def block(shape, *at):
    return pl.BlockSpec(shape, lambda i: (i + at[0],) + at[1:])


def per_device(
    feat_left, feat_right, hidden, disparity, motion_weight, gate_weight, cand_weight, grad_hidden
):
    rows, cols, chan = feat_left.shape
    taps = motion_weight.shape[0]
    radius = taps // 2
    scale = 1.0 / math.sqrt(chan)
    args = (taps, radius, scale)
    size = ROWS
    steps = rows // size
    half = rows // 2
    wide = cols + EDGE
    packed = 2 * chan + 3 * B
    params = pltpu.CompilerParams(vmem_limit_bytes=SMALL_VMEM)
    shape = jax.ShapeDtypeStruct
    vmem = pl.BlockSpec(memory_space=pltpu.VMEM)
    last8 = cols // 8 - 1
    pack_params = pltpu.CompilerParams(vmem_limit_bytes=PACK_VMEM)

    small_shapes = (shape((rows, HALO, packed), BF16), shape((rows, EDGE, chan), BF16))
    to_left, to_right = pl.pallas_call(
        pack_small_kernel,
        grid=(1,),
        in_specs=[
            block((rows, 8, chan), 0, 0, 0),
            block((rows, 8, chan), 0, 0, 0),
            block((rows, 8, B), 0, 0, 0),
            block((rows, 8, B), 0, 0, 0),
            block((rows, 8, chan), 0, (cols - B) // 8 - 1, 0),
            block((rows, 8, chan), 0, last8, 0),
            block((rows, 8, B), 0, last8, 0),
            block((rows, 8, B), 0, last8, 0),
            whole(disparity),
        ],
        out_specs=[whole(s) for s in small_shapes],
        out_shape=small_shapes,
        compiler_params=pack_params,
        cost_estimate=cost(1 << 16, 1 << 18),
        name="pack_small",
    )(
        feat_left,
        feat_right,
        hidden,
        grad_hidden,
        feat_right,
        feat_left,
        hidden,
        grad_hidden,
        disparity,
    )
    from_right = shift(to_left, "cols", -1)
    from_left = shift(to_right, "cols", 1)
    features = feat_right[:, cols - B :]
    second, from_right, from_left = lax.optimization_barrier(
        (features[half:], from_right, from_left)
    )
    before = [shift(features[:half], "cols", 1), shift(second, "cols", 1)]

    rim = shape((HALO + HALO // 2, wide, B), BF16)
    edge_shape = shape((rows, EDGE, 2 * B), BF16)
    first_rim, last_rim, edge = pl.pallas_call(
        rim_kernel,
        grid=(1,),
        in_specs=[
            block((HALO, cols, B), 0, 0, 0),
            block((HALO, cols, B), 0, 0, 0),
            block((HALO, cols, B), rows // HALO - 1, 0, 0),
            block((HALO, cols, B), rows // HALO - 1, 0, 0),
            whole(from_right),
            whole(from_left),
        ],
        out_specs=[whole(rim), whole(rim), whole(edge_shape)],
        out_shape=(rim, rim, edge_shape),
        scratch_shapes=[pltpu.VMEM((EDGE, 2 * B), F32)],
        compiler_params=params,
        cost_estimate=cost(1 << 16, 2 << 20),
        name="rims",
    )(hidden, grad_hidden, hidden, grad_hidden, from_right, from_left)
    hg_top = shift(last_rim, "rows", 1)
    hg_low = shift(first_rim, "rows", -1)

    mw16 = jnp.pad(motion_weight, ((0, 16 - taps), (0, 0)))
    pads = [pltpu.VMEM((size, B, chan), BF16), pltpu.VMEM((B, B), BF16)]
    right_shapes = (shape((rows, B + EDGE, B), BF16), shape((rows, B, B), F32))
    mot_right, pre_right = pl.pallas_call(
        lambda *refs: right_corr_kernel(*args, *refs),
        grid=(steps,),
        in_specs=[
            block((size, B, chan), 0, 1, 0),
            by_rows(feat_right, size),
            whole(disparity),
            by_rows(from_right, size),
            whole(mw16),
        ],
        out_specs=[by_rows(s, size) for s in right_shapes],
        out_shape=right_shapes,
        scratch_shapes=pads + [pltpu.VMEM((size, EDGE, packed), F32)],
        compiler_params=params,
        cost_estimate=cost(2 * rows * B * 2 * B * chan, 6 << 20),
        name="corr_right",
    )(feat_left, feat_right, disparity, from_right, mw16)

    def left_lookup(start, before, rim_step):
        at = start // size
        shapes = (
            shape((half, wide, B), BF16),
            shape((half, B, B), F32),
            shape((HALO, wide, B), BF16),
        )
        return pl.pallas_call(
            lambda *refs: left_corr_kernel(*args, start, rim_step, *refs),
            grid=(half // size,),
            in_specs=[
                block((size, B, chan), at, 0, 0),
                block((size, B, chan), at, 0, 0),
                by_rows(before, size),
                block((size, EDGE, chan), at, 0, 0),
                whole(disparity),
                block((size, B + EDGE, B), at, 0, 0),
                whole(mw16),
            ],
            out_specs=[by_rows(s, size) for s in shapes[:2]] + [whole(shapes[2])],
            out_shape=shapes,
            scratch_shapes=pads,
            compiler_params=params,
            cost_estimate=cost(rows * B * 2 * B * chan, 3 << 20),
            name="corr_left",
        )(feat_left, feat_right, before, from_left, disparity, mot_right, mw16)

    mot_a, pre_a, rim_a = left_lookup(0, before[0], 0)
    mot_low = shift(rim_a, "rows", -1)
    mot_b, pre_b, rim_b = left_lookup(half, before[1], half // size - 1)
    mot_top = shift(rim_b, "rows", 1)
    first_left, _ = lax.optimization_barrier((feat_left[:, :B], mot_b))
    next_left = shift(first_left, "cols", -1)

    total = rows + 2 * HALO
    own_shape = shape((rows, cols, B), BF16)
    gate_shape = shape((rows - 2, wide, 2 * B), F32)
    weight_shapes = [
        shape((9 * B, 2 * B), BF16),
        shape((24 * B, 2 * B), BF16),
        shape((2 * B, 9 * B), BF16),
        shape((2 * B, 24 * B), BF16),
    ]
    wg = gate_weight.reshape(-1, 2 * B)
    hid_operands = (hidden, edge, wg, cand_weight.reshape(-1, B))
    hid_shapes = (gate_shape, *weight_shapes)
    gates, wgm, wc, wcb, wgb = pl.pallas_call(
        gates_hidden_kernel,
        in_specs=[vmem] * len(hid_operands),
        out_specs=[vmem] * len(hid_shapes),
        out_shape=hid_shapes,
        scratch_shapes=[
            pltpu.VMEM((1, wide, B), BF16),
            pltpu.VMEM((rows, wide, 3 * B), BF16),
            pltpu.VMEM((9 * B, 2 * B), BF16),
        ],
        compiler_params=pltpu.CompilerParams(vmem_limit_bytes=GATES_VMEM),
        cost_estimate=cost(2 * 22 * wide * 9 * B * 2 * B, 16 << 20),
        name="gates_hidden",
    )(*hid_operands)
    operands = (
        hidden,
        grad_hidden,
        hg_top,
        hg_low,
        edge,
        mot_a,
        mot_b,
        mot_top,
        mot_low,
        wg,
        wgm,
        gates,
        wc,
        wcb,
        wgb,
        pre_a,
        pre_b,
        pre_right,
        disparity,
        mw16,
    )
    anywhere = pl.BlockSpec(memory_space=pl.ANY)
    halo_buffer = pltpu.VMEM((total, wide, B), BF16)
    new_hidden, pre_grad, tap_grad = pl.pallas_call(
        gru_kernel,
        in_specs=[vmem] * len(operands),
        out_specs=[vmem] * 3,
        out_shape=(own_shape, own_shape, shape((rows, 16, B), BF16)),
        scratch_shapes=[pltpu.VMEM((total, wide, 3 * B), BF16)] * 4
        + [pltpu.VMEM((rows, cols, B), F32), halo_buffer, halo_buffer]
        + [pltpu.VMEM((total - 2, wide, 2 * B), F32)],
        compiler_params=pltpu.CompilerParams(vmem_limit_bytes=GRU_VMEM),
        cost_estimate=cost(2 * 22 * wide * 256 * 256 * 20, 16 << 20),
        name="gru",
    )(*operands)
    next_grad = shift(tap_grad, "cols", -1)

    gsize = GRAD_ROWS
    gsteps = rows // gsize
    feat_shape = shape((rows, cols, chan), BF16)
    near_shape = shape((rows, B, B), BF16)
    mid = gsteps // 2
    grad_left, grad_first, near = pl.pallas_call(
        lambda *refs: grads_kernel(*args, *refs),
        grid=(gsteps,),
        in_specs=[
            by_rows(pre_grad, gsize),
            by_rows(feat_left, gsize),
            by_rows(feat_right, gsize),
            pl.BlockSpec((gsize, B, chan), lambda i: (jnp.minimum(i, mid - 1), 0, 0)),
            pl.BlockSpec((gsize, B, chan), lambda i: (jnp.maximum(i - mid, 0), 0, 0)),
            whole(disparity),
            whole(mw16),
        ],
        out_specs=[
            by_rows(feat_shape, gsize),
            block((gsize, B, chan), 0, 0, 0),
            by_rows(near_shape, gsize),
        ],
        out_shape=(feat_shape, feat_shape, near_shape),
        scratch_shapes=[pltpu.VMEM((B, B), BF16)],
        compiler_params=params,
        cost_estimate=cost(2 * rows * B * 2 * B * chan * 4, 12 << 20),
        name="grads",
    )(pre_grad, feat_left, feat_right, before[0], before[1], disparity, mw16)
    grad_right = pl.pallas_call(
        lambda *refs: last_kernel(*args, *refs),
        grid=(gsteps,),
        in_specs=[
            by_rows(near, gsize),
            by_rows(next_grad, gsize),
            block((gsize, B, chan), 0, 1, 0),
            by_rows(next_left, gsize),
            anywhere,
        ],
        out_specs=block((gsize, B, chan), 0, 1, 0),
        out_shape=feat_shape,
        input_output_aliases={4: 0},
        compiler_params=params,
        cost_estimate=cost(2 * rows * B * 2 * B * chan, 4 << 20),
        name="grad_right",
    )(near, next_grad, feat_left, next_left, grad_first)
    return (new_hidden, grad_left, grad_right)


def solution(mesh):
    grid3 = P("rows", "cols", None)
    return jax.shard_map(
        per_device,
        mesh=mesh,
        in_specs=(grid3, grid3, grid3, P("rows", "cols"), P(), P(), P(), grid3),
        out_specs=(grid3, grid3, grid3),
        check_vma=False,
    )
```

```python
import math

import jax
import jax.numpy as jnp
from jax import lax
from jax.experimental import pallas as pl
from jax.experimental.pallas import tpu as pltpu
from jax.sharding import PartitionSpec as P

B = 128
HALO = 4
EDGE = 16
F32 = jnp.float32
BF16 = jnp.bfloat16
ROWS = 4
GRAD_ROWS = 8
SMALL_VMEM = 16 * 1024 * 1024
GRU_VMEM = 36 * 1024 * 1024
GATES_VMEM = 12 * 1024 * 1024
PACK_VMEM = 60 * 1024 * 1024


def shift(array, axis, by):
    size = lax.axis_size(axis)
    pairs = [(i, i + by) for i in range(size) if 0 <= i + by < size]
    return lax.ppermute(array, axis, pairs)


def dot_nt(a, b):
    return lax.dot_general(a, b, (((1,), (1,)), ((), ())), preferred_element_type=F32)


def dot(a, b):
    return jnp.dot(a, b, preferred_element_type=F32)


def iota(shape, dim):
    return lax.broadcasted_iota(jnp.int32, shape, dim)


def lane_gather(values, index):
    return jnp.take_along_axis(values, index, axis=1, mode="promise_in_bounds")


def down_lanes(row):
    return jnp.transpose(jnp.broadcast_to(row, (B, B)), (1, 0))


def pick_taps(far, near, disp, taps, radius, scale, first=0):
    count = far.shape[0]
    pixel = iota((count, B), 0) + first
    lane = iota((count, B), 1)
    merged = jnp.where(lane > pixel, far, near)
    level = disp + lane - radius
    usable = (level >= 0) & (level < B) & (lane < taps)
    picked = lane_gather(merged, (pixel - level) & (B - 1))
    return (jnp.where(usable, picked, 0.0) * scale).astype(BF16)


def silu(v):
    return v * jax.nn.sigmoid(v)


def level_columns(disp_ref, at):
    return jnp.transpose(disp_ref[:, at : at + B].astype(F32), (1, 0))


def level_row(disp_ref, row, at):
    levels = disp_ref[:, at : at + B]
    return jnp.sum(jnp.where(iota(levels.shape, 0) == row, levels, 0), axis=0, keepdims=True)


def pack_small_kernel(
    left_ref,
    own_ref,
    hid_ref,
    grad_ref,
    beside_ref,
    left_last_ref,
    hid_last_ref,
    grad_last_ref,
    disp_ref,
    out_ref,
    last_ref,
):
    rows, _, chan = left_ref.shape
    levels = jnp.transpose(disp_ref[:, :B].astype(F32), (1, 0))
    last_levels = jnp.transpose(disp_ref[:, disp_ref.shape[1] - B :].astype(F32), (1, 0))
    low = iota((8, chan), 0) < HALO
    for r in range(rows):
        out_ref[r, :, :chan] = left_ref[r, :HALO]
        out_ref[r, :, chan : 2 * chan] = own_ref[r, :HALO]
        out_ref[r, :, 2 * chan : 2 * chan + B] = hid_ref[r, :HALO]
        out_ref[r, :, 2 * chan + B : 2 * chan + 2 * B] = grad_ref[r, :HALO]
        level = jnp.broadcast_to(levels[:8, r : r + 1], (8, B))
        out_ref[r, :, 2 * chan + 2 * B :] = level.astype(BF16)[:HALO]
        beside = pltpu.roll(beside_ref[r].astype(F32), HALO, 0)
        upper = jnp.where(low, beside, left_last_ref[r].astype(F32))
        level = jnp.broadcast_to(last_levels[B - 8 :, r : r + 1], (8, chan))
        hg = jnp.concatenate([hid_last_ref[r], grad_last_ref[r]], axis=1).astype(F32)
        lower = jnp.where(low, pltpu.roll(level, HALO, 0), hg)
        last_ref[r] = jnp.concatenate([upper, lower], axis=0).astype(BF16)


def join_columns(buf, row, own_row, edge_row):
    own = own_row.shape[0]
    buf[row, :own] = own_row
    buf[row, own:] = edge_row


def rim_kernel(
    hid_first_ref,
    grad_first_ref,
    hid_last_ref,
    grad_last_ref,
    right_ref,
    left_ref,
    first_ref,
    last_ref,
    edge_ref,
    pad_ref,
):
    rows = right_ref.shape[0]
    chan = left_ref.shape[2]
    pad_ref[...] = jnp.zeros_like(pad_ref)
    last = iota(pad_ref.shape, 0) >= EDGE - HALO
    for r in range(rows):
        pad_ref[:HALO] = right_ref[r, :, 2 * chan : 2 * chan + 2 * B].astype(F32)
        edge_ref[r] = jnp.where(last, left_ref[r].astype(F32), pad_ref[...]).astype(BF16)
    for r in range(HALO):
        join_columns(first_ref, r, hid_first_ref[r], edge_ref[r, :, :B])
        join_columns(last_ref, r, hid_last_ref[r], edge_ref[rows - HALO + r, :, :B])
    for r in range(HALO // 2):
        join_columns(first_ref, HALO + r, grad_first_ref[r], edge_ref[r, :, B:])
        row = HALO - HALO // 2 + r
        join_columns(last_ref, HALO + r, grad_last_ref[row], edge_ref[rows - HALO + row, :, B:])


def taps_matrix(weight_ref, pad_ref):
    pad_ref[...] = jnp.zeros_like(pad_ref)
    pad_ref[: weight_ref.shape[0]] = weight_ref[...]
    return pad_ref[...]


def right_corr_kernel(
    taps,
    radius,
    scale,
    left_ref,
    own_ref,
    disp_ref,
    edge_ref,
    weight_ref,
    mot_ref,
    pre_ref,
    pad_ref,
    mw_ref,
    side_ref,
):
    rows, _, chan = own_ref.shape
    first = pl.program_id(0) * rows
    pad_ref[...] = jnp.zeros_like(pad_ref)
    side_ref[...] = jnp.zeros_like(side_ref)
    weight = taps_matrix(weight_ref, mw_ref)
    for r in range(rows):
        side_ref[r, :HALO] = edge_ref[r].astype(F32)
        edge = side_ref[r]
        pad_ref[r, :EDGE] = edge[:, chan : 2 * chan].astype(BF16)
        side = edge[:, :chan].astype(BF16)
        scores = dot_nt(jnp.concatenate([left_ref[r], side], axis=0), own_ref[r])
        disp = down_lanes(level_row(disp_ref, first + r, B))
        main = pick_taps(scores[:B, :B], scores[:B, B:], disp, taps, radius, scale)
        disp = edge[:, 2 * chan + 2 * B :].astype(jnp.int32)
        beside = pick_taps(
            scores[B:, B:], dot_nt(side, pad_ref[r]), disp, taps, radius, scale
        )
        pre = dot(jnp.concatenate([main, beside], axis=0), weight)
        pre_ref[r] = pre[:B]
        mot_ref[r] = silu(pre).astype(BF16)


def left_corr_kernel(
    taps,
    radius,
    scale,
    start,
    rim_at,
    left_ref,
    own_ref,
    before_ref,
    extra_ref,
    disp_ref,
    mot_right_ref,
    weight_ref,
    mot_ref,
    pre_ref,
    rim_ref,
    pad_ref,
    mw_ref,
):
    rows, _, chan = own_ref.shape
    first = start
    pad_ref[...] = jnp.zeros_like(pad_ref)
    weight = taps_matrix(weight_ref, mw_ref)
    last = iota((EDGE, chan), 0) >= EDGE - HALO
    upper = iota((EDGE, B), 0) < EDGE // 2
    for r in range(rows):
        extra = extra_ref[r].astype(F32)
        pad_ref[r, B - EDGE :] = jnp.where(last, pltpu.roll(extra, 12, 0), 0.0).astype(BF16)
        side = jnp.where(last, pltpu.roll(extra, 8, 0), 0.0).astype(BF16)
        window = jnp.concatenate([before_ref[r], own_ref[r]], axis=0)
        scores = dot_nt(jnp.concatenate([left_ref[r], side], axis=0), window)
        disp = down_lanes(level_row(disp_ref, first + r, 0))
        main = pick_taps(scores[:B, :B], scores[:B, B:], disp, taps, radius, scale)
        disp = pltpu.roll(extra, 4, 0)[:, :B].astype(jnp.int32)
        beside = pick_taps(
            dot_nt(side, pad_ref[r]), scores[B:, :B], disp, taps, radius, scale, B - EDGE
        )
        pre = dot(jnp.concatenate([main, beside], axis=0), weight)
        pre_ref[r] = pre[:B]
        mot = silu(pre)
        mot_ref[r, :B] = mot[:B].astype(BF16)
        mot_ref[r, B : 2 * B] = mot_right_ref[r, :B]
        right_edge = mot_right_ref[r, B:].astype(F32)
        mot_ref[r, 2 * B :] = jnp.where(upper, right_edge, mot[B:]).astype(BF16)

    rim_ref[...] = mot_ref[rim_at : rim_at + HALO]


def shifted(value):
    return (
        pltpu.roll(value, 1, 0).astype(BF16),
        value.astype(BF16),
        pltpu.roll(value, value.shape[0] - 1, 0).astype(BF16),
    )


def store3(buf, row, value):
    for b, part in enumerate(shifted(value)):
        buf[row, :, b * B : (b + 1) * B] = part


def lanes(buf, rows, b):
    return jnp.concatenate([buf[r, :, b * B : (b + 1) * B] for r in rows], axis=0)


def patches(bufs, row_sets):
    return jnp.concatenate(
        [lanes(buf, rows, b) for rows in row_sets for b in range(3) for buf in bufs], axis=1
    )


def chunks(values, size):
    values = list(values)
    return [values[i : i + size] for i in range(0, len(values), size)]


CHUNK = 4


def gates_hidden_kernel(
    hid_ref,
    edge_ref,
    gate_ref,
    cand_ref,
    gh_ref,
    wgm_ref,
    wc_ref,
    wcb_ref,
    wgb_ref,
    h_ref,
    h3_ref,
    wgh_ref,
):
    rows, own, _ = hid_ref.shape
    wide = own + EDGE
    for row in range(rows):
        join_columns(h_ref, 0, hid_ref[row], edge_ref[row, :, :B])
        store3(h3_ref, row, h_ref[0].astype(F32))
    zeros = jnp.zeros((6 * B, B), BF16)
    wc_ref[18 * B :, :B] = zeros
    wc_ref[: 6 * B, B:] = zeros
    wc_ref[: 18 * B, :B] = cand_ref[...]
    wc_ref[6 * B :, B:] = cand_ref[...]
    wgb_ref[:B, 18 * B :] = jnp.zeros((B, 6 * B), BF16)
    wgb_ref[B:, : 6 * B] = jnp.zeros((B, 6 * B), BF16)
    for n in range(9):
        wgh_ref[n * B : (n + 1) * B] = gate_ref[2 * n * B : (2 * n + 1) * B]
        wgm_ref[n * B : (n + 1) * B] = gate_ref[(2 * n + 1) * B : (2 * n + 2) * B]
        at = (8 - n) * 2 * B
        wcb_ref[:, n * B : (n + 1) * B] = cand_ref[at : at + 2 * B]
        for s in range(2):
            col = (n + 3 * s) * 2 * B
            wgb_ref[s * B : (s + 1) * B, col : col + 2 * B] = gate_ref[at + B : at + 2 * B]
    for group in chunks(range(1, rows - 1), CHUNK):
        lhs = patches((h3_ref,), [[r + a - 1 for r in group] for a in range(3)])
        acc = dot(lhs, wgh_ref[...])
        for n, row in enumerate(group):
            gh_ref[row - 1] = acc[n * wide : (n + 1) * wide]


def gru_kernel(
    hid_ref,
    grad_ref,
    hgt_ref,
    hgb_ref,
    edge_ref,
    mota_ref,
    motb_ref,
    mott_ref,
    motl_ref,
    wg_ref,
    wgm_ref,
    gates_ref,
    wc_ref,
    wcb_ref,
    wgb_ref,
    prela_ref,
    prelb_ref,
    prer_ref,
    disp_ref,
    mw_ref,
    nh_ref,
    pg_ref,
    tg_ref,
    u3_ref,
    m3_ref,
    r3_ref,
    c3_ref,
    cb_ref,
    h_ref,
    g_ref,
    gh_ref,
):
    rows, own, _ = nh_ref.shape
    half = rows // 2
    wide = own + EDGE
    total = rows + 2 * HALO
    inner = range(HALO, HALO + rows)
    known = range(HALO + 1, HALO + rows - 1)
    for row in range(total):
        n = row - HALO
        if n < 0 or n >= rows:
            hg = hgt_ref[row] if n < 0 else hgb_ref[n - rows]
            mot = mott_ref[row] if n < 0 else motl_ref[n - rows]
            h_ref[row] = hg
        else:
            mot = mota_ref[n] if n < half else motb_ref[n - half]
            join_columns(h_ref, row, hid_ref[n], edge_ref[n, :, :B])
            join_columns(g_ref, row, grad_ref[n], edge_ref[n, :, B:])
        store3(m3_ref, row, mot.astype(F32))
        if row <= known[0] or row >= known[-1]:
            store3(u3_ref, row, h_ref[row].astype(F32))

    for n in range(HALO // 2):
        g_ref[HALO - HALO // 2 + n] = hgt_ref[HALO + n]
        g_ref[HALO + rows + n] = hgb_ref[HALO + n]

    def gate(row, value):
        value = jax.nn.sigmoid(value)
        gh_ref[row - 1] = value
        store3(r3_ref, row, value[:, B:] * h_ref[row].astype(F32))

    for group in (list(range(1, known[0])), list(range(known[-1] + 1, total - 1))):
        lhs = patches((u3_ref, m3_ref), [[r + a - 1 for r in group] for a in range(3)])
        acc = dot(lhs, wg_ref[...])
        for n, row in enumerate(group):
            gate(row, acc[n * wide : (n + 1) * wide])
    for group in chunks(known, CHUNK):
        lhs = patches((m3_ref,), [[r + a - 1 for r in group] for a in range(3)])
        acc = dot(lhs, wgm_ref[...])
        for n, row in enumerate(group):
            gate(row, acc[n * wide : (n + 1) * wide] + gates_ref[row - known[0]])

    for group in chunks(range(2, total - 2, 2), CHUNK):
        lhs = patches((r3_ref, m3_ref), [[r + t - 1 for r in group] for t in range(4)])
        acc = jnp.tanh(dot(lhs, wc_ref[...]))
        for n, top in enumerate(group):
            for row in (top, top + 1):
                s = row - top
                cand = acc[n * wide : (n + 1) * wide, s * B : (s + 1) * B]
                hidden = h_ref[row].astype(F32)
                update = gh_ref[row - 1, :, :B]
                if row in inner:
                    new = (1.0 - update) * hidden + update * cand
                    nh_ref[row - HALO] = new[:own].astype(BF16)
                gu = g_ref[row].astype(F32) * update
                store3(c3_ref, row, gu * (1.0 - cand * cand))
                store3(u3_ref, row, gu * (cand - hidden) * (1.0 - update))

    for group in chunks(range(3, total - 3), CHUNK):
        lhs = patches((c3_ref,), [[r + a - 1 for r in group] for a in range(3)])
        acc = dot_nt(lhs, wcb_ref[...])
        for n, row in enumerate(group):
            back = acc[n * wide : (n + 1) * wide]
            reset = gh_ref[row - 1, :, B:]
            store3(m3_ref, row, back[:, :B] * h_ref[row].astype(F32) * reset * (1.0 - reset))
            if row in inner:
                cb_ref[row - HALO] = back[:own, B:]

    for group in chunks(range(HALO, HALO + rows, 2), CHUNK):
        lhs = patches((u3_ref, m3_ref), [[r + t - 1 for r in group] for t in range(4)])
        acc = dot_nt(lhs, wgb_ref[...])
        for n, top in enumerate(group):
            for row in (top - HALO, top + 1 - HALO):
                s = row + HALO - top
                back = acc[n * wide : n * wide + own, s * B : (s + 1) * B]
                prel = prela_ref[row] if row < half else prelb_ref[row - half]
                pre = jnp.concatenate([prel, prer_ref[row]], axis=0)
                sig = jax.nn.sigmoid(pre)
                grad = (cb_ref[row] + back) * sig * (1.0 + pre * (1.0 - sig))
                grad = grad.astype(BF16)
                pg_ref[row] = grad
                tap = dot_nt(mw_ref[...], grad[:B])
                level = jnp.broadcast_to(disp_ref[row : row + 1, :B].astype(F32), tap.shape)
                tg_ref[row] = jnp.where(iota(tap.shape, 0) == 15, level, tap).astype(BF16)


def spread(grad, disp, taps, radius):
    pixel = iota((B, B), 0)
    lane = iota((B, B), 1)
    tap = ((pixel - lane) & (B - 1)) - disp + radius
    ok = (tap >= 0) & (tap < taps)
    value = jnp.where(ok, lane_gather(grad, tap & (B - 1)), 0.0)
    far = jnp.where(lane > pixel, value, 0.0).astype(BF16)
    near = jnp.where(lane > pixel, 0.0, value).astype(BF16)
    return far, near


def spread_t(grad, disp, taps, radius):
    column = iota((B, B), 0)
    pixel = iota((B, B), 1)
    tap = ((pixel - column) & (B - 1)) - disp + radius
    value = jnp.zeros((B, B), F32)
    for k in range(taps):
        value = jnp.where(tap == k, grad[k : k + 1], value)
    far = jnp.where(column > pixel, value, 0.0).astype(BF16)
    near = jnp.where(column > pixel, 0.0, value).astype(BF16)
    return far, near


def grads_kernel(
    taps,
    radius,
    scale,
    pg_ref,
    left_ref,
    own_ref,
    before_a_ref,
    before_b_ref,
    disp_ref,
    weight_ref,
    gl_ref,
    gr_ref,
    near_ref,
    mw_ref,
):
    rows = left_ref.shape[0]
    step = pl.program_id(0)
    head = step < pl.num_programs(0) // 2
    weight_t = weight_ref[...]
    weight = taps_matrix(weight_ref, mw_ref)
    for r in range(rows):
        grads = dot_nt(pg_ref[r], weight).astype(BF16).astype(F32)
        grads_t = dot_nt(weight_t, pg_ref[r]).astype(BF16).astype(F32)
        parts = []
        parts_t = []
        for block in range(2):
            at = slice(block * B, (block + 1) * B)
            row = level_row(disp_ref, step * rows + r, block * B)
            parts.append(spread(grads[at], down_lanes(row), taps, radius))
            parts_t.append(spread_t(grads_t[:, at], row, taps, radius))
        before = jnp.where(head, before_a_ref[r], before_b_ref[r])
        window = jnp.concatenate([before, own_ref[r, :B]], axis=0)
        gl_ref[r, :B] = (dot(jnp.concatenate(parts[0], axis=1), window) * scale).astype(BF16)
        gl_ref[r, B:] = (dot(jnp.concatenate(parts[1], axis=1), own_ref[r]) * scale).astype(BF16)
        sg = jnp.concatenate([parts_t[0][1], parts_t[1][0]], axis=1)
        gr_ref[r] = (dot(sg, left_ref[r]) * scale).astype(BF16)
        near_ref[r] = parts_t[1][1]


def last_kernel(taps, radius, scale, near_ref, grad_ref, left_ref, next_ref, first_ref, gr_ref):
    del first_ref
    rows = left_ref.shape[0]
    for r in range(rows):
        grad = grad_ref[r].astype(F32)
        disp = grad[15:16].astype(jnp.int32)
        far, _ = spread_t(grad, disp, taps, radius)
        sg = jnp.concatenate([near_ref[r], far], axis=1)
        window = jnp.concatenate([left_ref[r], next_ref[r]], axis=0)
        gr_ref[r] = (dot(sg, window) * scale).astype(BF16)


def whole(array):
    nd = array.ndim
    return pl.BlockSpec(array.shape, lambda i: (0,) * nd)


def by_rows(array, size, block=None, at=None):
    block = tuple(array.shape[1:]) if block is None else block
    at = (0,) * len(block) if at is None else at
    return pl.BlockSpec((size,) + block, lambda i: (i,) + at)


def cost(flops, bytes_accessed):
    return pl.CostEstimate(flops=flops, bytes_accessed=bytes_accessed, transcendentals=0)


def block(shape, *at):
    return pl.BlockSpec(shape, lambda i: (i + at[0],) + at[1:])


def per_device(
    feat_left, feat_right, hidden, disparity, motion_weight, gate_weight, cand_weight, grad_hidden
):
    rows, cols, chan = feat_left.shape
    taps = motion_weight.shape[0]
    radius = taps // 2
    scale = 1.0 / math.sqrt(chan)
    args = (taps, radius, scale)
    size = ROWS
    steps = rows // size
    half = rows // 2
    wide = cols + EDGE
    packed = 2 * chan + 3 * B
    params = pltpu.CompilerParams(vmem_limit_bytes=SMALL_VMEM)
    shape = jax.ShapeDtypeStruct
    vmem = pl.BlockSpec(memory_space=pltpu.VMEM)
    last8 = cols // 8 - 1
    pack_params = pltpu.CompilerParams(vmem_limit_bytes=PACK_VMEM)

    small_shapes = (shape((rows, HALO, packed), BF16), shape((rows, EDGE, chan), BF16))
    to_left, to_right = pl.pallas_call(
        pack_small_kernel,
        grid=(1,),
        in_specs=[
            block((rows, 8, chan), 0, 0, 0),
            block((rows, 8, chan), 0, 0, 0),
            block((rows, 8, B), 0, 0, 0),
            block((rows, 8, B), 0, 0, 0),
            block((rows, 8, chan), 0, (cols - B) // 8 - 1, 0),
            block((rows, 8, chan), 0, last8, 0),
            block((rows, 8, B), 0, last8, 0),
            block((rows, 8, B), 0, last8, 0),
            whole(disparity),
        ],
        out_specs=[whole(s) for s in small_shapes],
        out_shape=small_shapes,
        compiler_params=pack_params,
        cost_estimate=cost(1 << 16, 1 << 18),
        name="pack_small",
    )(
        feat_left,
        feat_right,
        hidden,
        grad_hidden,
        feat_right,
        feat_left,
        hidden,
        grad_hidden,
        disparity,
    )
    from_right = shift(to_left, "cols", -1)
    from_left = shift(to_right, "cols", 1)
    features = feat_right[:, cols - B :]
    second, from_right, from_left = lax.optimization_barrier(
        (features[half:], from_right, from_left)
    )
    before = [shift(features[:half], "cols", 1), shift(second, "cols", 1)]

    rim = shape((HALO + HALO // 2, wide, B), BF16)
    edge_shape = shape((rows, EDGE, 2 * B), BF16)
    first_rim, last_rim, edge = pl.pallas_call(
        rim_kernel,
        grid=(1,),
        in_specs=[
            block((HALO, cols, B), 0, 0, 0),
            block((HALO, cols, B), 0, 0, 0),
            block((HALO, cols, B), rows // HALO - 1, 0, 0),
            block((HALO, cols, B), rows // HALO - 1, 0, 0),
            whole(from_right),
            whole(from_left),
        ],
        out_specs=[whole(rim), whole(rim), whole(edge_shape)],
        out_shape=(rim, rim, edge_shape),
        scratch_shapes=[pltpu.VMEM((EDGE, 2 * B), F32)],
        compiler_params=params,
        cost_estimate=cost(1 << 16, 2 << 20),
        name="rims",
    )(hidden, grad_hidden, hidden, grad_hidden, from_right, from_left)
    hg_top = shift(last_rim, "rows", 1)
    hg_low = shift(first_rim, "rows", -1)

    mw16 = jnp.pad(motion_weight, ((0, 16 - taps), (0, 0)))
    pads = [pltpu.VMEM((size, B, chan), BF16), pltpu.VMEM((B, B), BF16)]
    right_shapes = (shape((rows, B + EDGE, B), BF16), shape((rows, B, B), F32))
    mot_right, pre_right = pl.pallas_call(
        lambda *refs: right_corr_kernel(*args, *refs),
        grid=(steps,),
        in_specs=[
            block((size, B, chan), 0, 1, 0),
            by_rows(feat_right, size),
            whole(disparity),
            by_rows(from_right, size),
            whole(mw16),
        ],
        out_specs=[by_rows(s, size) for s in right_shapes],
        out_shape=right_shapes,
        scratch_shapes=pads + [pltpu.VMEM((size, EDGE, packed), F32)],
        compiler_params=params,
        cost_estimate=cost(2 * rows * B * 2 * B * chan, 6 << 20),
        name="corr_right",
    )(feat_left, feat_right, disparity, from_right, mw16)

    def left_lookup(start, before, rim_at):
        at = start // half
        shapes = (
            shape((half, wide, B), BF16),
            shape((half, B, B), F32),
            shape((HALO, wide, B), BF16),
        )
        return pl.pallas_call(
            lambda *refs: left_corr_kernel(*args, start, rim_at, *refs),
            grid=(1,),
            in_specs=[
                block((half, B, chan), at, 0, 0),
                block((half, B, chan), at, 0, 0),
                by_rows(before, half),
                block((half, EDGE, chan), at, 0, 0),
                whole(disparity),
                block((half, B + EDGE, B), at, 0, 0),
                whole(mw16),
            ],
            out_specs=[by_rows(s, half) for s in shapes[:2]] + [whole(shapes[2])],
            out_shape=shapes,
            scratch_shapes=[pltpu.VMEM((half, B, chan), BF16), pads[1]],
            compiler_params=params,
            cost_estimate=cost(rows * B * 2 * B * chan, 3 << 20),
            name="corr_left",
        )(feat_left, feat_right, before, from_left, disparity, mot_right, mw16)

    mot_a, pre_a, rim_a = left_lookup(0, before[0], 0)
    mot_low = shift(rim_a, "rows", -1)
    mot_b, pre_b, rim_b = left_lookup(half, before[1], half - HALO)
    mot_top = shift(rim_b, "rows", 1)
    first_left, _ = lax.optimization_barrier((feat_left[:, :B], mot_b))
    next_left = shift(first_left, "cols", -1)

    total = rows + 2 * HALO
    own_shape = shape((rows, cols, B), BF16)
    gate_shape = shape((rows - 2, wide, 2 * B), F32)
    weight_shapes = [
        shape((9 * B, 2 * B), BF16),
        shape((24 * B, 2 * B), BF16),
        shape((2 * B, 9 * B), BF16),
        shape((2 * B, 24 * B), BF16),
    ]
    wg = gate_weight.reshape(-1, 2 * B)
    hid_operands = (hidden, edge, wg, cand_weight.reshape(-1, B))
    hid_shapes = (gate_shape, *weight_shapes)
    gates, wgm, wc, wcb, wgb = pl.pallas_call(
        gates_hidden_kernel,
        in_specs=[vmem] * len(hid_operands),
        out_specs=[vmem] * len(hid_shapes),
        out_shape=hid_shapes,
        scratch_shapes=[
            pltpu.VMEM((1, wide, B), BF16),
            pltpu.VMEM((rows, wide, 3 * B), BF16),
            pltpu.VMEM((9 * B, 2 * B), BF16),
        ],
        compiler_params=pltpu.CompilerParams(vmem_limit_bytes=GATES_VMEM),
        cost_estimate=cost(2 * 22 * wide * 9 * B * 2 * B, 16 << 20),
        name="gates_hidden",
    )(*hid_operands)
    operands = (
        hidden,
        grad_hidden,
        hg_top,
        hg_low,
        edge,
        mot_a,
        mot_b,
        mot_top,
        mot_low,
        wg,
        wgm,
        gates,
        wc,
        wcb,
        wgb,
        pre_a,
        pre_b,
        pre_right,
        disparity,
        mw16,
    )
    anywhere = pl.BlockSpec(memory_space=pl.ANY)
    halo_buffer = pltpu.VMEM((total, wide, B), BF16)
    new_hidden, pre_grad, tap_grad = pl.pallas_call(
        gru_kernel,
        in_specs=[vmem] * len(operands),
        out_specs=[vmem] * 3,
        out_shape=(own_shape, own_shape, shape((rows, 16, B), BF16)),
        scratch_shapes=[pltpu.VMEM((total, wide, 3 * B), BF16)] * 4
        + [pltpu.VMEM((rows, cols, B), F32), halo_buffer, halo_buffer]
        + [pltpu.VMEM((total - 2, wide, 2 * B), F32)],
        compiler_params=pltpu.CompilerParams(vmem_limit_bytes=GRU_VMEM),
        cost_estimate=cost(2 * 22 * wide * 256 * 256 * 20, 16 << 20),
        name="gru",
    )(*operands)
    next_grad = shift(tap_grad, "cols", -1)

    gsize = GRAD_ROWS
    gsteps = rows // gsize
    feat_shape = shape((rows, cols, chan), BF16)
    near_shape = shape((rows, B, B), BF16)
    mid = gsteps // 2
    grad_left, grad_first, near = pl.pallas_call(
        lambda *refs: grads_kernel(*args, *refs),
        grid=(gsteps,),
        in_specs=[
            by_rows(pre_grad, gsize),
            by_rows(feat_left, gsize),
            by_rows(feat_right, gsize),
            pl.BlockSpec((gsize, B, chan), lambda i: (jnp.minimum(i, mid - 1), 0, 0)),
            pl.BlockSpec((gsize, B, chan), lambda i: (jnp.maximum(i - mid, 0), 0, 0)),
            whole(disparity),
            whole(mw16),
        ],
        out_specs=[
            by_rows(feat_shape, gsize),
            block((gsize, B, chan), 0, 0, 0),
            by_rows(near_shape, gsize),
        ],
        out_shape=(feat_shape, feat_shape, near_shape),
        scratch_shapes=[pltpu.VMEM((B, B), BF16)],
        compiler_params=params,
        cost_estimate=cost(2 * rows * B * 2 * B * chan * 4, 12 << 20),
        name="grads",
    )(pre_grad, feat_left, feat_right, before[0], before[1], disparity, mw16)
    grad_right = pl.pallas_call(
        lambda *refs: last_kernel(*args, *refs),
        grid=(gsteps,),
        in_specs=[
            by_rows(near, gsize),
            by_rows(next_grad, gsize),
            block((gsize, B, chan), 0, 1, 0),
            by_rows(next_left, gsize),
            anywhere,
        ],
        out_specs=block((gsize, B, chan), 0, 1, 0),
        out_shape=feat_shape,
        input_output_aliases={4: 0},
        compiler_params=params,
        cost_estimate=cost(2 * rows * B * 2 * B * chan, 4 << 20),
        name="grad_right",
    )(near, next_grad, feat_left, next_left, grad_first)
    return (new_hidden, grad_left, grad_right)


def solution(mesh):
    grid3 = P("rows", "cols", None)
    return jax.shard_map(
        per_device,
        mesh=mesh,
        in_specs=(grid3, grid3, grid3, P("rows", "cols"), P(), P(), P(), grid3),
        out_specs=(grid3, grid3, grid3),
        check_vma=False,
    )
```
